32 devices in a mesh: dp: 4 (over y, x), seq: 2 (over core), head: 4 (over z).
Axes of the slice: x: 2, y: 2, z: 4, core: 2. Of those that a mesh axis runs over, the one named last changes fastest.
Arguments:
- hidden_in: bfloat16 [1, 4, 512, 1024], P(None, 'dp', 'seq', 'head'), may hold values from -6 to 6
- cotangent: bfloat16 [1, 4, 512, 1024], P(None, 'dp', 'seq', 'head'), may hold values from -6 to 6
- norm_gain: bfloat16 [1024], P(('dp', 'seq')), may hold values from 0.5 to 1.5
- w_zx: bfloat16 [1024, 2, 2048], P(('dp', 'seq'), None, 'head'), may hold values from -0.1875 to 0.1875
- w_bc: bfloat16 [1024, 256], P(('dp', 'seq')), may hold values from -0.1875 to 0.1875
- w_dt: bfloat16 [1024, 32], P(('dp', 'seq'), 'head'), may hold values from -0.1875 to 0.1875
- w_out: bfloat16 [2048, 1024], P('head', ('dp', 'seq')), may hold values from -0.125 to 0.125
- conv_x: float32 [5, 2048], P(None, 'head'), may hold values from -0.5 to 0.5
- conv_bc: float32 [5, 256], replicated, may hold values from -0.5 to 0.5
- head_params: float32 [3, 32], P(None, 'head'), may hold values from -11 to 2.5, as said below
- gate_gain: float32 [2048], P('head'), may hold values from 0.5 to 1.5
Outputs:
- output: bfloat16 [1, 4, 512, 1024], P(None, 'dp', 'seq', 'head')
- grad_input: bfloat16 [1, 4, 512, 1024], P(None, 'dp', 'seq', 'head')
- grad_norm_gain: float32 [1024], P(('dp', 'seq'))
- grad_w_zx: float32 [1024, 2, 2048], P(('dp', 'seq'), None, 'head')
- grad_w_bc: float32 [1024, 256], P(('dp', 'seq'))
- grad_w_dt: float32 [1024, 32], P(('dp', 'seq'), 'head')
- grad_w_out: float32 [2048, 1024], P('head', ('dp', 'seq'))
- grad_conv_x: float32 [5, 2048], P(None, 'head')
- grad_conv_bc: float32 [5, 256], replicated
- grad_head_params: float32 [3, 32], P(None, 'head')
- grad_gate_gain: float32 [2048], P('head')
The draws below stay inside these ranges and needn't reach their ends.
Inputs may be any that keep to these rules, and one draw needn't show every extreme that they name: `head_params`: row 0 holds the step-size bias of each head, row 1 the logarithm of minus A (0 to 2.5), row 2 the skip factor D (0.5 to 1.5).
All inputs are finite; a program needn't handle non-finite values.
Results may differ from the reference program's by a relative error of at most 0.0092.
Values may be sent and summed in bfloat16 or wider, within the bound.
No kernel may reach another device: no remote copies, remote signals or barrier semaphores. Data moves between devices by JAX's collectives and lax.ppermute only.
A program may use at most 64 MiB of HBM per device.

```python
import jax
import jax.numpy as jnp
from jax import lax

D = 1024
INNER = 2048
NH = 32
NS = 128
K = 4
GROUP = 256
MB = 1
SEQS = 4
LEN = 512


def draw_head_params(key, part):
    key_bias = jax.random.fold_in(key, 11)
    key_rate = jax.random.fold_in(key, 12)
    key_skip = jax.random.fold_in(key, 13)
    step_bias = jax.random.uniform(key_bias, (NH,), jnp.float32, -10.0, -4.0)
    log_rate = jax.random.uniform(key_rate, (NH,), jnp.float32, 0.0, 2.5)
    skip_gain = jax.random.uniform(key_skip, (NH,), jnp.float32, 0.5, 1.5)
    return jnp.stack([step_bias, log_rate, skip_gain], axis=0).astype(jnp.float32)


def levels(stream_key, dims, cuts, least, top_value):
    def one(axis_at, blocks):
        steps = jax.random.uniform(jax.random.fold_in(jax.random.fold_in(stream_key, 6), axis_at), (blocks,), jnp.float32, least / len(cuts), top_value / len(cuts))
        return jnp.repeat(jnp.exp(steps), dims[axis_at] // blocks).reshape((-1,) + (1,) * (len(dims) - axis_at - 1))

    loudness = one(*cuts[0])
    for cut in cuts[1:]:
        loudness = loudness * one(*cut)
    return loudness


def centred(key, extent, width, bound, split=(), kind=jnp.bfloat16):
    array = jax.random.normal(key, extent, jnp.float32) * width
    if len(split) > 0:
        array = levels(key, extent, split, -0.22, 0.18) * array
    return jnp.clip(array, min=-bound, max=bound).astype(kind)


def setup_inputs(seed: int = 0) -> dict:
    seeds = jax.random.split(jax.random.key(seed), 12)
    return {
        "hidden_in": centred(seeds[0], (MB, SEQS, LEN, D), 1.0, 6.0, ((1, 4), (2, 2), (3, 4))),
        "cotangent": centred(seeds[1], (MB, SEQS, LEN, D), 1.0, 6.0, ((1, 4), (2, 2), (3, 4))),
        "norm_gain": jnp.clip(1.0 + 0.1 * jax.random.normal(seeds[2], (D,), jnp.float32), 0.5, 1.5).astype(jnp.bfloat16),
        "w_zx": centred(seeds[3], (D, 2, INNER), D ** -0.5, 0.1875, ((0, 8), (2, 4))),
        "w_bc": centred(seeds[4], (D, 2 * NS), D ** -0.5, 0.1875, ((0, 8),)),
        "w_dt": centred(seeds[5], (D, NH), D ** -0.5, 0.1875, ((0, 8), (1, 4))),
        "w_out": centred(seeds[6], (INNER, D), INNER ** -0.5, 0.125, ((0, 4), (1, 8))),
        "conv_x": jnp.clip(jax.random.uniform(seeds[7], (K + 1, INNER), jnp.float32, -0.5, 0.5) * levels(seeds[7], (K + 1, INNER), ((1, 4),), -0.4, 0.0), -0.5, 0.5),
        "conv_bc": jnp.clip(jax.random.uniform(seeds[8], (K + 1, 2 * NS), jnp.float32, -0.5, 0.5), -0.5, 0.5),
        "head_params": draw_head_params(jax.random.fold_in(seeds[11], 71), 0),
        "gate_gain": jnp.clip(1.0 + 0.1 * jax.random.normal(seeds[10], (INNER,), jnp.float32), 0.5, 1.5),
    }


epsilon = 1e-05
highest = lax.Precision.HIGHEST

def silu_of(values):
    return values * jax.nn.sigmoid(values)

def norm_input(x_float, gain_float):
    inv_root = lax.rsqrt(lax.optimization_barrier(jnp.mean(x_float * x_float, axis=-1, keepdims=True)) + epsilon)
    return x_float * inv_root * gain_float

def causal_conv(values, taps_bias):
    tap_count = taps_bias.shape[0] - 1
    length = values.shape[0]
    padded = jnp.concatenate([jnp.zeros((tap_count - 1, values.shape[1]), jnp.float32), values], axis=0)
    summed = jnp.broadcast_to(taps_bias[tap_count], values.shape)
    for tap_k in range(tap_count):
        summed = summed + taps_bias[tap_k] * padded[tap_k:tap_k + length]
    return summed

def group_step(state_in, inputs):
    x_part, b_part, c_part, step_part, log_part = inputs
    cum_log = jnp.cumsum(log_part, axis=0).T
    group_len = cum_log.shape[1]
    lower_mask = jnp.arange(group_len)[:, None] >= jnp.arange(group_len)[None, :]
    decay_mat = jnp.exp(jnp.where(lower_mask[None], cum_log[:, :, None] - cum_log[:, None, :], -jnp.inf))
    gram_mat = jnp.dot(c_part, b_part.T, precision=highest)
    scaled_in = x_part * step_part[:, :, None]
    y_inner = jnp.einsum('hij,ij,jhp->ihp', decay_mat, gram_mat, scaled_in, precision=highest)
    y_cross = jnp.einsum('in,hpn->ihp', c_part, state_in, precision=highest) * jnp.exp(cum_log).T[:, :, None]
    to_end = jnp.exp(cum_log[:, -1:] - cum_log)
    new_state = jnp.exp(cum_log[:, -1])[:, None, None] * state_in + jnp.einsum('jhp,jn,hj->hpn', scaled_in, b_part, to_end, precision=highest)
    return (new_state, y_inner + y_cross)

def ssd_full(x_heads, b_all, c_all, step_size, log_decay):
    length, head_count, width_p = x_heads.shape
    state_n = b_all.shape[1]
    groups = length // GROUP
    inputs = (x_heads.reshape(groups, GROUP, head_count, width_p), b_all.reshape(groups, GROUP, state_n), c_all.reshape(groups, GROUP, state_n), step_size.reshape(groups, GROUP, head_count), log_decay.reshape(groups, GROUP, head_count))
    initial = jnp.zeros((head_count, width_p, state_n), jnp.float32)
    final_state, y_groups = lax.scan(group_step, initial, inputs)
    return y_groups.reshape(length, head_count, width_p)

def mixer_core(z_float, x_float, bc_float, dt_raw, conv_x, conv_bc, head_params, gate_gain):
    length = z_float.shape[0]
    head_count = head_params.shape[1]
    width_p = x_float.shape[1] // head_count
    state_n = bc_float.shape[1] // 2
    x_act = silu_of(causal_conv(x_float, conv_x))
    bc_act = silu_of(causal_conv(bc_float, conv_bc))
    step_size = jax.nn.softplus(dt_raw + head_params[0])
    rate_a = -jnp.exp(head_params[1])
    log_decay = step_size * rate_a
    x_heads = x_act.reshape(length, head_count, width_p)
    y_heads = ssd_full(x_heads, bc_act[:, :state_n], bc_act[:, state_n:], step_size, log_decay)
    y_heads = y_heads + x_heads * head_params[2][:, None]
    y_flat = y_heads.reshape(length, head_count * width_p)
    gated_in = y_flat * silu_of(z_float)
    inv_root = lax.rsqrt(lax.optimization_barrier(jnp.mean(gated_in * gated_in, axis=-1, keepdims=True)) + epsilon)
    return gated_in * inv_root * gate_gain

def reference(hidden_in, cotangent, norm_gain, w_zx, w_bc, w_dt, w_out, conv_x, conv_bc, head_params, gate_gain):
    micro_n, seq_count, length, width_d = hidden_in.shape
    inner_w = w_out.shape[0]
    flat_in = hidden_in.reshape(micro_n * seq_count, length, width_d)
    flat_cot = cotangent.reshape(micro_n * seq_count, length, width_d)
    gain_float = norm_gain.astype(jnp.float32)
    w_zx_flat = w_zx.reshape(width_d, 2 * inner_w)

    def one_sequence(grad_acc, seq_pair):
        seq_in, seq_cot = seq_pair
        x_float = seq_in.astype(jnp.float32)
        normed_f, norm_back = jax.vjp(norm_input, x_float, gain_float)
        normed = normed_f.astype(jnp.bfloat16)
        zx_val = jnp.dot(normed, w_zx_flat, preferred_element_type=jnp.float32).astype(jnp.bfloat16).reshape(length, 2, inner_w)
        bc_val = jnp.dot(normed, w_bc, preferred_element_type=jnp.float32).astype(jnp.bfloat16)
        dt_raw = jnp.dot(normed, w_dt, preferred_element_type=jnp.float32)
        gated_f, core_back = jax.vjp(mixer_core, zx_val[:, 0].astype(jnp.float32), zx_val[:, 1].astype(jnp.float32), bc_val.astype(jnp.float32), dt_raw, conv_x, conv_bc, head_params, gate_gain)
        gated = gated_f.astype(jnp.bfloat16)
        output = (x_float + jnp.dot(gated, w_out, preferred_element_type=jnp.float32)).astype(jnp.bfloat16)
        grad_gated = jnp.dot(seq_cot, w_out.T, preferred_element_type=jnp.float32)
        grad_z, grad_x, grad_bc, grad_dt, grad_cx, grad_cbc, grad_head, grad_ggain = core_back(grad_gated)
        grad_zx = jnp.stack([grad_z, grad_x], axis=1).astype(jnp.bfloat16).reshape(length, 2 * inner_w)
        grad_bc16 = grad_bc.astype(jnp.bfloat16)
        grad_dt16 = grad_dt.astype(jnp.bfloat16)
        normalized_gradient = jnp.dot(grad_zx, w_zx_flat.T, preferred_element_type=jnp.float32) + jnp.dot(grad_bc16, w_bc.T, preferred_element_type=jnp.float32) + jnp.dot(grad_dt16, w_dt.T, preferred_element_type=jnp.float32)
        grad_xf, grad_ngain = norm_back(normalized_gradient)
        grad_in_seq = (seq_cot.astype(jnp.float32) + grad_xf).astype(jnp.bfloat16)
        updates = (grad_ngain, jnp.dot(normed.T, grad_zx, preferred_element_type=jnp.float32).reshape(width_d, 2, inner_w), jnp.dot(normed.T, grad_bc16, preferred_element_type=jnp.float32), jnp.dot(normed.T, grad_dt16, preferred_element_type=jnp.float32), jnp.dot(gated.T, seq_cot, preferred_element_type=jnp.float32), grad_cx, grad_cbc, grad_head, grad_ggain)
        grad_acc = tuple((acc_item + upd_item for acc_item, upd_item in zip(grad_acc, updates)))
        return (grad_acc, (output, grad_in_seq))
    zero_grads = tuple((jnp.zeros(item.shape, jnp.float32) for item in (norm_gain, w_zx, w_bc, w_dt, w_out, conv_x, conv_bc, head_params, gate_gain)))
    grad_acc, (out_all, grad_all) = lax.scan(one_sequence, zero_grads, (flat_in, flat_cot))
    return (out_all.reshape(hidden_in.shape), grad_all.reshape(hidden_in.shape), grad_acc[0], grad_acc[1], grad_acc[2], grad_acc[3], grad_acc[4], grad_acc[5], grad_acc[6], grad_acc[7], grad_acc[8])
```

```python
import functools

import jax
import jax.numpy as jnp
from jax import lax
from jax.experimental import pallas as pl
from jax.experimental.pallas import tpu as pltpu
from jax.sharding import PartitionSpec as P

epsilon = 1e-05
f32 = jnp.float32
bf16 = jnp.bfloat16
exact = lax.Precision.HIGHEST
LANES = 128
HALO = 16
EDGE = 8


def xor_route(count, k):
    return [(i, i ^ k) for i in range(count)]


def exchanged(block, axis):
    count = lax.axis_size(axis)
    return [block] + [lax.ppermute(block, axis, xor_route(count, k)) for k in range(1, count)]


def scattered(blocks, axis):
    count = lax.axis_size(axis)
    return [blocks[0]] + [
        lax.ppermute(blocks[k], axis, xor_route(count, k)) for k in range(1, count)
    ]


def tree_sum(parts):
    while len(parts) > 1:
        parts = [a + b for a, b in zip(parts[0::2], parts[1::2])]
    return parts[0]


def f32_sum(parts):
    return tree_sum([part.astype(f32) for part in parts])


def passed_along(block, axis, distance):
    devices = range(lax.axis_size(axis))
    route = [(i - distance, i) for i in devices if i - distance in devices]
    return lax.ppermute(block, axis, route)


def entering(decay, state, axis, reverse):
    count, place = lax.axis_size(axis), lax.axis_index(axis)
    if count == 2:
        return passed_along(state, axis, -1 if reverse else 1)
    decays, states = lax.all_gather(decay, axis), lax.all_gather(state, axis)

    def turn(k, before):
        at = count - 1 - k if reverse else k
        reached = at > place if reverse else at < place
        return jnp.where(reached, decays[at] * before + states[at], before)

    return lax.fori_loop(0, count, turn, jnp.zeros_like(state))


def dot(a, b, left, right):
    return lax.dot_general(
        a.astype(bf16), b.astype(bf16), (((left,), (right,)), ((), ())), preferred_element_type=f32
    )


def nn(a, b):
    return dot(a, b, 1, 0)


def nt(a, b):
    return dot(a, b, 1, 1)


def tn(a, b):
    return dot(a, b, 0, 0)


def sigmoid(v):
    return 1.0 / (1.0 + jnp.exp(-v))


def softplus(v):
    e = jnp.exp(-jnp.abs(v))
    small = e * (1.0 - e * (0.5 - e * (1.0 / 3.0 - e * 0.25)))
    return jnp.maximum(v, 0.0) + jnp.where(e < 0.03, small, jnp.log(1.0 + e))


def iota(shape, axis):
    return lax.broadcasted_iota(jnp.int32, shape, axis)


def row_of(column):
    return jnp.broadcast_to(column, (column.shape[0], LANES)).T[0:1]


def column_of(row):
    return jnp.broadcast_to(row, (LANES, row.shape[1])).T


def per_head(values, pair_at, width):
    first = values[:, 2 * pair_at : 2 * pair_at + 1]
    second = values[:, 2 * pair_at + 1 : 2 * pair_at + 2]
    lane = iota((values.shape[0], 2 * width), 1)
    return jnp.where(lane < width, first, second)


def spread(values, heads, width):
    return jnp.concatenate([per_head(values, q, width) for q in range(heads // 2)], axis=1)


def gathered_heads(values, heads, width):
    lane = iota((values.shape[0], LANES), 1)
    wide = iota((values.shape[0], 2 * width), 1)
    total = jnp.zeros((values.shape[0], LANES), f32)
    for q in range(heads // 2):
        both = values[:, 2 * width * q : 2 * width * (q + 1)]
        first = jnp.sum(jnp.where(wide < width, both, 0.0), axis=1, keepdims=True)
        second = jnp.sum(jnp.where(wide < width, 0.0, both), axis=1, keepdims=True)
        total = jnp.where(lane == 2 * q, first, total)
        total = jnp.where(lane == 2 * q + 1, second, total)
    return total


def unit(pair, p, where):
    if pair:
        t, k = divmod(p, 4)
        return k ^ where[0], pl.multiple_of((t ^ where[1]) * LANES, LANES)
    j, u = divmod(p, 2)
    return j ^ where[0], u * LANES


def assembled(scratch, pieces, axis):
    at = 0
    for piece in pieces:
        size = piece.shape[axis]
        if axis == 0:
            scratch[at : at + size, :] = piece[...]
        else:
            scratch[:, at : at + size] = piece[...]
        at += size


def norm_kernel(pair, gain_lane, n_blocks, n_pieces, where, *refs):
    blocks, pieces = refs[:n_blocks], refs[n_blocks : n_blocks + n_pieces]
    normed, x_perm, inv_ref, gain_ref, edge_ref, hold = refs[n_blocks + n_pieces :]
    rows, part = blocks[0].shape
    swap = n_blocks * part // LANES // 2 if pair else 0
    total = jnp.zeros((rows, 1), f32)
    for k, block in enumerate(blocks):
        value = block[...].astype(f32)
        hold[k] = value
        total += jnp.sum(value * value, axis=1, keepdims=True)
    inv = lax.rsqrt(total / (n_blocks * part) + epsilon)
    inv_ref[...] = jnp.broadcast_to(inv, inv_ref.shape)
    eye = iota((LANES, LANES), 0) == iota((LANES, LANES), 1)
    per_piece = pieces[0].shape[0] // LANES
    for p in range(n_blocks * part // LANES):
        piece = pieces[p // per_piece]
        at = p % per_piece * LANES
        gain = piece[at : at + LANES, 2 * LANES : 3 * LANES][:, gain_lane : gain_lane + 1]
        gain = jnp.sum(jnp.where(eye, gain.astype(f32), 0.0), axis=0, keepdims=True)
        block, lane = unit(pair, p, where)
        value = hold[block, :, pl.ds(lane, LANES)]
        cut = slice(p * LANES, (p + 1) * LANES)
        value16 = (value * inv * gain).astype(bf16)
        normed[:, cut] = value16
        there = p ^ swap
        edge_ref[:, there * LANES : (there + 1) * LANES] = value16[rows - HALO :, :]
        x_perm[:, cut] = value.astype(bf16)
        gain_ref[:, cut] = gain


def forward_kernel(heads, n_zx, n_bcd, *refs):
    normed, edge, conv_x, conv_bc, params = refs[:5]
    zx_pieces, bcd_pieces = refs[5 : 5 + n_zx], refs[5 + n_zx : 5 + n_zx + n_bcd]
    (z_ref, xe_ref, be_ref, ux_ref, ubc_ref, dt_ref, cum_ref, y_ref, state_ref) = refs[
        5 + n_zx + n_bcd : 14 + n_zx + n_bcd
    ]
    w_zx, w_bcd, rows_in, xe, be = refs[14 + n_zx + n_bcd :]
    rows, inner = ux_ref.shape
    width = inner // heads
    state_n = ubc_ref.shape[1] // 2
    taps = conv_x.shape[0] - 1
    assembled(w_zx, zx_pieces, 0)
    assembled(w_bcd, bcd_pieces, 0)
    rows_in[0:HALO, :] = edge[...]
    rows_in[HALO : HALO + rows, :] = normed[...]
    z_ref[...] = nn(normed[...], w_zx[:, 0:inner]).astype(bf16)
    x_raw = nn(rows_in[...], w_zx[:, inner : 2 * inner]).astype(bf16)
    xe_ref[...] = x_raw
    xe[...] = x_raw.astype(f32)
    bcd = nn(rows_in[...], w_bcd[...])
    bc_raw = bcd[:, 0 : 2 * state_n].astype(bf16)
    be_ref[...] = bc_raw
    be[...] = bc_raw.astype(f32)
    dt = bcd[HALO:, 2 * state_n :]
    dt_ref[...] = dt

    def conv(extended, weights):
        total = weights[taps : taps + 1, :]
        for k in range(taps):
            total = total + weights[k : k + 1, :] * extended[
                HALO - taps + 1 + k : HALO - taps + 1 + k + rows, :
            ]
        return total

    u_x = conv(xe, conv_x)
    ux_ref[...] = u_x
    u_bc = conv(be, conv_bc)
    ubc_ref[...] = u_bc
    x_act = u_x * sigmoid(u_x)
    bc_act = u_bc * sigmoid(u_bc)
    b_mat = bc_act[:, 0:state_n].astype(bf16)
    c_mat = bc_act[:, state_n:].astype(bf16)
    lane = iota((rows, LANES), 1)
    step = jnp.where(lane < heads, softplus(dt + params[0:1, :]), 0.0)
    lower = iota((rows, rows), 0) >= iota((rows, rows), 1)
    cum = lax.dot_general(
        lower.astype(f32),
        -step * jnp.exp(params[1:2, :]),
        (((1,), (0,)), ((), ())),
        precision=exact,
        preferred_element_type=f32,
    )
    cum_ref[...] = cum
    cum_t = cum.T
    gram = nt(c_mat, b_mat)
    scaled = x_act * spread(step, heads, width)
    scaled16 = scaled.astype(bf16)
    pair_lane = iota((rows, 2 * width), 1)
    for q in range(heads // 2):
        cut = slice(2 * width * q, 2 * width * (q + 1))
        both = []
        for h in (2 * q, 2 * q + 1):
            decay = jnp.exp(jnp.where(lower, cum[:, h : h + 1] - cum_t[h : h + 1, :], -jnp.inf))
            both.append(nn(decay * gram, scaled16[:, cut]))
        y_ref[:, cut] = (
            jnp.where(pair_lane < width, both[0], both[1])
            + x_act[:, cut] * per_head(jnp.broadcast_to(params[2:3, :], (rows, LANES)), q, width)
        )
    to_end = jnp.exp(cum[rows - 1 : rows, :] - cum)
    state_ref[...] = tn(scaled * spread(to_end, heads, width), b_mat)


def gate_kernel(pair, heads, n_blocks, n_pieces, where, *refs):
    state, ubc, cum, y_loc, z, gain = refs[:6]
    blocks = refs[6 : 6 + n_blocks]
    pieces = refs[6 + n_blocks : 6 + n_blocks + n_pieces]
    y_ref, go_ref, raw_ref, stats_ref, cot_ref, w_ref, hold = refs[6 + n_blocks + n_pieces :]
    rows, inner = y_ref.shape
    width = inner // heads
    state_n = ubc.shape[1] // 2
    assembled(w_ref, pieces, 1)
    for k, block in enumerate(blocks):
        hold[k] = block[...].astype(f32)
    for p in range(cot_ref.shape[1] // LANES):
        block, lane = unit(pair, p, where)
        cot_ref[:, p * LANES : (p + 1) * LANES] = hold[block, :, pl.ds(lane, LANES)].astype(bf16)
    u_c = ubc[:, state_n:]
    c_mat = u_c * sigmoid(u_c)
    y = y_loc[...] + nt(c_mat, state[...]) * spread(jnp.exp(cum[...]), heads, width)
    y_ref[...] = y
    z_val = z[...].astype(f32)
    gated = y * z_val * sigmoid(z_val)
    raw_ref[...] = (gated * gain[...]).astype(bf16)
    grad_o = nt(cot_ref[...], w_ref[...])
    go_ref[...] = grad_o
    squares = jnp.sum(gated * gated, axis=1, keepdims=True)
    cross = jnp.sum(grad_o * gain[...] * gated, axis=1, keepdims=True)
    lane = iota((rows, LANES), 1)
    both = jnp.where(lane == 0, squares, jnp.where(lane == 1, cross, 0.0))
    stats_ref[...] = both.T[0:8, :]


def out_kernel(pair, where, raw, weights, blocks_ref):
    part = nn(raw[...], weights[...]).astype(bf16)
    for p in range(weights.shape[1] // LANES):
        block, lane = unit(pair, p, where)
        blocks_ref[block, :, pl.ds(lane, LANES)] = part[:, p * LANES : (p + 1) * LANES]


def gate_back_kernel(heads, full_inner, n_stats, *refs):
    stats = refs[:n_stats]
    go, y, z, gain, ubc, cum = refs[n_stats : n_stats + 6]
    dy_ref, dz_ref, state_ref, inv_ref, ggain_ref = refs[n_stats + 6 :]
    rows, inner = y.shape
    width = inner // heads
    state_n = ubc.shape[1] // 2
    total = tree_sum([s[...] for s in stats])
    total = jnp.concatenate([total, jnp.zeros((LANES - total.shape[0], rows), f32)], axis=0).T
    inv = lax.rsqrt(total[:, 0:1] / full_inner + epsilon)
    coef = inv * inv * inv * (total[:, 1:2] / full_inner)
    inv_ref[...] = jnp.broadcast_to(inv, inv_ref.shape)
    z_val = z[...].astype(f32)
    sig = sigmoid(z_val)
    silu = z_val * sig
    y_val = y[...]
    gated = y_val * silu
    grad_o = go[...]
    ggain_ref[...] = jnp.sum(grad_o * gated * inv, axis=0, keepdims=True)
    grad_gin = inv * grad_o * gain[...] - gated * coef
    dy = grad_gin * silu
    dy_ref[...] = dy
    dz_ref[...] = (grad_gin * y_val * sig * (1.0 + z_val * (1.0 - sig))).astype(bf16)
    u_c = ubc[:, state_n:]
    c_mat = u_c * sigmoid(u_c)
    state_ref[...] = tn(dy * spread(jnp.exp(cum[...]), heads, width), c_mat)


def inner_back_kernel(
    heads, dy_ref, dz, cum_ref, dt, params, ux, ubc, state, raw, cot, inv, normed,
    dxs_ref, dbc_ref, dcum_ref, early_ref,
):
    rows, inner = dy_ref.shape
    width = inner // heads
    state_n = ubc.shape[1] // 2
    cum = cum_ref[...]
    cum_t = cum.T
    u_x, u_bc = ux[...], ubc[...]
    x_act = u_x * sigmoid(u_x)
    bc_act = u_bc * sigmoid(u_bc)
    b_mat = bc_act[:, 0:state_n].astype(bf16)
    c_mat = bc_act[:, state_n:].astype(bf16)
    lane = iota((rows, LANES), 1)
    step = jnp.where(lane < heads, softplus(dt[...] + params[0:1, :]), 0.0)
    scaled16 = (x_act * spread(step, heads, width)).astype(bf16)
    dy = dy_ref[...]
    dy16 = dy.astype(bf16)
    gram = nt(c_mat, b_mat)
    lower = iota((rows, rows), 0) >= iota((rows, rows), 1)
    pair_lane = iota((rows, 2 * width), 1)
    grad_gram = jnp.zeros((rows, rows), f32)
    dcum = jnp.zeros((rows, LANES), f32)
    sub = iota((LANES, rows), 0)
    dcum_t = jnp.zeros((LANES, rows), f32)
    for q in range(heads // 2):
        cut = slice(2 * width * q, 2 * width * (q + 1))
        both = []
        for h in (2 * q, 2 * q + 1):
            decay = jnp.exp(jnp.where(lower, cum[:, h : h + 1] - cum_t[h : h + 1, :], -jnp.inf))
            mix = decay * gram
            both.append(tn(mix, dy16[:, cut]))
            own = (pair_lane < width) == (h % 2 == 0)
            grad_mix = nt(jnp.where(own, dy[:, cut], 0.0), scaled16[:, cut])
            grad_gram = grad_gram + grad_mix * decay
            expo = grad_mix * mix
            dcum = jnp.where(lane == h, jnp.sum(expo, axis=1, keepdims=True), dcum)
            dcum_t = jnp.where(sub == h, jnp.sum(expo, axis=0, keepdims=True), dcum_t)
        dxs_ref[:, cut] = jnp.where(pair_lane < width, both[0], both[1])
    exp_cum = spread(jnp.exp(cum), heads, width)
    cross = nt(c_mat, state[...]) * exp_cum
    dcum_ref[...] = dcum - dcum_t.T + gathered_heads(dy * cross, heads, width)
    dbc_ref[:, 0:state_n] = tn(grad_gram, c_mat)
    dbc_ref[:, state_n:] = nn(dy * exp_cum, state[...]) + nn(grad_gram, b_mat)
    weighted = (cot[...].astype(f32) * inv[:, 0:1]).astype(bf16)
    early_ref[:, 0:inner] = tn(normed[...], dz[...]).astype(bf16)
    early_ref[:, inner:] = tn(weighted, raw[...]).astype(bf16)


def ssd_back_kernel(
    heads, next_ref, dxs, dbc, dcum_ref, dy_ref, cum_ref, dt, params, ux, ubc, state,
    gux_ref, gubc_ref, edge_ref, raw_ref, ghead_ref,
):
    rows, inner = dy_ref.shape
    width = inner // heads
    state_n = ubc.shape[1] // 2
    cum = cum_ref[...]
    u_x, u_bc = ux[...], ubc[...]
    sig_x, sig_bc = sigmoid(u_x), sigmoid(u_bc)
    x_act = u_x * sig_x
    bc_act = u_bc * sig_bc
    b_mat = bc_act[:, 0:state_n].astype(bf16)
    lane = iota((rows, LANES), 1)
    shifted = dt[...] + params[0:1, :]
    step = jnp.where(lane < heads, softplus(shifted), 0.0)
    rate = -jnp.exp(params[1:2, :])
    step_wide = spread(step, heads, width)
    scaled = x_act * step_wide
    dy = dy_ref[...]
    grad_next = next_ref[...]
    to_end = spread(jnp.exp(cum[rows - 1 : rows, :] - cum), heads, width)
    from_next = nt(b_mat, grad_next) * to_end
    grad_scaled = dxs[...] + from_next
    grad_b = dbc[:, 0:state_n] + nn(scaled * to_end, grad_next)
    end_term = gathered_heads(scaled * from_next, heads, width)
    held = jnp.sum(state[...] * grad_next, axis=1, keepdims=True)
    held = jnp.broadcast_to(held, (inner, LANES))
    head_of = iota((inner, LANES), 0) // width == iota((inner, LANES), 1)
    held = jnp.sum(jnp.where(head_of, held, 0.0), axis=0, keepdims=True)
    last = jnp.sum(end_term, axis=0, keepdims=True) + jnp.exp(cum[rows - 1 : rows, :]) * held
    upper = iota((rows, rows), 0) <= iota((rows, rows), 1)
    grad_log = last + lax.dot_general(
        upper.astype(f32),
        dcum_ref[...] - end_term,
        (((1,), (0,)), ((), ())),
        precision=exact,
        preferred_element_type=f32,
    )
    grad_step = gathered_heads(grad_scaled * x_act, heads, width) + grad_log * rate
    grad_raw = jnp.where(lane < heads, grad_step * sigmoid(shifted), 0.0)
    raw_ref[...] = grad_raw.astype(bf16)
    row = iota((8, LANES), 0)
    bias_grad = jnp.sum(grad_raw, axis=0, keepdims=True)
    rate_grad = jnp.sum(grad_log * step, axis=0, keepdims=True) * rate
    skip_grad = jnp.sum(gathered_heads(dy * x_act, heads, width), axis=0, keepdims=True)
    ghead_ref[...] = jnp.where(
        row == 0, bias_grad, jnp.where(row == 1, rate_grad, jnp.where(row == 2, skip_grad, 0.0))
    )
    skip = spread(jnp.broadcast_to(params[2:3, :], (rows, LANES)), heads, width)
    gux = (grad_scaled * step_wide + dy * skip) * (sig_x * (1.0 + u_x * (1.0 - sig_x)))
    gux_ref[...] = gux
    slope = sig_bc * (1.0 + u_bc * (1.0 - sig_bc))
    gubc_ref[:, 0:state_n] = grad_b * slope[:, 0:state_n]
    gubc_ref[:, state_n:] = dbc[:, state_n:] * slope[:, state_n:]
    edge_ref[:, 0:inner] = gux_ref[0:EDGE, :]
    edge_ref[:, inner:] = gubc_ref[0:EDGE, :]


def last_kernel(pair, gain_lane, n_zx, n_bcd, where, *refs):
    edge, gux, gubc, xe, be, dz, raw, normed, x_perm, inv, gain, conv_x, conv_bc = refs[:13]
    zx_pieces, bcd_pieces = refs[13 : 13 + n_zx], refs[13 + n_zx : 13 + n_zx + n_bcd]
    blocks_ref, gx_ref, gbc_ref, taps_ref, w_zx, w_bcd, gx_ext, gb_ext, x_ext, b_ext = refs[
        13 + n_zx + n_bcd :
    ]
    rows, inner = gux.shape
    wide_bc = gubc.shape[1]
    taps = conv_x.shape[0] - 1
    assembled(w_zx, zx_pieces, 0)
    assembled(w_bcd, bcd_pieces, 0)
    taps_ref[...] = jnp.zeros(taps_ref.shape, f32)

    def conv_back(grad, ext, raw_ref, raw_ext, weights, next_rows, first, width):
        value = grad[...]
        ext[0:rows, :] = value
        ext[rows : rows + EDGE, :] = next_rows
        raw_ext[...] = raw_ref[...].astype(f32)
        total = jnp.zeros((rows, width), f32)
        for k in range(taps):
            ahead = taps - 1 - k
            total = total + weights[k : k + 1, :] * ext[ahead : ahead + rows, :]
            back = HALO - taps + 1 + k
            taps_ref[first + k : first + k + 1, 0:width] = jnp.sum(
                raw_ext[back : back + rows, :] * value, axis=0, keepdims=True
            )
        taps_ref[first + taps : first + taps + 1, 0:width] = jnp.sum(value, axis=0, keepdims=True)
        return total.astype(bf16)

    dx = conv_back(gux, gx_ext, xe, x_ext, conv_x, edge[:, 0:inner], 0, inner)
    dbc = conv_back(gubc, gb_ext, be, b_ext, conv_bc, edge[:, inner:], taps + 1, wide_bc)
    dbcd = jnp.concatenate([dbc, raw[...]], axis=1)
    part = (
        nt(dz[...], w_zx[:, 0:inner]) + nt(dx, w_zx[:, inner:]) + nt(dbcd, w_bcd[...])
    )
    for p in range(part.shape[1] // LANES):
        block, lane = unit(pair, p, where)
        blocks_ref[block, 0:rows, pl.ds(lane, LANES)] = part[:, p * LANES : (p + 1) * LANES].astype(bf16)
    along = part * (x_perm[...].astype(f32) * inv[:, 0:1])
    dots = row_of(jnp.sum(along * gain[...], axis=1, keepdims=True))
    high = dots.astype(bf16).astype(f32)
    extra = jnp.where(iota((16, rows), 0) == 0, high, dots - high)
    extra = jnp.where(iota((16, rows), 0) < 2, extra, 0.0).astype(bf16)
    for k in range(blocks_ref.shape[0]):
        blocks_ref[k, rows : rows + 16, :] = extra
    gx_ref[...] = tn(normed[...], dx).astype(bf16)
    g_bcd = tn(normed[...], dbcd)
    g_gain = tn(along, jnp.ones((rows, LANES), bf16))
    at = iota((part.shape[1], LANES), 1) == gain_lane
    gbc_ref[:, 0:wide_bc] = g_bcd[:, 0:wide_bc].astype(bf16)
    gbc_ref[:, wide_bc:] = jnp.where(at, g_gain, g_bcd[:, wide_bc:]).astype(bf16)


def input_kernel(pair, full_d, n_blocks, where, *refs):
    blocks = refs[:n_blocks]
    x_local, cot, inv, gain, out = refs[n_blocks:]
    rows, part = x_local.shape
    total = tree_sum([b[...].astype(f32) for b in blocks])
    dots = column_of((total[rows : rows + 1, :] + total[rows + 1 : rows + 2, :]) / full_d)[:, 0:1]
    scale = inv[:, 0:1]
    for p in range(gain.shape[1] // LANES):
        block, lane = unit(pair, p, where)

        @pl.when(block == 0)
        def _():
            cut = pl.ds(lane, LANES)
            xhat = x_local[:, cut].astype(f32) * scale
            out[:, cut] = gain[:, p * LANES : (p + 1) * LANES] + 0.0 * xhat

    gains = out[...]
    xhat = x_local[...].astype(f32) * scale
    out[...] = cot[...].astype(f32) + scale * (total[0:rows, :] * gains - xhat * dots)


VMEM = pl.BlockSpec(memory_space=pltpu.VMEM)
SMEM = pl.BlockSpec(memory_space=pltpu.SMEM)


def call(kernel, name, outs, inputs, scratch=(), scalars=0):
    return pl.pallas_call(
        kernel,
        out_shape=[jax.ShapeDtypeStruct(shape, kind) for shape, kind in outs],
        in_specs=[SMEM] * scalars + [VMEM] * (len(inputs) - scalars),
        out_specs=[VMEM] * len(outs),
        scratch_shapes=[pltpu.VMEM(shape, kind) for shape, kind in scratch],
        name=name,
    )(*inputs)


def local(
    hidden_in, cotangent, norm_gain, w_zx, w_bc, w_dt, w_out, conv_x, conv_bc, head_params, gate_gain
):
    rows, part_d = hidden_in.shape[2:]
    heads = head_params.shape[1]
    inner = conv_x.shape[1]
    wide_bc = w_bc.shape[1]
    taps = conv_x.shape[0] - 1
    shard = w_zx.shape[0]
    dp_n, seq_n, head_n = lax.axis_size("dp"), lax.axis_size("seq"), lax.axis_size("head")
    full_d = part_d * head_n
    full_inner = inner * head_n
    dp_i, seq_i, head_i = lax.axis_index("dp"), lax.axis_index("seq"), lax.axis_index("head")
    pair = seq_n == 2 and dp_n == head_n == 4 and shard == LANES and part_d == 2 * LANES
    state_n = wide_bc // 2

    where = jnp.stack([head_i ^ dp_i, seq_i] if pair else [head_i, seq_i]).astype(jnp.int32)

    def gathered(part, axis):
        if not pair:
            return [lax.all_gather(part, ("dp", "seq"), axis=axis, tiled=True)]
        own = exchanged(part, "dp")
        return own + [lax.ppermute(p, "seq", xor_route(2, 1)) for p in own]

    def reduced(array):
        if not pair:
            return lax.psum_scatter(
                array.astype(f32), ("dp", "seq"), scatter_dimension=0, tiled=True
            )
        half = dp_n * shard
        both = f32_sum([array[:half], lax.ppermute(array[half:], "seq", xor_route(2, 1))])
        both = both.astype(bf16)
        return f32_sum(
            scattered([both[k * shard : (k + 1) * shard] for k in range(dp_n)], "dp")
        )

    def summed(array):
        if not pair:
            return lax.psum(array, ("dp", "seq"))
        array = array + lax.ppermute(array, "seq", xor_route(2, 1))
        return tree_sum(exchanged(array, "dp"))

    x_local = hidden_in[0, 0]
    cot_local = cotangent[0, 0]
    pad = jnp.zeros((shard, LANES - heads - 1), bf16)
    bcd_pieces = gathered(jnp.concatenate([w_bc, w_dt, norm_gain[:, None], pad], axis=1), 0)
    zx_pieces = gathered(w_zx.reshape(shard, 2 * inner), 0)
    x_blocks = exchanged(x_local, "head")
    out_pieces = gathered(w_out, 1)
    cot_blocks = exchanged(cot_local, "head")
    params = jnp.pad(head_params, ((0, 5), (0, LANES - heads)))
    gain_row = gate_gain[None]
    n_zx, n_bcd, n_out = len(zx_pieces), len(bcd_pieces), len(out_pieces)

    normed, x_perm, inv_in, norm_row, edge = call(
        functools.partial(norm_kernel, pair, heads, head_n, n_bcd),
        "norm",
        [
            ((rows, full_d), bf16),
            ((rows, full_d), bf16),
            ((rows, LANES), f32),
            ((1, full_d), f32),
            ((HALO, full_d), bf16),
        ],
        [where, *x_blocks, *bcd_pieces],
        [((head_n, rows, part_d), f32)],
        1,
    )
    edge = passed_along(edge, "seq", 1)
    wide_bcd = wide_bc + LANES
    z, x_ext, bc_ext, u_x, u_bc, dt, cum, y_loc, own_state = call(
        functools.partial(forward_kernel, heads, n_zx, n_bcd),
        "forward",
        [
            ((rows, inner), bf16),
            ((HALO + rows, inner), bf16),
            ((HALO + rows, wide_bc), bf16),
            ((rows, inner), f32),
            ((rows, wide_bc), f32),
            ((rows, LANES), f32),
            ((rows, LANES), f32),
            ((rows, inner), f32),
            ((inner, state_n), f32),
        ],
        [normed, edge, conv_x, conv_bc, params, *zx_pieces, *bcd_pieces],
        [
            ((full_d, 2 * inner), bf16),
            ((full_d, wide_bcd), bf16),
            ((HALO + rows, full_d), bf16),
            ((HALO + rows, inner), f32),
            ((HALO + rows, wide_bc), f32),
        ],
    )
    total_decay = jnp.repeat(jnp.exp(cum[rows - 1, :heads]), inner // heads)[:, None]
    state_in = entering(total_decay, own_state, "seq", False)
    y, grad_o, gated_raw, stats, cot_perm, w_out_full = call(
        functools.partial(gate_kernel, pair, heads, head_n, n_out),
        "gate",
        [
            ((rows, inner), f32),
            ((rows, inner), f32),
            ((rows, inner), bf16),
            ((8, rows), f32),
            ((rows, full_d), bf16),
            ((inner, full_d), bf16),
        ],
        [where, state_in, u_bc, cum, y_loc, z, gain_row, *cot_blocks, *out_pieces],
        [((head_n, rows, part_d), f32)],
        1,
    )
    stats = exchanged(stats, "head")
    (out_blocks,) = call(
        functools.partial(out_kernel, pair),
        "out",
        [((head_n, rows, part_d), bf16)],
        [where, gated_raw, w_out_full],
        (),
        1,
    )
    out_sum = f32_sum(scattered([out_blocks[k] for k in range(head_n)], "head"))

    dy, dz, from_cross, inv_gate, g_ggain = call(
        functools.partial(gate_back_kernel, heads, full_inner, head_n),
        "gate_back",
        [
            ((rows, inner), f32),
            ((rows, inner), bf16),
            ((inner, state_n), f32),
            ((rows, LANES), f32),
            ((1, inner), f32),
        ],
        [*stats, grad_o, y, z, gain_row, u_bc, cum],
    )
    output = (x_local.astype(f32) + out_sum * inv_gate[:, :1]).astype(bf16)
    grad_next = entering(total_decay, from_cross, "seq", True)
    dxs, dbc, dcum, early = call(
        functools.partial(inner_back_kernel, heads),
        "inner_back",
        [
            ((rows, inner), f32),
            ((rows, wide_bc), f32),
            ((rows, LANES), f32),
            ((full_d, 2 * inner), bf16),
        ],
        [dy, dz, cum, dt, params, u_x, u_bc, state_in, gated_raw, cot_perm, inv_gate, normed],
    )
    early = reduced(early)
    gux, gubc, edge_out, raw16, g_head = call(
        functools.partial(ssd_back_kernel, heads),
        "ssd_back",
        [
            ((rows, inner), f32),
            ((rows, wide_bc), f32),
            ((EDGE, inner + wide_bc), f32),
            ((rows, LANES), bf16),
            ((8, LANES), f32),
        ],
        [grad_next, dxs, dbc, dcum, dy, cum, dt, params, u_x, u_bc, state_in],
    )
    edge_next = passed_along(edge_out, "seq", -1)
    n = taps + 1
    blocks, g_x, g_bcd, tap_grads = call(
        functools.partial(last_kernel, pair, heads, n_zx, n_bcd),
        "last",
        [
            ((head_n, rows + 16, part_d), bf16),
            ((full_d, inner), bf16),
            ((full_d, wide_bcd), bf16),
            ((16, inner), f32),
        ],
        [
            where, edge_next, gux, gubc, x_ext, bc_ext, dz, raw16, normed, x_perm, inv_in, norm_row,
            conv_x, conv_bc, *zx_pieces, *bcd_pieces,
        ],
        [
            ((full_d, 2 * inner), bf16),
            ((full_d, wide_bcd), bf16),
            ((rows + EDGE, inner), f32),
            ((rows + EDGE, wide_bc), f32),
            ((HALO + rows, inner), f32),
            ((HALO + rows, wide_bc), f32),
        ],
        1,
    )
    g_bcd = reduced(g_bcd)
    small = jnp.concatenate(
        [tap_grads[: 2 * n], g_ggain, jnp.pad(g_head[:3], ((0, 0), (0, inner - LANES)))], axis=0
    )
    small = summed(small)
    g_x = reduced(g_x)
    parts = scattered([blocks[k] for k in range(head_n)], "head")
    (grad_input,) = call(
        functools.partial(input_kernel, pair, full_d, head_n),
        "input",
        [((rows, part_d), f32)],
        [where, *parts, x_local, cot_local, inv_in, norm_row],
        (),
        1,
    )
    grad_input = grad_input.astype(bf16)
    shared = jnp.concatenate(
        [g_bcd, jnp.pad(small[n : 2 * n, :wide_bc], ((0, 8 - n), (0, LANES)))], axis=0
    )
    shared = tree_sum(exchanged(shared, "head"))
    g_zx = jnp.stack([early[:, :inner], g_x], axis=1)
    return (
        output[None, None],
        grad_input[None, None],
        shared[:shard, wide_bc + heads],
        g_zx,
        shared[:shard, :wide_bc],
        g_bcd[:, wide_bc : wide_bc + heads],
        early[:, inner:].T,
        small[:n],
        shared[shard : shard + n, :wide_bc],
        small[2 * n + 1 : 2 * n + 4, :heads],
        small[2 * n],
    )


def solution(mesh):
    tokens = P(None, "dp", "seq", "head")
    zx = P(("dp", "seq"), None, "head")
    bc = P(("dp", "seq"), None)
    dt = P(("dp", "seq"), "head")
    out = P("head", ("dp", "seq"))
    gain, heads = P(("dp", "seq")), P(None, "head")
    return jax.shard_map(
        local,
        mesh=mesh,
        in_specs=(tokens, tokens, gain, zx, bc, dt, out, heads, P(), heads, P("head")),
        out_specs=(tokens, tokens, gain, zx, bc, dt, out, heads, P(), heads, P("head")),
        check_vma=False,
    )
```

```python
import functools

import jax
import jax.numpy as jnp
from jax import lax
from jax.experimental import pallas as pl
from jax.experimental.pallas import tpu as pltpu
from jax.sharding import PartitionSpec as P


epsilon = 1e-05
f32 = jnp.float32
bf16 = jnp.bfloat16
exact = lax.Precision.HIGHEST
LANES = 128
HALO = 16
EDGE = 8


def xor_route(count, k):
    return [(i, i ^ k) for i in range(count)]


def sent(block, axis, k):
    return lax.ppermute(block, axis, xor_route(lax.axis_size(axis), k))


def exchanged(block, axis):
    count = lax.axis_size(axis)
    return [block] + [sent(block, axis, k) for k in range(1, count)]


def scattered(blocks, axis):
    count = lax.axis_size(axis)
    return [blocks[0]] + [sent(blocks[k], axis, k) for k in range(1, count)]


def tree_sum(parts):
    while len(parts) > 1:
        parts = [a + b for a, b in zip(parts[0::2], parts[1::2])]
    return parts[0]


def f32_sum(parts):
    return tree_sum([part.astype(f32) for part in parts])


def passed_along(block, axis, distance):
    devices = range(lax.axis_size(axis))
    route = [(i - distance, i) for i in devices if i - distance in devices]
    return lax.ppermute(block, axis, route)


def entering(decay, state, axis, reverse):
    count, place = lax.axis_size(axis), lax.axis_index(axis)
    if count == 2:
        return passed_along(state, axis, -1 if reverse else 1)
    decays, states = lax.all_gather(decay, axis), lax.all_gather(state, axis)

    def turn(k, before):
        at = count - 1 - k if reverse else k
        reached = at > place if reverse else at < place
        return jnp.where(reached, decays[at] * before + states[at], before)

    return lax.fori_loop(0, count, turn, jnp.zeros_like(state))


def dot(a, b, left, right):
    return lax.dot_general(
        a.astype(bf16), b.astype(bf16), (((left,), (right,)), ((), ())), preferred_element_type=f32
    )


def nn(a, b):
    return dot(a, b, 1, 0)


def nt(a, b):
    return dot(a, b, 1, 1)


def tn(a, b):
    return dot(a, b, 0, 0)


def sigmoid(v):
    return 1.0 / (1.0 + jnp.exp(-v))


def softplus(v):
    e = jnp.exp(-jnp.abs(v))
    small = e * (1.0 - e * (0.5 - e * (1.0 / 3.0 - e * 0.25)))
    return jnp.maximum(v, 0.0) + jnp.where(e < 0.03, small, jnp.log(1.0 + e))


def iota(shape, axis):
    return lax.broadcasted_iota(jnp.int32, shape, axis)


def row_of(column):
    return jnp.broadcast_to(column, (column.shape[0], LANES)).T[0:1]


def column_of(row):
    return jnp.broadcast_to(row, (LANES, row.shape[1])).T


def per_head(values, pair_at, width):
    first = values[:, 2 * pair_at : 2 * pair_at + 1]
    second = values[:, 2 * pair_at + 1 : 2 * pair_at + 2]
    lane = iota((values.shape[0], 2 * width), 1)
    return jnp.where(lane < width, first, second)


def spread(values, heads, width):
    return jnp.concatenate([per_head(values, q, width) for q in range(heads // 2)], axis=1)


def gathered_heads(values, heads, width):
    lane = iota((values.shape[0], LANES), 1)
    wide = iota((values.shape[0], 2 * width), 1)
    total = jnp.zeros((values.shape[0], LANES), f32)
    for q in range(heads // 2):
        both = values[:, 2 * width * q : 2 * width * (q + 1)]
        first = jnp.sum(jnp.where(wide < width, both, 0.0), axis=1, keepdims=True)
        second = jnp.sum(jnp.where(wide < width, 0.0, both), axis=1, keepdims=True)
        total = jnp.where(lane == 2 * q, first, total)
        total = jnp.where(lane == 2 * q + 1, second, total)
    return total


def unit(pair, p, where):
    if pair:
        t, k = divmod(p, 4)
        return k ^ where[0], pl.multiple_of((t ^ where[1]) * LANES, LANES)
    j, u = divmod(p, 2)
    return j ^ where[0], u * LANES


def assembled(scratch, pieces, axis):
    at = 0
    for piece in pieces:
        size = piece.shape[axis]
        if axis == 0:
            scratch[at : at + size, :] = piece[...]
        else:
            scratch[:, at : at + size] = piece[...]
        at += size


def norm_kernel(pair, gain_lane, n_blocks, n_pieces, where, *refs):
    blocks, pieces = refs[:n_blocks], refs[n_blocks : n_blocks + n_pieces]
    normed, x_perm, inv_ref, gain_ref, edge_ref, hold = refs[n_blocks + n_pieces :]
    rows, part = blocks[0].shape
    swap = n_blocks * part // LANES // 2 if pair else 0
    total = jnp.zeros((rows, 1), f32)
    for k, block in enumerate(blocks):
        value = block[...].astype(f32)
        hold[k] = value
        total += jnp.sum(value * value, axis=1, keepdims=True)
    inv = lax.rsqrt(total / (n_blocks * part) + epsilon)
    inv_ref[...] = jnp.broadcast_to(inv, inv_ref.shape)
    eye = iota((LANES, LANES), 0) == iota((LANES, LANES), 1)
    per_piece = pieces[0].shape[0] // LANES
    for p in range(n_blocks * part // LANES):
        piece = pieces[p // per_piece]
        at = p % per_piece * LANES
        tile = piece.shape[1] - LANES
        gain = piece[at : at + LANES, tile : tile + LANES][:, gain_lane : gain_lane + 1]
        gain = jnp.sum(jnp.where(eye, gain.astype(f32), 0.0), axis=0, keepdims=True)
        block, lane = unit(pair, p, where)
        value = hold[block, :, pl.ds(lane, LANES)]
        cut = slice(p * LANES, (p + 1) * LANES)
        value16 = (value * inv * gain).astype(bf16)
        normed[:, cut] = value16
        there = p ^ swap
        edge_ref[:, there * LANES : (there + 1) * LANES] = value16[rows - HALO :, :]
        x_perm[:, cut] = value.astype(bf16)
        gain_ref[:, cut] = gain


def forward_kernel(heads, n_pieces, *refs):
    normed, edge, conv_x, conv_bc, params = refs[:5]
    pieces = refs[5 : 5 + n_pieces]
    (z_ref, xe_ref, be_ref, ux_ref, ubc_ref, dt_ref, cum_ref, y_ref, state_ref, w_in) = refs[
        5 + n_pieces : 15 + n_pieces
    ]
    rows_in, xe, be = refs[15 + n_pieces :]
    rows, inner = ux_ref.shape
    width = inner // heads
    state_n = ubc_ref.shape[1] // 2
    taps = conv_x.shape[0] - 1
    assembled(w_in, pieces, 0)
    rows_in[0:HALO, :] = edge[...]
    rows_in[HALO : HALO + rows, :] = normed[...]
    z_ref[...] = nn(normed[...], w_in[:, 0:inner]).astype(bf16)
    x_raw = nn(rows_in[...], w_in[:, inner : 2 * inner]).astype(bf16)
    xe_ref[...] = x_raw
    xe[...] = x_raw.astype(f32)
    bcd = nn(rows_in[...], w_in[:, 2 * inner :])
    bc_raw = bcd[:, 0 : 2 * state_n].astype(bf16)
    be_ref[...] = bc_raw
    be[...] = bc_raw.astype(f32)
    dt = bcd[HALO:, 2 * state_n :]
    dt_ref[...] = dt

    def conv(extended, weights):
        total = weights[taps : taps + 1, :]
        for k in range(taps):
            total = total + weights[k : k + 1, :] * extended[
                HALO - taps + 1 + k : HALO - taps + 1 + k + rows, :
            ]
        return total

    u_x = conv(xe, conv_x)
    ux_ref[...] = u_x
    u_bc = conv(be, conv_bc)
    ubc_ref[...] = u_bc
    x_act = u_x * sigmoid(u_x)
    bc_act = u_bc * sigmoid(u_bc)
    b_mat = bc_act[:, 0:state_n].astype(bf16)
    c_mat = bc_act[:, state_n:].astype(bf16)
    lane = iota((rows, LANES), 1)
    step = jnp.where(lane < heads, softplus(dt + params[0:1, :]), 0.0)
    lower = iota((rows, rows), 0) >= iota((rows, rows), 1)
    cum = lax.dot_general(
        lower.astype(f32),
        -step * jnp.exp(params[1:2, :]),
        (((1,), (0,)), ((), ())),
        precision=exact,
        preferred_element_type=f32,
    )
    cum_ref[...] = cum
    cum_t = cum.T
    gram = nt(c_mat, b_mat)
    scaled = x_act * spread(step, heads, width)
    scaled16 = scaled.astype(bf16)
    pair_lane = iota((rows, 2 * width), 1)
    for q in range(heads // 2):
        cut = slice(2 * width * q, 2 * width * (q + 1))
        both = []
        for h in (2 * q, 2 * q + 1):
            decay = jnp.exp(jnp.where(lower, cum[:, h : h + 1] - cum_t[h : h + 1, :], -jnp.inf))
            both.append(nn(decay * gram, scaled16[:, cut]))
        y_ref[:, cut] = (
            jnp.where(pair_lane < width, both[0], both[1])
            + x_act[:, cut] * per_head(jnp.broadcast_to(params[2:3, :], (rows, LANES)), q, width)
        )
    to_end = jnp.exp(cum[rows - 1 : rows, :] - cum)
    state_ref[...] = tn(scaled * spread(to_end, heads, width), b_mat)


def gate_kernel(pair, heads, n_blocks, n_pieces, where, *refs):
    state, ubc, cum, y_loc, z, gain = refs[:6]
    blocks = refs[6 : 6 + n_blocks]
    pieces = refs[6 + n_blocks : 6 + n_blocks + n_pieces]
    y_ref, go_ref, raw_ref, stats_ref, cot_ref, w_ref, hold = refs[6 + n_blocks + n_pieces :]
    rows, inner = y_ref.shape
    width = inner // heads
    state_n = ubc.shape[1] // 2
    assembled(w_ref, pieces, 1)
    for k, block in enumerate(blocks):
        hold[k] = block[...].astype(f32)
    for p in range(cot_ref.shape[1] // LANES):
        block, lane = unit(pair, p, where)
        cot_ref[:, p * LANES : (p + 1) * LANES] = hold[block, :, pl.ds(lane, LANES)].astype(bf16)
    u_c = ubc[:, state_n:]
    c_mat = u_c * sigmoid(u_c)
    y = y_loc[...] + nt(c_mat, state[...]) * spread(jnp.exp(cum[...]), heads, width)
    y_ref[...] = y
    z_val = z[...].astype(f32)
    gated = y * z_val * sigmoid(z_val)
    raw_ref[...] = (gated * gain[...]).astype(bf16)
    grad_o = nt(cot_ref[...], w_ref[...])
    go_ref[...] = grad_o
    squares = jnp.sum(gated * gated, axis=1, keepdims=True)
    cross = jnp.sum(grad_o * gain[...] * gated, axis=1, keepdims=True)
    lane = iota((rows, LANES), 1)
    both = jnp.where(lane == 0, squares, jnp.where(lane == 1, cross, 0.0))
    stats_ref[...] = both.T[0:8, :]


def out_kernel(pair, where, raw, weights, *refs):
    hold = refs[-1]
    part = nn(raw[...], weights[...]).astype(bf16)
    for p in range(weights.shape[1] // LANES):
        block, lane = unit(pair, p, where)
        hold[block, :, pl.ds(lane, LANES)] = part[:, p * LANES : (p + 1) * LANES]
    for k, ref in enumerate(refs[:-1]):
        ref[...] = hold[k]


def gate_back_kernel(heads, full_inner, n_stats, *refs):
    stats = refs[:n_stats]
    go, y, z, gain, ubc, cum = refs[n_stats : n_stats + 6]
    dy_ref, dz_ref, state_ref, inv_ref, ggain_ref = refs[n_stats + 6 :]
    rows, inner = y.shape
    width = inner // heads
    state_n = ubc.shape[1] // 2
    total = tree_sum([s[...] for s in stats])
    total = jnp.concatenate([total, jnp.zeros((LANES - total.shape[0], rows), f32)], axis=0).T
    inv = lax.rsqrt(total[:, 0:1] / full_inner + epsilon)
    coef = inv * inv * inv * (total[:, 1:2] / full_inner)
    inv_ref[...] = jnp.broadcast_to(inv, inv_ref.shape)
    z_val = z[...].astype(f32)
    sig = sigmoid(z_val)
    silu = z_val * sig
    y_val = y[...]
    gated = y_val * silu
    grad_o = go[...]
    ggain_ref[...] = jnp.sum(grad_o * gated * inv, axis=0, keepdims=True)
    grad_gin = inv * grad_o * gain[...] - gated * coef
    dy = grad_gin * silu
    dy_ref[...] = dy
    dz_ref[...] = (grad_gin * y_val * sig * (1.0 + z_val * (1.0 - sig))).astype(bf16)
    u_c = ubc[:, state_n:]
    c_mat = u_c * sigmoid(u_c)
    state_ref[...] = tn(dy * spread(jnp.exp(cum[...]), heads, width), c_mat)


def inner_back_kernel(
    heads, dy_ref, dz, cum_ref, dt, params, ux, ubc, state, raw, cot, inv, normed,
    dxs_ref, dbc_ref, dcum_ref, own_ref, other_ref,
):
    rows, inner = dy_ref.shape
    width = inner // heads
    state_n = ubc.shape[1] // 2
    cum = cum_ref[...]
    cum_t = cum.T
    u_x, u_bc = ux[...], ubc[...]
    x_act = u_x * sigmoid(u_x)
    bc_act = u_bc * sigmoid(u_bc)
    b_mat = bc_act[:, 0:state_n].astype(bf16)
    c_mat = bc_act[:, state_n:].astype(bf16)
    lane = iota((rows, LANES), 1)
    step = jnp.where(lane < heads, softplus(dt[...] + params[0:1, :]), 0.0)
    scaled16 = (x_act * spread(step, heads, width)).astype(bf16)
    dy = dy_ref[...]
    dy16 = dy.astype(bf16)
    gram = nt(c_mat, b_mat)
    lower = iota((rows, rows), 0) >= iota((rows, rows), 1)
    pair_lane = iota((rows, 2 * width), 1)
    grad_gram = jnp.zeros((rows, rows), f32)
    dcum = jnp.zeros((rows, LANES), f32)
    sub = iota((LANES, rows), 0)
    dcum_t = jnp.zeros((LANES, rows), f32)
    for q in range(heads // 2):
        cut = slice(2 * width * q, 2 * width * (q + 1))
        both = []
        for h in (2 * q, 2 * q + 1):
            decay = jnp.exp(jnp.where(lower, cum[:, h : h + 1] - cum_t[h : h + 1, :], -jnp.inf))
            mix = decay * gram
            both.append(tn(mix, dy16[:, cut]))
            own = (pair_lane < width) == (h % 2 == 0)
            grad_mix = nt(jnp.where(own, dy[:, cut], 0.0), scaled16[:, cut])
            grad_gram = grad_gram + grad_mix * decay
            expo = grad_mix * mix
            dcum = jnp.where(lane == h, jnp.sum(expo, axis=1, keepdims=True), dcum)
            dcum_t = jnp.where(sub == h, jnp.sum(expo, axis=0, keepdims=True), dcum_t)
        dxs_ref[:, cut] = jnp.where(pair_lane < width, both[0], both[1])
    exp_cum = spread(jnp.exp(cum), heads, width)
    cross = nt(c_mat, state[...]) * exp_cum
    dcum_ref[...] = dcum - dcum_t.T + gathered_heads(dy * cross, heads, width)
    dbc_ref[:, 0:state_n] = tn(grad_gram, c_mat)
    dbc_ref[:, state_n:] = nn(dy * exp_cum, state[...]) + nn(grad_gram, b_mat)
    weighted = (cot[...].astype(f32) * inv[:, 0:1]).astype(bf16)
    half = own_ref.shape[0]
    for ref, cut in ((own_ref, slice(0, half)), (other_ref, slice(half, 2 * half))):
        ref[:, 0:inner] = tn(normed[:, cut], dz[...]).astype(bf16)
        ref[:, inner:] = tn(weighted[:, cut], raw[...]).astype(bf16)


def ssd_back_kernel(
    heads, next_ref, dxs, dbc, dcum_ref, dy_ref, cum_ref, dt, params, ux, ubc, state,
    gux_ref, gubc_ref, edge_ref, raw_ref, ghead_ref,
):
    rows, inner = dy_ref.shape
    width = inner // heads
    state_n = ubc.shape[1] // 2
    cum = cum_ref[...]
    u_x, u_bc = ux[...], ubc[...]
    sig_x, sig_bc = sigmoid(u_x), sigmoid(u_bc)
    x_act = u_x * sig_x
    bc_act = u_bc * sig_bc
    b_mat = bc_act[:, 0:state_n].astype(bf16)
    lane = iota((rows, LANES), 1)
    shifted = dt[...] + params[0:1, :]
    step = jnp.where(lane < heads, softplus(shifted), 0.0)
    rate = -jnp.exp(params[1:2, :])
    step_wide = spread(step, heads, width)
    scaled = x_act * step_wide
    dy = dy_ref[...]
    grad_next = next_ref[...]
    to_end = spread(jnp.exp(cum[rows - 1 : rows, :] - cum), heads, width)
    from_next = nt(b_mat, grad_next) * to_end
    grad_scaled = dxs[...] + from_next
    grad_b = dbc[:, 0:state_n] + nn(scaled * to_end, grad_next)
    end_term = gathered_heads(scaled * from_next, heads, width)
    held = jnp.sum(state[...] * grad_next, axis=1, keepdims=True)
    held = jnp.broadcast_to(held, (inner, LANES))
    head_of = iota((inner, LANES), 0) // width == iota((inner, LANES), 1)
    held = jnp.sum(jnp.where(head_of, held, 0.0), axis=0, keepdims=True)
    last = jnp.sum(end_term, axis=0, keepdims=True) + jnp.exp(cum[rows - 1 : rows, :]) * held
    upper = iota((rows, rows), 0) <= iota((rows, rows), 1)
    grad_log = last + lax.dot_general(
        upper.astype(f32),
        dcum_ref[...] - end_term,
        (((1,), (0,)), ((), ())),
        precision=exact,
        preferred_element_type=f32,
    )
    grad_step = gathered_heads(grad_scaled * x_act, heads, width) + grad_log * rate
    grad_raw = jnp.where(lane < heads, grad_step * sigmoid(shifted), 0.0)
    raw_ref[...] = grad_raw.astype(bf16)
    row = iota((8, LANES), 0)
    bias_grad = jnp.sum(grad_raw, axis=0, keepdims=True)
    rate_grad = jnp.sum(grad_log * step, axis=0, keepdims=True) * rate
    skip_grad = jnp.sum(gathered_heads(dy * x_act, heads, width), axis=0, keepdims=True)
    ghead_ref[...] = jnp.where(
        row == 0, bias_grad, jnp.where(row == 1, rate_grad, jnp.where(row == 2, skip_grad, 0.0))
    )
    skip = spread(jnp.broadcast_to(params[2:3, :], (rows, LANES)), heads, width)
    gux = (grad_scaled * step_wide + dy * skip) * (sig_x * (1.0 + u_x * (1.0 - sig_x)))
    gux_ref[...] = gux
    slope = sig_bc * (1.0 + u_bc * (1.0 - sig_bc))
    gubc_ref[:, 0:state_n] = grad_b * slope[:, 0:state_n]
    gubc_ref[:, state_n:] = dbc[:, state_n:] * slope[:, state_n:]
    edge_ref[:, 0:inner] = gux_ref[0:EDGE, :]
    edge_ref[:, inner:] = gubc_ref[0:EDGE, :]


def last_kernel(pair, gain_lane, n_blocks, where, *refs):
    edge, gux, gubc, xe, be, dz, raw, normed, x_perm, inv, gain, conv_x, conv_bc, w_in = refs[:14]
    ggain, ghead = refs[14:16]
    blocks = refs[16 : 16 + n_blocks]
    gx_own, gx_other, gb_own, gb_other = refs[16 + n_blocks : 20 + n_blocks]
    hold, gx_ext, gb_ext, x_ext, b_ext, small = refs[20 + n_blocks :]
    rows, inner = gux.shape
    wide_bc = gubc.shape[1]
    taps = conv_x.shape[0] - 1
    small[...] = jnp.zeros(small.shape, f32)

    def conv_back(grad, ext, raw_ref, raw_ext, weights, next_rows, firsts, width):
        value = grad[...]
        ext[0:rows, :] = value
        ext[rows : rows + EDGE, :] = next_rows
        raw_ext[...] = raw_ref[...].astype(f32)

        def kept(k, row):
            for j, first in enumerate(firsts):
                small[first + k : first + k + 1, 0:wide_bc] = row[:, j * wide_bc : (j + 1) * wide_bc]

        total = jnp.zeros((rows, width), f32)
        for k in range(taps):
            ahead = taps - 1 - k
            total = total + weights[k : k + 1, :] * ext[ahead : ahead + rows, :]
            back = HALO - taps + 1 + k
            kept(k, jnp.sum(raw_ext[back : back + rows, :] * value, axis=0, keepdims=True))
        kept(taps, jnp.sum(value, axis=0, keepdims=True))
        return total.astype(bf16)

    n = taps + 1
    dx = conv_back(gux, gx_ext, xe, x_ext, conv_x, edge[:, 0:inner], (0, n), inner)
    dbc = conv_back(gubc, gb_ext, be, b_ext, conv_bc, edge[:, inner:], (2 * n,), wide_bc)
    for j in range(2):
        small[3 * n + j : 3 * n + j + 1, 0:wide_bc] = ggain[:, j * wide_bc : (j + 1) * wide_bc]
    small[3 * n + 2 : 3 * n + 5, 0:LANES] = ghead[0:3, :]
    dbcd = jnp.concatenate([dbc, raw[...]], axis=1)
    part = (
        nt(dz[...], w_in[:, 0:inner])
        + nt(dx, w_in[:, inner : 2 * inner])
        + nt(dbcd, w_in[:, 2 * inner :])
    )
    for p in range(part.shape[1] // LANES):
        block, lane = unit(pair, p, where)
        hold[block, :, pl.ds(lane, LANES)] = part[:, p * LANES : (p + 1) * LANES].astype(bf16)
    along = part * (x_perm[...].astype(f32) * inv[:, 0:1])
    dots = row_of(jnp.sum(along * gain[...], axis=1, keepdims=True))
    high = dots.astype(bf16).astype(f32)
    extra = jnp.where(iota((16, rows), 0) == 0, high, dots - high)
    extra = jnp.where(iota((16, rows), 0) < 2, extra, 0.0).astype(bf16)
    for k, ref in enumerate(blocks):
        ref[0:rows, :] = hold[k]
        ref[rows : rows + 16, :] = extra
    half = gx_own.shape[0]
    at = iota((half, LANES), 1) == gain_lane
    high = small[...].astype(bf16)
    low = (small[...] - high.astype(f32)).astype(bf16)
    count = small.shape[0]
    for cut, gx_ref, gb_ref in (
        (slice(0, half), gx_own, gb_own),
        (slice(half, 2 * half), gx_other, gb_other),
    ):
        gx_ref[...] = tn(normed[:, cut], dx).astype(bf16)
        g_bcd = tn(normed[:, cut], dbcd)
        g_gain = tn(along[:, cut], jnp.ones((rows, LANES), bf16))
        gb_ref[0:half, 0:wide_bc] = g_bcd[:, 0:wide_bc].astype(bf16)
        gb_ref[0:half, wide_bc:] = jnp.where(at, g_gain, g_bcd[:, wide_bc:]).astype(bf16)
        gb_ref[half : half + count, :] = high
        gb_ref[half + count :, :] = low


def fold_kernel(n_blocks, own, other, *blocks):
    size = (own.shape[0] - blocks[0].shape[0]) // (n_blocks - 1)
    extra = blocks[0].shape[0] - size
    for k, ref in enumerate(blocks):
        cut = slice(k * size, (k + 1) * size)
        ref[0:size, :] = (own[cut, :].astype(f32) + other[cut, :].astype(f32)).astype(bf16)
    if extra > 0:
        first, half = n_blocks * size, extra // 2
        total = [ref[first:, :].astype(f32) for ref in (own, other)]
        total = (total[0][:half] + total[0][half:]) + (total[1][:half] + total[1][half:])
        high = total.astype(bf16)
        low = (total - high.astype(f32)).astype(bf16)
        for ref in blocks:
            ref[size : size + half, :] = high
            ref[size + half :, :] = low


def small_kernel(taps, heads, n_blocks, *refs):
    gdt_ref, cx_ref, ghead_ref, ggain_ref, shared_ref = refs[n_blocks:]
    total = tree_sum([b[...].astype(f32) for b in refs[:n_blocks]])
    wide_bc = cx_ref.shape[1] // 2
    n, size = taps + 1, gdt_ref.shape[0]
    half = (total.shape[0] - size) // 2
    small = total[size : size + half] + total[size + half :]
    gdt_ref[...] = total[0:size, wide_bc : wide_bc + heads]
    for j in range(2):
        cut = slice(j * wide_bc, (j + 1) * wide_bc)
        cx_ref[:, cut] = small[j * n : (j + 1) * n, 0:wide_bc]
        ggain_ref[:, cut] = small[3 * n + j : 3 * n + j + 1, 0:wide_bc]
    ghead_ref[...] = small[3 * n + 2 : 3 * n + 5, 0:heads]
    shared_ref[0:size, :] = total[0:size].astype(bf16)
    high = small[2 * n : 2 * n + 8].astype(bf16)
    shared_ref[size : size + 8, :] = high
    shared_ref[size + 8 :, :] = (small[2 * n : 2 * n + 8] - high.astype(f32)).astype(bf16)


def shared_kernel(gain_lane, n_blocks, *refs):
    gbc_ref, cbc_ref, ngain_ref = refs[n_blocks:]
    total = tree_sum([b[...].astype(f32) for b in refs[:n_blocks]])
    size, wide_bc = gbc_ref.shape
    gbc_ref[...] = total[0:size, 0:wide_bc]
    rows = total[size : size + 8, 0:wide_bc] + total[size + 8 :, 0:wide_bc]
    cbc_ref[...] = rows[0 : cbc_ref.shape[0]]
    ngain_ref[...] = row_of(total[0:size, wide_bc:][:, gain_lane : gain_lane + 1])


def input_kernel(pair, full_d, n_blocks, where, *refs):
    blocks = refs[:n_blocks]
    x_local, cot, inv, gain, out_ref, out = refs[n_blocks:]
    rows, _ = x_local.shape
    total = tree_sum([b[...].astype(f32) for b in blocks])
    dots = column_of((total[rows : rows + 1, :] + total[rows + 1 : rows + 2, :]) / full_d)[:, 0:1]
    scale = inv[:, 0:1]
    for p in range(gain.shape[1] // LANES):
        block, lane = unit(pair, p, where)

        @pl.when(block == 0)
        def _():
            cut = pl.ds(lane, LANES)
            xhat = x_local[:, cut].astype(f32) * scale
            out[:, cut] = gain[:, p * LANES : (p + 1) * LANES] + 0.0 * xhat

    gains = out[...]
    xhat = x_local[...].astype(f32) * scale
    grad = cot[...].astype(f32) + scale * (total[0:rows, :] * gains - xhat * dots)
    out_ref[...] = grad.astype(bf16)


VMEM = pl.BlockSpec(memory_space=pltpu.VMEM)
SMEM = pl.BlockSpec(memory_space=pltpu.SMEM)


def call(kernel, outs, inputs, scratch=(), scalars=0):
    return pl.pallas_call(
        kernel,
        out_shape=[jax.ShapeDtypeStruct(shape, kind) for shape, kind in outs],
        in_specs=[SMEM] * scalars + [VMEM] * (len(inputs) - scalars),
        out_specs=[VMEM] * len(outs),
        scratch_shapes=[pltpu.VMEM(shape, kind) for shape, kind in scratch],
    )(*inputs)


def local(
    hidden_in, cotangent, norm_gain, w_zx, w_bc, w_dt, w_out, conv_x, conv_bc, head_params, gate_gain
):
    rows, part_d = hidden_in.shape[2:]
    heads = head_params.shape[1]
    inner = conv_x.shape[1]
    wide_bc = w_bc.shape[1]
    taps = conv_x.shape[0] - 1
    shard = w_zx.shape[0]
    dp_n, seq_n, head_n = lax.axis_size("dp"), lax.axis_size("seq"), lax.axis_size("head")
    full_d = part_d * head_n
    full_inner = inner * head_n
    dp_i, seq_i, head_i = lax.axis_index("dp"), lax.axis_index("seq"), lax.axis_index("head")
    pair = seq_n == 2 and dp_n == head_n == 4 and shard == LANES and part_d == 2 * LANES
    state_n = wide_bc // 2

    where = jnp.stack([head_i ^ dp_i, seq_i] if pair else [head_i, seq_i]).astype(jnp.int32)

    def gathered(part, axis):
        if not pair:
            return [lax.all_gather(part, ("dp", "seq"), axis=axis, tiled=True)]
        own = exchanged(part, "dp")
        return own + [sent(p, "seq", 1) for p in own]

    def reduced(own, other, extra=0):
        recv = sent(other, "seq", 1)
        blocks = call(
            functools.partial(fold_kernel, dp_n),
            [((shard + extra, own.shape[1]), bf16)] * dp_n,
            [own, recv],
        )
        return scattered(blocks, "dp")

    def reduced_apart(own, other):
        both = jnp.concatenate([own[: full_d // 2], other[: full_d // 2]], axis=0).astype(f32)
        return lax.psum_scatter(both, ("dp", "seq"), scatter_dimension=0, tiled=True)

    x_local = hidden_in[0, 0]
    cot_local = cotangent[0, 0]
    pad = jnp.zeros((shard, LANES - heads - 1), bf16)
    packed = [w_zx.reshape(shard, 2 * inner), w_bc, w_dt, norm_gain[:, None], pad]
    pieces = gathered(jnp.concatenate(packed, axis=1), 0)
    x_blocks = exchanged(x_local, "head")
    out_pieces = gathered(w_out, 1)
    cot_blocks = exchanged(cot_local, "head")
    params = jnp.pad(head_params, ((0, 5), (0, LANES - heads)))
    gain_row = gate_gain[None]
    n_in, n_out = len(pieces), len(out_pieces)
    wide_bcd = wide_bc + LANES

    normed, x_perm, inv_in, norm_row, edge = call(
        functools.partial(norm_kernel, pair, heads, head_n, n_in),
        [
            ((rows, full_d), bf16),
            ((rows, full_d), bf16),
            ((rows, LANES), f32),
            ((1, full_d), f32),
            ((HALO, full_d), bf16),
        ],
        [where, *x_blocks, *pieces],
        [((head_n, rows, part_d), f32)],
        1,
    )
    edge = passed_along(edge, "seq", 1)
    z, x_ext, bc_ext, u_x, u_bc, dt, cum, y_loc, own_state, w_in = call(
        functools.partial(forward_kernel, heads, n_in),
        [
            ((rows, inner), bf16),
            ((HALO + rows, inner), bf16),
            ((HALO + rows, wide_bc), bf16),
            ((rows, inner), f32),
            ((rows, wide_bc), f32),
            ((rows, LANES), f32),
            ((rows, LANES), f32),
            ((rows, inner), f32),
            ((inner, state_n), f32),
            ((full_d, 2 * inner + wide_bcd), bf16),
        ],
        [normed, edge, conv_x, conv_bc, params, *pieces],
        [
            ((HALO + rows, full_d), bf16),
            ((HALO + rows, inner), f32),
            ((HALO + rows, wide_bc), f32),
        ],
    )
    total_decay = jnp.repeat(jnp.exp(cum[rows - 1, :heads]), inner // heads)[:, None]
    state_in = entering(total_decay, own_state, "seq", False)
    y, grad_o, gated_raw, stats, cot_perm, w_out_full = call(
        functools.partial(gate_kernel, pair, heads, head_n, n_out),
        [
            ((rows, inner), f32),
            ((rows, inner), f32),
            ((rows, inner), bf16),
            ((8, rows), f32),
            ((rows, full_d), bf16),
            ((inner, full_d), bf16),
        ],
        [where, state_in, u_bc, cum, y_loc, z, gain_row, *cot_blocks, *out_pieces],
        [((head_n, rows, part_d), f32)],
        1,
    )
    stats = exchanged(stats, "head")
    out_blocks = call(
        functools.partial(out_kernel, pair),
        [((rows, part_d), bf16)] * head_n,
        [where, gated_raw, w_out_full],
        [((head_n, rows, part_d), bf16)],
        1,
    )
    out_sum = f32_sum(scattered(out_blocks, "head"))

    dy, dz, from_cross, inv_gate, g_ggain = call(
        functools.partial(gate_back_kernel, heads, full_inner, head_n),
        [
            ((rows, inner), f32),
            ((rows, inner), bf16),
            ((inner, state_n), f32),
            ((rows, LANES), f32),
            ((1, inner), f32),
        ],
        [*stats, grad_o, y, z, gain_row, u_bc, cum],
    )
    output = (x_local.astype(f32) + out_sum * inv_gate[:, :1]).astype(bf16)
    grad_next = entering(total_decay, from_cross, "seq", True)
    dxs, dbc, dcum, early_own, early_other = call(
        functools.partial(inner_back_kernel, heads),
        [
            ((rows, inner), f32),
            ((rows, wide_bc), f32),
            ((rows, LANES), f32),
            ((full_d // 2, 2 * inner), bf16),
            ((full_d // 2, 2 * inner), bf16),
        ],
        [dy, dz, cum, dt, params, u_x, u_bc, state_in, gated_raw, cot_perm, inv_gate, normed],
    )
    gux, gubc, edge_out, raw16, g_head = call(
        functools.partial(ssd_back_kernel, heads),
        [
            ((rows, inner), f32),
            ((rows, wide_bc), f32),
            ((EDGE, inner + wide_bc), f32),
            ((rows, LANES), bf16),
            ((8, LANES), f32),
        ],
        [grad_next, dxs, dbc, dcum, dy, cum, dt, params, u_x, u_bc, state_in],
    )
    edge_next = passed_along(edge_out, "seq", -1)
    n = taps + 1
    count = 24
    results = call(
        functools.partial(last_kernel, pair, heads, head_n),
        [((rows + 16, part_d), bf16)] * head_n
        + [((full_d // 2, inner), bf16)] * 2
        + [((full_d // 2 + 2 * count, wide_bcd), bf16)] * 2,
        [
            where, edge_next, gux, gubc, x_ext, bc_ext, dz, raw16, normed, x_perm, inv_in, norm_row,
            conv_x, conv_bc, w_in, g_ggain, g_head,
        ],
        [
            ((head_n, rows, part_d), bf16),
            ((rows + EDGE, inner), f32),
            ((rows + EDGE, wide_bc), f32),
            ((HALO + rows, inner), f32),
            ((HALO + rows, wide_bc), f32),
            ((count, wide_bcd), f32),
        ],
        1,
    )
    blocks, (gx_own, gx_other, gb_own, gb_other) = results[:head_n], results[head_n:]
    if pair:
        early = f32_sum(reduced(early_own, early_other))
        g_bcd = reduced(gb_own, gb_other, 2 * count)
        g_x = f32_sum(reduced(gx_own, gx_other))
        g_dt, g_cx, g_head, g_ggain, shared = call(
            functools.partial(small_kernel, taps, heads, dp_n),
            [
                ((shard, heads), f32),
                ((n, inner), f32),
                ((3, heads), f32),
                ((1, inner), f32),
                ((shard + 16, wide_bcd), bf16),
            ],
            g_bcd,
        )
    else:
        early = reduced_apart(early_own, early_other)
        g_bcd = reduced_apart(gb_own, gb_other)
        g_x = reduced_apart(gx_own, gx_other)
        small = lax.psum(
            gb_own[full_d // 2 :][:count].astype(f32) + gb_own[full_d // 2 + count :].astype(f32),
            ("dp", "seq"),
        )
        g_dt = g_bcd[:, wide_bc : wide_bc + heads]
        g_cx = jnp.concatenate([small[:n, :wide_bc], small[n : 2 * n, :wide_bc]], axis=1)
        g_ggain = small[3 * n : 3 * n + 2, :wide_bc].reshape(1, inner)
        g_head = small[3 * n + 2 : 3 * n + 5, :heads]
        shared = jnp.concatenate([g_bcd, small[2 * n : 3 * n]], axis=0)
    parts = scattered(blocks, "head")
    (grad_input,) = call(
        functools.partial(input_kernel, pair, full_d, head_n),
        [((rows, part_d), bf16)],
        [where, *parts, x_local, cot_local, inv_in, norm_row],
        [((rows, part_d), f32)],
        1,
    )
    shared = exchanged(shared, "head")
    if pair:
        g_bc, g_cbc, g_ngain = call(
            functools.partial(shared_kernel, heads, head_n),
            [((shard, wide_bc), f32), ((n, wide_bc), f32), ((1, shard), f32)],
            shared,
        )
        g_ngain = g_ngain.reshape(shard)
    else:
        shared = tree_sum(shared)
        g_bc, g_cbc = shared[:shard, :wide_bc], shared[shard:, :wide_bc]
        g_ngain = shared[:shard, wide_bc + heads]
    g_zx = jnp.stack([early[:, :inner], g_x], axis=1)
    return (
        output[None, None],
        grad_input[None, None],
        g_ngain,
        g_zx,
        g_bc,
        g_dt,
        early[:, inner:].T,
        g_cx,
        g_cbc,
        g_head,
        g_ggain.reshape(inner),
    )


def solution(mesh):
    tokens = P(None, "dp", "seq", "head")
    zx = P(("dp", "seq"), None, "head")
    bc = P(("dp", "seq"), None)
    dt = P(("dp", "seq"), "head")
    out = P("head", ("dp", "seq"))
    gain, heads = P(("dp", "seq")), P(None, "head")

    return jax.shard_map(
        local,
        mesh=mesh,
        in_specs=(tokens, tokens, gain, zx, bc, dt, out, heads, P(), heads, P("head")),
        out_specs=(tokens, tokens, gain, zx, bc, dt, out, heads, P(), heads, P("head")),
        check_vma=False,
    )
```

```python
import functools

import jax
import jax.numpy as jnp
from jax import lax
from jax.experimental import pallas as pl
from jax.experimental.pallas import tpu as pltpu
from jax.sharding import PartitionSpec as P


epsilon = 1e-05
f32 = jnp.float32
bf16 = jnp.bfloat16
LANES = 128
HALO = 16
EDGE = 8


def xor_route(count, k):
    return [(i, i ^ k) for i in range(count)]


def sent(block, axis, k):
    return lax.ppermute(block, axis, xor_route(lax.axis_size(axis), k))


def exchanged(block, axis):
    count = lax.axis_size(axis)
    return [block] + [sent(block, axis, k) for k in range(1, count)]


def scattered(blocks, axis):
    count = lax.axis_size(axis)
    return [blocks[0]] + [sent(blocks[k], axis, k) for k in range(1, count)]


def tree_sum(parts):
    while len(parts) > 1:
        parts = [a + b for a, b in zip(parts[0::2], parts[1::2])]
    return parts[0]


def passed_along(block, axis, distance):
    devices = range(lax.axis_size(axis))
    route = [(i - distance, i) for i in devices if i - distance in devices]
    return lax.ppermute(block, axis, route)


def entering(decay, state, axis, reverse):
    count, place = lax.axis_size(axis), lax.axis_index(axis)
    if count == 2:
        return passed_along(state, axis, -1 if reverse else 1)
    decays, states = lax.all_gather(decay, axis), lax.all_gather(state, axis)

    def turn(k, before):
        at = count - 1 - k if reverse else k
        reached = at > place if reverse else at < place
        return jnp.where(reached, decays[at] * before + states[at], before)

    return lax.fori_loop(0, count, turn, jnp.zeros_like(state))


def dot(a, b, left, right):
    return lax.dot_general(
        a.astype(bf16), b.astype(bf16), (((left,), (right,)), ((), ())), preferred_element_type=f32
    )


def nn(a, b):
    return dot(a, b, 1, 0)


def nt(a, b):
    return dot(a, b, 1, 1)


def tn(a, b):
    return dot(a, b, 0, 0)


def sigmoid(v):
    return 1.0 / (1.0 + jnp.exp(-v))


def softplus(v):
    e = jnp.exp(-jnp.abs(v))
    small = e * (1.0 - e * (0.5 - e * (1.0 / 3.0 - e * 0.25)))
    return jnp.maximum(v, 0.0) + jnp.where(e < 0.03, small, jnp.log(1.0 + e))


def iota(shape, axis):
    return lax.broadcasted_iota(jnp.int32, shape, axis)


def row_of(column):
    return jnp.broadcast_to(column, (column.shape[0], LANES)).T[0:1]


def column_of(row):
    return jnp.broadcast_to(row, (LANES, row.shape[1])).T


def terms(values, count):
    parts = []
    for _ in range(count):
        parts.append(values.astype(bf16))
        values = values - parts[-1].astype(f32)
    return parts


def spread(values, heads, width):
    same = iota((LANES, heads * width), 1) // width == iota((LANES, heads * width), 0)
    same = same.astype(bf16)
    return sum(nn(part, same) for part in terms(values, 2))


def gathered_heads(values, heads, width):
    same = iota((heads * width, LANES), 0) // width == iota((heads * width, LANES), 1)
    same = same.astype(bf16)
    return sum(nn(part, same) for part in terms(values, 2))


def running(mask, values):
    mask = mask.astype(bf16)
    return sum(nn(mask, part) for part in terms(values, 3))


def unit(pair, p, where):
    if pair:
        t, k = divmod(p, 4)
        return k ^ where[0], pl.multiple_of((t ^ where[1]) * LANES, LANES)
    j, u = divmod(p, 2)
    return j ^ where[0], u * LANES


def assembled(scratch, pieces, axis):
    at = 0
    for piece in pieces:
        size = piece.shape[axis]
        if axis == 0:
            scratch[at : at + size, :] = piece[...]
        else:
            scratch[:, at : at + size] = piece[...]
        at += size


def pack_kernel(w_zx, w_bc, w_dt, gain, params, out, params_out):
    shard, inner = w_zx.shape[0], w_zx.shape[2]
    heads, wide_bc = w_dt.shape[0], w_bc.shape[1]
    both = w_zx[...].astype(f32)
    for j in range(2):
        out[:, j * inner : (j + 1) * inner] = both[:, j, :].astype(bf16)
    out[:, 2 * inner : 2 * inner + wide_bc] = w_bc[...]
    row = iota((LANES - heads, shard), 0)
    rest = jnp.where(row == 0, gain[...].astype(f32), 0.0)
    tile = jnp.concatenate([w_dt[...].astype(f32), rest], axis=0).T
    out[:, 2 * inner + wide_bc :] = tile.astype(bf16)
    params_out[...] = jnp.zeros(params_out.shape, f32)
    params_out[0:3, 0:heads] = params[...]


def norm_kernel(pair, n_blocks, where, *refs):
    blocks = refs[:n_blocks]
    x_perm, inv_ref, edge_ref, hold = refs[n_blocks:]
    rows, part = blocks[0].shape
    swap = n_blocks * part // LANES // 2 if pair else 0
    total = jnp.zeros((rows, 1), f32)
    for k, block in enumerate(blocks):
        value = block[...].astype(f32)
        hold[k] = value
        total += jnp.sum(value * value, axis=1, keepdims=True)
    inv = lax.rsqrt(total / (n_blocks * part) + epsilon)
    inv_ref[...] = jnp.broadcast_to(inv, inv_ref.shape)
    for p in range(n_blocks * part // LANES):
        block, lane = unit(pair, p, where)
        value = hold[block, :, pl.ds(lane, LANES)].astype(bf16)
        x_perm[:, p * LANES : (p + 1) * LANES] = value
        there = p ^ swap
        edge_ref[:, there * LANES : (there + 1) * LANES] = value[rows - HALO :, :]


def forward_kernel(heads, n_pieces, *refs):
    x_perm, inv, edge, conv_x, conv_bc, params = refs[:6]
    pieces = refs[6 : 6 + n_pieces]
    (z_ref, xe_ref, be_ref, ux_ref, ubc_ref, dt_ref, cum_ref, y_ref, state_ref, w_in) = refs[
        6 + n_pieces : 16 + n_pieces
    ]
    normed, gain_ref, rows_in, xe, be = refs[16 + n_pieces :]
    rows, inner = ux_ref.shape
    width = inner // heads
    state_n = ubc_ref.shape[1] // 2
    taps = conv_x.shape[0] - 1
    assembled(w_in, pieces, 0)
    tile = 2 * inner + 2 * state_n
    eye = iota((LANES, LANES), 0) == iota((LANES, LANES), 1)
    for p in range(w_in.shape[0] // LANES):
        cut = slice(p * LANES, (p + 1) * LANES)
        gain = w_in[cut, tile : tile + LANES][:, heads : heads + 1].astype(f32)
        gain_ref[:, cut] = jnp.sum(jnp.where(eye, gain, 0.0), axis=0, keepdims=True)
    gains = gain_ref[...]
    normed[...] = (x_perm[...].astype(f32) * inv[:, 0:1] * gains).astype(bf16)
    before = edge[...].astype(f32)
    before_inv = lax.rsqrt(
        jnp.sum(before * before, axis=1, keepdims=True) / before.shape[1] + epsilon
    )
    rows_in[0:HALO, :] = (before * before_inv * gains).astype(bf16)
    rows_in[HALO : HALO + rows, :] = normed[...]
    z_ref[...] = nn(normed[...], w_in[:, 0:inner]).astype(bf16)
    x_raw = nn(rows_in[...], w_in[:, inner : 2 * inner]).astype(bf16)
    xe_ref[...] = x_raw
    xe[...] = x_raw.astype(f32)
    bcd = nn(rows_in[...], w_in[:, 2 * inner :])
    bc_raw = bcd[:, 0 : 2 * state_n].astype(bf16)
    be_ref[...] = bc_raw
    be[...] = bc_raw.astype(f32)
    dt = bcd[HALO:, 2 * state_n :]
    dt_ref[...] = dt

    def conv(extended, weights):
        total = weights[taps : taps + 1, :]
        for k in range(taps):
            total = total + weights[k : k + 1, :] * extended[
                HALO - taps + 1 + k : HALO - taps + 1 + k + rows, :
            ]
        return total

    u_x = conv(xe, conv_x)
    ux_ref[...] = u_x
    u_bc = conv(be, conv_bc)
    ubc_ref[...] = u_bc
    x_act = u_x * sigmoid(u_x)
    bc_act = u_bc * sigmoid(u_bc)
    b_mat = bc_act[:, 0:state_n].astype(bf16)
    c_mat = bc_act[:, state_n:].astype(bf16)
    lane = iota((rows, LANES), 1)
    step = jnp.where(lane < heads, softplus(dt + params[0:1, :]), 0.0)
    lower = iota((rows, rows), 0) >= iota((rows, rows), 1)
    cum = running(lower, -step * jnp.exp(params[1:2, :]))
    cum_ref[...] = cum
    cum_t = cum.T
    gram = nt(c_mat, b_mat)
    scaled = x_act * spread(step, heads, width)
    scaled16 = scaled.astype(bf16)
    skip = spread(params[...], heads, width)[2:3, :]
    pair_lane = iota((rows, 2 * width), 1)
    for q in range(heads // 2):
        cut = slice(2 * width * q, 2 * width * (q + 1))
        both = []
        for h in (2 * q, 2 * q + 1):
            decay = jnp.exp(jnp.where(lower, cum[:, h : h + 1] - cum_t[h : h + 1, :], -jnp.inf))
            both.append(nn(decay * gram, scaled16[:, cut]))
        y_ref[:, cut] = (
            jnp.where(pair_lane < width, both[0], both[1]) + x_act[:, cut] * skip[:, cut]
        )
    to_end = jnp.exp(cum[rows - 1 : rows, :] - cum)
    state_ref[...] = tn(scaled * spread(to_end, heads, width), b_mat)


def cot_kernel(pair, n_blocks, n_pieces, where, *refs):
    normed = refs[0]
    blocks = refs[1 : 1 + n_blocks]
    pieces = refs[1 + n_blocks : 1 + n_blocks + n_pieces]
    go_ref, w_ref, normed_t, cot_t, hold, cot = refs[1 + n_blocks + n_pieces :]
    assembled(w_ref, pieces, 1)
    for k, block in enumerate(blocks):
        hold[k] = block[...].astype(f32)
    for p in range(cot.shape[1] // LANES):
        block, lane = unit(pair, p, where)
        cut = slice(p * LANES, (p + 1) * LANES)
        value = hold[block, :, pl.ds(lane, LANES)]
        cot[:, cut] = value.astype(bf16)
        cot_t[cut, :] = value.T.astype(bf16)
        normed_t[cut, :] = normed[:, cut].astype(f32).T.astype(bf16)
    go_ref[...] = nt(cot[...], w_ref[...])


def gate_kernel(heads, state, ubc, cum, y_loc, z, gain, go, y_ref, raw_ref, stats_ref):
    rows, inner = y_ref.shape
    width = inner // heads
    state_n = ubc.shape[1] // 2
    u_c = ubc[:, state_n:]
    c_mat = u_c * sigmoid(u_c)
    y = y_loc[...] + nt(c_mat, state[...]) * spread(jnp.exp(cum[...]), heads, width)
    y_ref[...] = y
    z_val = z[...].astype(f32)
    gated = y * z_val * sigmoid(z_val)
    raw = gated * gain[...]
    raw_ref[...] = raw.astype(bf16)
    squares = jnp.sum(gated * gated, axis=1, keepdims=True)
    cross = jnp.sum(go[...] * raw, axis=1, keepdims=True)
    lane = iota((rows, LANES), 1)
    both = jnp.where(lane == 0, squares, jnp.where(lane == 1, cross, 0.0))
    stats_ref[...] = both.T[0:8, :]


def out_kernel(pair, where, raw, weights, *refs):
    hold = refs[-1]
    part = nn(raw[...], weights[...]).astype(bf16)
    for p in range(weights.shape[1] // LANES):
        block, lane = unit(pair, p, where)
        hold[block, :, pl.ds(lane, LANES)] = part[:, p * LANES : (p + 1) * LANES]
    for k, ref in enumerate(refs[:-1]):
        ref[...] = hold[k]


def gate_back_kernel(heads, full_inner, n_stats, *refs):
    stats = refs[:n_stats]
    go, y, z, gain, ubc, cum = refs[n_stats : n_stats + 6]
    dy_ref, dz_ref, state_ref, inv_ref, ggain_ref, gated_ref = refs[n_stats + 6 :]
    rows, inner = y.shape
    width = inner // heads
    state_n = ubc.shape[1] // 2
    total = tree_sum([s[...] for s in stats])
    total = jnp.concatenate([total, jnp.zeros((LANES - total.shape[0], rows), f32)], axis=0).T
    inv = lax.rsqrt(total[:, 0:1] / full_inner + epsilon)
    coef = inv * inv * inv * (total[:, 1:2] / full_inner)
    inv_ref[...] = jnp.broadcast_to(inv, inv_ref.shape)
    z_val = z[...].astype(f32)
    sig = sigmoid(z_val)
    silu = z_val * sig
    y_val = y[...]
    gated = y_val * silu
    grad_o = go[...]
    unit_gated = gated * inv
    gated_ref[...] = (unit_gated * gain[...]).astype(bf16)
    ggain_ref[...] = jnp.sum(grad_o * unit_gated, axis=0, keepdims=True)
    grad_gin = inv * grad_o * gain[...] - gated * coef
    dy = grad_gin * silu
    dy_ref[...] = dy
    dz_ref[...] = (grad_gin * y_val * sig * (1.0 + z_val * (1.0 - sig))).astype(bf16)
    u_c = ubc[:, state_n:]
    c_mat = u_c * sigmoid(u_c)
    state_ref[...] = tn(dy * spread(jnp.exp(cum[...]), heads, width), c_mat)


def inner_back_kernel(
    heads, dy_ref, dz, cum_ref, dt, params, ux, ubc, state, gated, cot_t, normed_t,
    dxs_ref, dbc_ref, dcum_ref, own_ref, other_ref,
):
    rows, inner = dy_ref.shape
    width = inner // heads
    state_n = ubc.shape[1] // 2
    cum = cum_ref[...]
    cum_t = cum.T
    u_x, u_bc = ux[...], ubc[...]
    x_act = u_x * sigmoid(u_x)
    bc_act = u_bc * sigmoid(u_bc)
    b_mat = bc_act[:, 0:state_n].astype(bf16)
    c_mat = bc_act[:, state_n:].astype(bf16)
    lane = iota((rows, LANES), 1)
    step = jnp.where(lane < heads, softplus(dt[...] + params[0:1, :]), 0.0)
    scaled16 = (x_act * spread(step, heads, width)).astype(bf16)
    dy = dy_ref[...]
    dy16 = dy.astype(bf16)
    gram = nt(c_mat, b_mat)
    lower = iota((rows, rows), 0) >= iota((rows, rows), 1)
    pair_lane = iota((rows, 2 * width), 1)
    grad_gram = jnp.zeros((rows, rows), f32)
    dcum = jnp.zeros((rows, LANES), f32)
    sub = iota((LANES, rows), 0)
    dcum_t = jnp.zeros((LANES, rows), f32)
    for q in range(heads // 2):
        cut = slice(2 * width * q, 2 * width * (q + 1))
        both = []
        for h in (2 * q, 2 * q + 1):
            decay = jnp.exp(jnp.where(lower, cum[:, h : h + 1] - cum_t[h : h + 1, :], -jnp.inf))
            mix = decay * gram
            both.append(tn(mix, dy16[:, cut]))
            own = (pair_lane < width) == (h % 2 == 0)
            grad_mix = nt(jnp.where(own, dy[:, cut], 0.0), scaled16[:, cut])
            grad_gram = grad_gram + grad_mix * decay
            expo = grad_mix * mix
            dcum = jnp.where(lane == h, jnp.sum(expo, axis=1, keepdims=True), dcum)
            dcum_t = jnp.where(sub == h, jnp.sum(expo, axis=0, keepdims=True), dcum_t)
        dxs_ref[:, cut] = jnp.where(pair_lane < width, both[0], both[1])
    exp_cum = spread(jnp.exp(cum), heads, width)
    cross = nt(c_mat, state[...]) * exp_cum
    dcum_ref[...] = dcum - dcum_t.T + gathered_heads(dy * cross, heads, width)
    dbc_ref[:, 0:state_n] = tn(grad_gram, c_mat)
    dbc_ref[:, state_n:] = nn(dy * exp_cum, state[...]) + nn(grad_gram, b_mat)
    half = own_ref.shape[0]
    for ref, cut in ((own_ref, slice(0, half)), (other_ref, slice(half, 2 * half))):
        ref[:, 0:inner] = nn(normed_t[cut, :], dz[...]).astype(bf16)
        ref[:, inner:] = nn(cot_t[cut, :], gated[...]).astype(bf16)


def ssd_back_kernel(
    heads, next_ref, dxs, dbc, dcum_ref, dy_ref, cum_ref, dt, params, ux, ubc, state,
    gux_ref, gubc_ref, edge_ref, raw_ref, ghead_ref,
):
    rows, inner = dy_ref.shape
    width = inner // heads
    state_n = ubc.shape[1] // 2
    cum = cum_ref[...]
    u_x, u_bc = ux[...], ubc[...]
    sig_x, sig_bc = sigmoid(u_x), sigmoid(u_bc)
    x_act = u_x * sig_x
    bc_act = u_bc * sig_bc
    b_mat = bc_act[:, 0:state_n].astype(bf16)
    lane = iota((rows, LANES), 1)
    shifted = dt[...] + params[0:1, :]
    step = jnp.where(lane < heads, softplus(shifted), 0.0)
    rate = -jnp.exp(params[1:2, :])
    step_wide = spread(step, heads, width)
    scaled = x_act * step_wide
    dy = dy_ref[...]
    grad_next = next_ref[...]
    to_end = spread(jnp.exp(cum[rows - 1 : rows, :] - cum), heads, width)
    from_next = nt(b_mat, grad_next) * to_end
    grad_scaled = dxs[...] + from_next
    grad_b = dbc[:, 0:state_n] + nn(scaled * to_end, grad_next)
    end_term = gathered_heads(scaled * from_next, heads, width)
    held = jnp.sum(state[...] * grad_next, axis=1, keepdims=True)
    held = jnp.broadcast_to(held, (inner, LANES))
    head_of = iota((inner, LANES), 0) // width == iota((inner, LANES), 1)
    held = jnp.sum(jnp.where(head_of, held, 0.0), axis=0, keepdims=True)
    last = jnp.sum(end_term, axis=0, keepdims=True) + jnp.exp(cum[rows - 1 : rows, :]) * held
    upper = iota((rows, rows), 0) <= iota((rows, rows), 1)
    grad_log = last + running(upper, dcum_ref[...] - end_term)
    grad_step = gathered_heads(grad_scaled * x_act, heads, width) + grad_log * rate
    grad_raw = jnp.where(lane < heads, grad_step * sigmoid(shifted), 0.0)
    raw_ref[...] = grad_raw.astype(bf16)
    row = iota((8, LANES), 0)
    bias_grad = jnp.sum(grad_raw, axis=0, keepdims=True)
    rate_grad = jnp.sum(grad_log * step, axis=0, keepdims=True) * rate
    skip_rows = jnp.broadcast_to(jnp.sum(dy * x_act, axis=0, keepdims=True), (8, inner))
    skip_grad = gathered_heads(skip_rows, heads, width)[0:1, :]
    ghead_ref[...] = jnp.where(
        row == 0, bias_grad, jnp.where(row == 1, rate_grad, jnp.where(row == 2, skip_grad, 0.0))
    )
    skip = spread(params[...], heads, width)[2:3, :]
    gux = (grad_scaled * step_wide + dy * skip) * (sig_x * (1.0 + u_x * (1.0 - sig_x)))
    gux_ref[...] = gux
    slope = sig_bc * (1.0 + u_bc * (1.0 - sig_bc))
    gubc_ref[:, 0:state_n] = grad_b * slope[:, 0:state_n]
    gubc_ref[:, state_n:] = dbc[:, state_n:] * slope[:, state_n:]
    edge_ref[:, 0:inner] = gux_ref[0:EDGE, :]
    edge_ref[:, inner:] = gubc_ref[0:EDGE, :]


def last_kernel(pair, gain_lane, n_blocks, where, *refs):
    edge, gux, gubc, xe, be, dz, raw, normed_t, x_perm, inv, gain, conv_x, conv_bc, w_in = refs[:14]
    ggain, ghead = refs[14:16]
    blocks = refs[16 : 16 + n_blocks]
    gx_own, gx_other, gb_own, gb_other = refs[16 + n_blocks : 20 + n_blocks]
    hold, gx_ext, gb_ext, x_ext, b_ext, small, grads = refs[20 + n_blocks :]
    rows, inner = gux.shape
    wide_bc = gubc.shape[1]
    taps = conv_x.shape[0] - 1
    small[...] = jnp.zeros(small.shape, f32)

    def conv_back(grad, ext, raw_ref, raw_ext, weights, next_rows, firsts, width):
        value = grad[...]
        ext[0:rows, :] = value
        ext[rows : rows + EDGE, :] = next_rows
        raw_ext[...] = raw_ref[...].astype(f32)

        def kept(k, row):
            for j, first in enumerate(firsts):
                small[first + k : first + k + 1, 0:wide_bc] = row[:, j * wide_bc : (j + 1) * wide_bc]

        total = jnp.zeros((rows, width), f32)
        for k in range(taps):
            ahead = taps - 1 - k
            total = total + weights[k : k + 1, :] * ext[ahead : ahead + rows, :]
            back = HALO - taps + 1 + k
            kept(k, jnp.sum(raw_ext[back : back + rows, :] * value, axis=0, keepdims=True))
        kept(taps, jnp.sum(value, axis=0, keepdims=True))
        return total.astype(bf16)

    n = taps + 1
    dx = conv_back(gux, gx_ext, xe, x_ext, conv_x, edge[:, 0:inner], (0, n), inner)
    dbc = conv_back(gubc, gb_ext, be, b_ext, conv_bc, edge[:, inner:], (2 * n,), wide_bc)
    for j in range(2):
        small[3 * n + j : 3 * n + j + 1, 0:wide_bc] = ggain[:, j * wide_bc : (j + 1) * wide_bc]
    small[3 * n + 2 : 3 * n + 5, 0:LANES] = ghead[0:3, :]
    grads[:, 0:inner] = dz[...]
    grads[:, inner : 2 * inner] = dx
    grads[:, 2 * inner : 2 * inner + wide_bc] = dbc
    grads[:, 2 * inner + wide_bc :] = raw[...]
    part = nt(grads[...], w_in[...])
    for p in range(part.shape[1] // LANES):
        block, lane = unit(pair, p, where)
        hold[block, :, pl.ds(lane, LANES)] = part[:, p * LANES : (p + 1) * LANES].astype(bf16)
    along = part * (x_perm[...].astype(f32) * inv[:, 0:1])
    dots = row_of(jnp.sum(along * gain[...], axis=1, keepdims=True))
    high = dots.astype(bf16).astype(f32)
    extra = jnp.where(iota((16, rows), 0) == 0, high, dots - high)
    extra = jnp.where(iota((16, rows), 0) < 2, extra, 0.0).astype(bf16)
    for k, ref in enumerate(blocks):
        ref[0:rows, :] = hold[k]
        ref[rows : rows + 16, :] = extra
    half = gx_own.shape[0]
    at = iota((half, LANES), 1) == gain_lane
    high = small[...].astype(bf16)
    low = (small[...] - high.astype(f32)).astype(bf16)
    count = small.shape[0]
    gain_sum = jnp.sum(along, axis=0, keepdims=True)
    for first, gx_ref, gb_ref in ((0, gx_own, gb_own), (half, gx_other, gb_other)):
        cut = slice(first, first + half)
        g_both = nn(normed_t[cut, :], grads[:, inner:])
        gx_ref[...] = g_both[:, 0:inner].astype(bf16)
        g_bcd = g_both[:, inner:]
        g_gain = jnp.concatenate(
            [column_of(gain_sum[:, j : j + LANES]) for j in range(first, first + half, LANES)], axis=0
        )
        gb_ref[0:half, 0:wide_bc] = g_bcd[:, 0:wide_bc].astype(bf16)
        gb_ref[0:half, wide_bc:] = jnp.where(at, g_gain, g_bcd[:, wide_bc:]).astype(bf16)
        gb_ref[half : half + count, :] = high
        gb_ref[half + count :, :] = low


def fold_kernel(n_blocks, own, other, *blocks):
    size = (own.shape[0] - blocks[0].shape[0]) // (n_blocks - 1)
    extra = blocks[0].shape[0] - size
    for k, ref in enumerate(blocks):
        cut = slice(k * size, (k + 1) * size)
        ref[0:size, :] = (own[cut, :].astype(f32) + other[cut, :].astype(f32)).astype(bf16)
    if extra > 0:
        first, half = n_blocks * size, extra // 2
        total = [ref[first:, :].astype(f32) for ref in (own, other)]
        total = (total[0][:half] + total[0][half:]) + (total[1][:half] + total[1][half:])
        high = total.astype(bf16)
        low = (total - high.astype(f32)).astype(bf16)
        for ref in blocks:
            ref[size : size + half, :] = high
            ref[size + half :, :] = low


def small_kernel(taps, heads, n_blocks, *refs):
    gdt_ref, cx_ref, ghead_ref, ggain_ref, shared_ref = refs[n_blocks:]
    total = tree_sum([b[...].astype(f32) for b in refs[:n_blocks]])
    wide_bc = cx_ref.shape[1] // 2
    n, size = taps + 1, gdt_ref.shape[1]
    half = (total.shape[0] - size) // 2
    small = total[size : size + half] + total[size + half :]
    gdt_ref[...] = total[0:size, wide_bc:].T[0:heads, :]
    for j in range(2):
        cut = slice(j * wide_bc, (j + 1) * wide_bc)
        cx_ref[:, cut] = small[j * n : (j + 1) * n, 0:wide_bc]
        ggain_ref[:, cut] = small[3 * n + j : 3 * n + j + 1, 0:wide_bc]
    ghead_ref[...] = small[3 * n + 2 : 3 * n + 5, 0:heads]
    shared_ref[0:size, :] = total[0:size].astype(bf16)
    high = small[2 * n : 2 * n + 8].astype(bf16)
    shared_ref[size : size + 8, :] = high
    shared_ref[size + 8 :, :] = (small[2 * n : 2 * n + 8] - high.astype(f32)).astype(bf16)


def shared_kernel(gain_lane, n_blocks, *refs):
    gbc_ref, cbc_ref, ngain_ref = refs[n_blocks:]
    total = tree_sum([b[...].astype(f32) for b in refs[:n_blocks]])
    size, wide_bc = gbc_ref.shape
    gbc_ref[...] = total[0:size, 0:wide_bc]
    rows = total[size : size + 8, 0:wide_bc] + total[size + 8 :, 0:wide_bc]
    cbc_ref[...] = rows[0 : cbc_ref.shape[0]]
    ngain_ref[...] = row_of(total[0:size, wide_bc:][:, gain_lane : gain_lane + 1])


def input_kernel(pair, full_d, n_blocks, n_grads, where, *refs):
    blocks, outs = refs[:n_blocks], refs[n_blocks : 2 * n_blocks]
    early, late = (refs[(2 * n_blocks + j * n_grads) :][:n_grads] for j in range(2))
    rest = refs[2 * n_blocks + 2 * n_grads :]
    x_local, cot, inv, gain, inv_gate = rest[:5]
    gains = rest[-1]
    output_ref, grad_ref = rest[5:7]
    rows, _ = x_local.shape
    total = tree_sum([b[...].astype(f32) for b in outs])
    x_val = x_local[...].astype(f32)
    output_ref[...] = (x_val + total * inv_gate[:, 0:1]).astype(bf16)
    total = tree_sum([b[...].astype(f32) for b in blocks])
    dots = column_of((total[rows : rows + 1, :] + total[rows + 1 : rows + 2, :]) / full_d)[:, 0:1]
    scale = inv[:, 0:1]
    for p in range(gain.shape[1] // LANES):
        block, lane = unit(pair, p, where)

        @pl.when(block == 0)
        def _():
            gains[:, pl.ds(lane, LANES)] = jnp.broadcast_to(
                gain[:, p * LANES : (p + 1) * LANES], (8, LANES)
            )

    grad = scale * (total[0:rows, :] * gains[0:1, :] - x_val * (scale * dots))
    grad_ref[...] = (cot[...].astype(f32) + grad).astype(bf16)
    if n_grads > 0:
        gzx_ref, gout_ref = rest[7:9]
        inner = gzx_ref.shape[2]
        total = tree_sum([b[...].astype(f32) for b in early])
        gzx_ref[:, 0, :] = total[:, 0:inner]
        gzx_ref[:, 1, :] = tree_sum([b[...].astype(f32) for b in late])
        gout_ref[...] = total[:, inner:].T


VMEM = pl.BlockSpec(memory_space=pltpu.VMEM)
SMEM = pl.BlockSpec(memory_space=pltpu.SMEM)


def call(kernel, outs, inputs, scratch=(), scalars=0):
    return pl.pallas_call(
        kernel,
        out_shape=[jax.ShapeDtypeStruct(shape, kind) for shape, kind in outs],
        in_specs=[SMEM] * scalars + [VMEM] * (len(inputs) - scalars),
        out_specs=[VMEM] * len(outs),
        scratch_shapes=[pltpu.VMEM(shape, kind) for shape, kind in scratch],
    )(*inputs)


def local(
    hidden_in, cotangent, norm_gain, w_zx, w_bc, w_dt, w_out, conv_x, conv_bc, head_params, gate_gain
):
    rows, part_d = hidden_in.shape[2:]
    heads = head_params.shape[1]
    inner = conv_x.shape[1]
    wide_bc = w_bc.shape[1]
    taps = conv_x.shape[0] - 1
    shard = w_zx.shape[0]
    dp_n, seq_n, head_n = lax.axis_size("dp"), lax.axis_size("seq"), lax.axis_size("head")
    full_d = part_d * head_n
    full_inner = inner * head_n
    dp_i, seq_i, head_i = lax.axis_index("dp"), lax.axis_index("seq"), lax.axis_index("head")
    pair = seq_n == 2 and dp_n == head_n == 4 and shard == LANES and part_d == 2 * LANES
    state_n = wide_bc // 2

    where = jnp.stack([head_i ^ dp_i, seq_i] if pair else [head_i, seq_i]).astype(jnp.int32)

    def gathered(part, axis):
        if not pair:
            return [lax.all_gather(part, ("dp", "seq"), axis=axis, tiled=True)]
        own = exchanged(part, "dp")
        return own + [sent(p, "seq", 1) for p in own]

    def reduced(own, other, extra=0):
        recv = sent(other, "seq", 1)
        if extra == 0:
            both = (own.astype(f32) + recv.astype(f32)).astype(bf16)
            blocks = [both[k * shard : (k + 1) * shard] for k in range(dp_n)]
        else:
            blocks = call(
                functools.partial(fold_kernel, dp_n),
                [((shard + extra, own.shape[1]), bf16)] * dp_n,
                [own, recv],
            )
        return scattered(blocks, "dp")

    def reduced_apart(own, other):
        both = jnp.concatenate([own[: full_d // 2], other[: full_d // 2]], axis=0).astype(f32)
        return lax.psum_scatter(both, ("dp", "seq"), scatter_dimension=0, tiled=True)

    x_local = hidden_in[0, 0]
    cot_local = cotangent[0, 0]
    wide_bcd = wide_bc + LANES
    if pair:
        packed, params = call(
            pack_kernel,
            [((shard, 2 * inner + wide_bcd), bf16), ((8, LANES), f32)],
            [w_zx, w_bc, w_dt.T, norm_gain[None], head_params],
        )
    else:
        pad = jnp.zeros((shard, LANES - heads - 1), bf16)
        packed = [w_zx.reshape(shard, 2 * inner), w_bc, w_dt, norm_gain[:, None], pad]
        packed = jnp.concatenate(packed, axis=1)
        params = jnp.pad(head_params, ((0, 5), (0, LANES - heads)))
    pieces = gathered(packed, 0)
    x_blocks = exchanged(x_local, "head")
    out_pieces = gathered(w_out, 1)
    cot_blocks = exchanged(cot_local, "head")
    gain_row = gate_gain[None]
    n_in, n_out = len(pieces), len(out_pieces)

    x_perm, inv_in, edge = call(
        functools.partial(norm_kernel, pair, head_n),
        [((rows, full_d), bf16), ((rows, LANES), f32), ((HALO, full_d), bf16)],
        [where, *x_blocks],
        [((head_n, rows, part_d), f32)],
        1,
    )
    edge = passed_along(edge, "seq", 1)
    z, x_ext, bc_ext, u_x, u_bc, dt, cum, y_loc, own_state, w_in, normed, norm_row = call(
        functools.partial(forward_kernel, heads, n_in),
        [
            ((rows, inner), bf16),
            ((HALO + rows, inner), bf16),
            ((HALO + rows, wide_bc), bf16),
            ((rows, inner), f32),
            ((rows, wide_bc), f32),
            ((rows, LANES), f32),
            ((rows, LANES), f32),
            ((rows, inner), f32),
            ((inner, state_n), f32),
            ((full_d, 2 * inner + wide_bcd), bf16),
            ((rows, full_d), bf16),
            ((1, full_d), f32),
        ],
        [x_perm, inv_in, edge, conv_x, conv_bc, params, *pieces],
        [
            ((HALO + rows, full_d), bf16),
            ((HALO + rows, inner), f32),
            ((HALO + rows, wide_bc), f32),
        ],
    )
    total_decay = jnp.repeat(jnp.exp(cum[rows - 1, :heads]), inner // heads)[:, None]
    state_in = entering(total_decay, own_state, "seq", False)
    grad_o, w_out_full, normed_t, cot_t = call(
        functools.partial(cot_kernel, pair, head_n, n_out),
        [
            ((rows, inner), f32),
            ((inner, full_d), bf16),
            ((full_d, rows), bf16),
            ((full_d, rows), bf16),
        ],
        [where, normed, *cot_blocks, *out_pieces],
        [((head_n, rows, part_d), f32), ((rows, full_d), bf16)],
        1,
    )
    y, gated_raw, stats = call(
        functools.partial(gate_kernel, heads),
        [((rows, inner), f32), ((rows, inner), bf16), ((8, rows), f32)],
        [state_in, u_bc, cum, y_loc, z, gain_row, grad_o],
    )
    stats = exchanged(stats, "head")
    out_blocks = call(
        functools.partial(out_kernel, pair),
        [((rows, part_d), bf16)] * head_n,
        [where, gated_raw, w_out_full],
        [((head_n, rows, part_d), bf16)],
        1,
    )
    out_parts = scattered(out_blocks, "head")

    dy, dz, from_cross, inv_gate, g_ggain, gated = call(
        functools.partial(gate_back_kernel, heads, full_inner, head_n),
        [
            ((rows, inner), f32),
            ((rows, inner), bf16),
            ((inner, state_n), f32),
            ((rows, LANES), f32),
            ((1, inner), f32),
            ((rows, inner), bf16),
        ],
        [*stats, grad_o, y, z, gain_row, u_bc, cum],
    )
    grad_next = entering(total_decay, from_cross, "seq", True)
    dxs, dbc, dcum, early_own, early_other = call(
        functools.partial(inner_back_kernel, heads),
        [
            ((rows, inner), f32),
            ((rows, wide_bc), f32),
            ((rows, LANES), f32),
            ((full_d // 2, 2 * inner), bf16),
            ((full_d // 2, 2 * inner), bf16),
        ],
        [dy, dz, cum, dt, params, u_x, u_bc, state_in, gated, cot_t, normed_t],
    )
    gux, gubc, edge_out, raw16, g_head = call(
        functools.partial(ssd_back_kernel, heads),
        [
            ((rows, inner), f32),
            ((rows, wide_bc), f32),
            ((EDGE, inner + wide_bc), f32),
            ((rows, LANES), bf16),
            ((8, LANES), f32),
        ],
        [grad_next, dxs, dbc, dcum, dy, cum, dt, params, u_x, u_bc, state_in],
    )
    edge_next = passed_along(edge_out, "seq", -1)
    n = taps + 1
    count = 24
    results = call(
        functools.partial(last_kernel, pair, heads, head_n),
        [((rows + 16, part_d), bf16)] * head_n
        + [((full_d // 2, inner), bf16)] * 2
        + [((full_d // 2 + 2 * count, wide_bcd), bf16)] * 2,
        [
            where, edge_next, gux, gubc, x_ext, bc_ext, dz, raw16, normed_t, x_perm, inv_in, norm_row,
            conv_x, conv_bc, w_in, g_ggain, g_head,
        ],
        [
            ((head_n, rows, part_d), bf16),
            ((rows + EDGE, inner), f32),
            ((rows + EDGE, wide_bc), f32),
            ((HALO + rows, inner), f32),
            ((HALO + rows, wide_bc), f32),
            ((count, wide_bcd), f32),
            ((rows, 2 * inner + wide_bcd), bf16),
        ],
        1,
    )
    blocks, (gx_own, gx_other, gb_own, gb_other) = results[:head_n], results[head_n:]
    if pair:
        early = reduced(early_own, early_other)
        g_bcd = reduced(gb_own, gb_other, 2 * count)
        g_x = reduced(gx_own, gx_other)
        g_dt, g_cx, g_head, g_ggain, shared = call(
            functools.partial(small_kernel, taps, heads, dp_n),
            [
                ((heads, shard), f32),
                ((n, inner), f32),
                ((3, heads), f32),
                ((1, inner), f32),
                ((shard + 16, wide_bcd), bf16),
            ],
            g_bcd,
        )
        g_dt = g_dt.T
    else:
        early = reduced_apart(early_own, early_other)
        g_bcd = reduced_apart(gb_own, gb_other)
        g_x = reduced_apart(gx_own, gx_other)
        small = lax.psum(
            gb_own[full_d // 2 :][:count].astype(f32) + gb_own[full_d // 2 + count :].astype(f32),
            ("dp", "seq"),
        )
        g_dt = g_bcd[:, wide_bc : wide_bc + heads]
        g_cx = jnp.concatenate([small[:n, :wide_bc], small[n : 2 * n, :wide_bc]], axis=1)
        g_ggain = small[3 * n : 3 * n + 2, :wide_bc].reshape(1, inner)
        g_head = small[3 * n + 2 : 3 * n + 5, :heads]
        shared = jnp.concatenate([g_bcd, small[2 * n : 3 * n]], axis=0)
    parts = scattered(blocks, "head")
    grads = [((shard, 2, inner), f32), ((inner, shard), f32)] if pair else []
    output, grad_input, *grads = call(
        functools.partial(input_kernel, pair, full_d, head_n, dp_n if pair else 0),
        [((rows, part_d), bf16), ((rows, part_d), bf16), *grads],
        [
            where, *parts, *out_parts, *(early if pair else []), *(g_x if pair else []),
            x_local, cot_local, inv_in, norm_row, inv_gate,
        ],
        [((8, part_d), f32)],
        1,
    )
    shared = exchanged(shared, "head")
    if pair:
        g_bc, g_cbc, g_ngain = call(
            functools.partial(shared_kernel, heads, head_n),
            [((shard, wide_bc), f32), ((n, wide_bc), f32), ((1, shard), f32)],
            shared,
        )
        g_ngain = g_ngain.reshape(shard)
        g_zx, g_out = grads
    else:
        shared = tree_sum(shared)
        g_bc, g_cbc = shared[:shard, :wide_bc], shared[shard:, :wide_bc]
        g_ngain = shared[:shard, wide_bc + heads]
        g_zx = jnp.stack([early[:, :inner], g_x], axis=1)
        g_out = early[:, inner:].T
    return (
        output[None, None],
        grad_input[None, None],
        g_ngain,
        g_zx,
        g_bc,
        g_dt,
        g_out,
        g_cx,
        g_cbc,
        g_head,
        g_ggain.reshape(inner),
    )


def solution(mesh):
    tokens = P(None, "dp", "seq", "head")
    zx = P(("dp", "seq"), None, "head")
    bc = P(("dp", "seq"), None)
    dt = P(("dp", "seq"), "head")
    out = P("head", ("dp", "seq"))
    gain, heads = P(("dp", "seq")), P(None, "head")

    return jax.shard_map(
        local,
        mesh=mesh,
        in_specs=(tokens, tokens, gain, zx, bc, dt, out, heads, P(), heads, P("head")),
        out_specs=(tokens, tokens, gain, zx, bc, dt, out, heads, P(), heads, P("head")),
        check_vma=False,
    )
```

```python
import functools

import jax
import jax.numpy as jnp
from jax import lax
from jax.experimental import pallas as pl
from jax.experimental.pallas import tpu as pltpu
from jax.sharding import PartitionSpec as P


epsilon = 1e-05
f32 = jnp.float32
bf16 = jnp.bfloat16
LANES = 128
HALO = 16
EDGE = 8


def xor_route(count, k):
    return [(i, i ^ k) for i in range(count)]


def sent(block, axis, k):
    return lax.ppermute(block, axis, xor_route(lax.axis_size(axis), k))


def exchanged(block, axis):
    count = lax.axis_size(axis)
    return [block] + [sent(block, axis, k) for k in range(1, count)]


def scattered(blocks, axis):
    count = lax.axis_size(axis)
    return [blocks[0]] + [sent(blocks[k], axis, k) for k in range(1, count)]


def tree_sum(parts):
    while len(parts) > 1:
        parts = [a + b for a, b in zip(parts[0::2], parts[1::2])]
    return parts[0]


def passed_along(block, axis, distance):
    devices = range(lax.axis_size(axis))
    route = [(i - distance, i) for i in devices if i - distance in devices]
    return lax.ppermute(block, axis, route)


def entering(decay, state, axis, reverse):
    count, place = lax.axis_size(axis), lax.axis_index(axis)
    if count == 2:
        return passed_along(state, axis, -1 if reverse else 1)
    decays, states = lax.all_gather(decay, axis), lax.all_gather(state, axis)

    def turn(k, before):
        at = count - 1 - k if reverse else k
        reached = at > place if reverse else at < place
        return jnp.where(reached, decays[at] * before + states[at], before)

    return lax.fori_loop(0, count, turn, jnp.zeros_like(state))


def dot(a, b, left, right):
    return lax.dot_general(
        a.astype(bf16), b.astype(bf16), (((left,), (right,)), ((), ())), preferred_element_type=f32
    )


def nn(a, b):
    return dot(a, b, 1, 0)


def nt(a, b):
    return dot(a, b, 1, 1)


def tn(a, b):
    return dot(a, b, 0, 0)


def sigmoid(v):
    return 1.0 / (1.0 + jnp.exp(-v))


def softplus(v):
    e = jnp.exp(-jnp.abs(v))
    small = e * (1.0 - e * (0.5 - e * (1.0 / 3.0 - e * 0.25)))
    return jnp.maximum(v, 0.0) + jnp.where(e < 0.03, small, jnp.log(1.0 + e))


def iota(shape, axis):
    return lax.broadcasted_iota(jnp.int32, shape, axis)


def row_of(column):
    return jnp.broadcast_to(column, (column.shape[0], LANES)).T[0:1]


def column_of(row):
    return jnp.broadcast_to(row, (LANES, row.shape[1])).T


def terms(values, count):
    parts = []
    for _ in range(count):
        parts.append(values.astype(bf16))
        values = values - parts[-1].astype(f32)
    return parts


def spread(values, heads, width):
    same = iota((LANES, heads * width), 1) // width == iota((LANES, heads * width), 0)
    same = same.astype(bf16)
    return sum(nn(part, same) for part in terms(values, 2))


def gathered_heads(values, heads, width):
    same = iota((heads * width, LANES), 0) // width == iota((heads * width, LANES), 1)
    same = same.astype(bf16)
    return sum(nn(part, same) for part in terms(values, 2))


def running(mask, values):
    mask = mask.astype(bf16)
    return sum(nn(mask, part) for part in terms(values, 3))


def unit(pair, p, where):
    if pair:
        t, k = divmod(p, 4)
        return k ^ (where[0] >> 1), pl.multiple_of((t ^ (where[0] & 1)) * LANES, LANES)
    j, u = divmod(p, 2)
    return j ^ (where[0] >> 1), u * LANES


def assembled(scratch, pieces, axis):
    at = 0
    for piece in pieces:
        size = piece.shape[axis]
        if axis == 0:
            scratch[at : at + size, :] = piece[...]
        else:
            scratch[:, at : at + size] = piece[...]
        at += size


def pack_kernel(w_bc, w_dt, gain, params, out, params_out):
    shard, wide_bc = w_bc.shape
    heads = w_dt.shape[0]
    out[:, 0:wide_bc] = w_bc[...]
    row = iota((LANES - heads, shard), 0)
    rest = jnp.where(row == 0, gain[...].astype(f32), 0.0)
    tile = jnp.concatenate([w_dt[...].astype(f32), rest], axis=0).T
    out[:, wide_bc:] = tile.astype(bf16)
    params_out[...] = jnp.zeros(params_out.shape, f32)
    params_out[0:3, 0:heads] = params[...]


def forward_kernel(pair, heads, n_blocks, n_pieces, where, *refs):
    conv_x, conv_bc, params = refs[:3]
    blocks = refs[3 : 3 + n_blocks]
    zx_pieces = refs[3 + n_blocks : 3 + n_blocks + n_pieces]
    bcd_pieces = refs[3 + n_blocks + n_pieces : 3 + n_blocks + 2 * n_pieces]
    (
        z_ref, xe_ref, be_ref, ux_ref, ubc_ref, dt_ref, cum_ref, y_ref, state_ref, w_in, x_perm,
        inv_ref, normed, gain_ref, rows_in, xe, be, hold,
    ) = refs[3 + n_blocks + 2 * n_pieces :]
    rows, inner = ux_ref.shape
    width = inner // heads
    state_n = ubc_ref.shape[1] // 2
    taps = conv_x.shape[0] - 1
    assembled(w_in.at[:, 0 : 2 * inner], zx_pieces, 0)
    assembled(w_in.at[:, 2 * inner :], bcd_pieces, 0)
    total = jnp.zeros((HALO + rows, 1), f32)
    for k, block in enumerate(blocks):
        value = block[...].astype(f32)
        hold[k] = value
        total += jnp.sum(value * value, axis=1, keepdims=True)
    inv = lax.rsqrt(total / x_perm.shape[1] + epsilon)
    inv_ref[...] = jnp.broadcast_to(inv[HALO:], inv_ref.shape)
    tile = 2 * inner + 2 * state_n
    eye = iota((LANES, LANES), 0) == iota((LANES, LANES), 1)
    for p in range(w_in.shape[0] // LANES):
        cut = slice(p * LANES, (p + 1) * LANES)
        gain = w_in[cut, tile : tile + LANES][:, heads : heads + 1].astype(f32)
        gain = jnp.sum(jnp.where(eye, gain, 0.0), axis=0, keepdims=True)
        gain_ref[:, cut] = gain
        block, lane = unit(pair, p, where)
        value = hold[block, :, pl.ds(lane, LANES)]
        x_perm[:, cut] = value[HALO:].astype(bf16)
        rows_in[:, cut] = (value * inv * gain).astype(bf16)
    normed[...] = rows_in[HALO : HALO + rows, :]
    z_ref[...] = nn(normed[...], w_in[:, 0:inner]).astype(bf16)
    x_raw = nn(rows_in[...], w_in[:, inner : 2 * inner]).astype(bf16)
    xe_ref[...] = x_raw
    xe[...] = x_raw.astype(f32)
    bcd = nn(rows_in[...], w_in[:, 2 * inner :])
    bc_raw = bcd[:, 0 : 2 * state_n].astype(bf16)
    be_ref[...] = bc_raw
    be[...] = bc_raw.astype(f32)
    dt = bcd[HALO:, 2 * state_n :]
    dt_ref[...] = dt

    def conv(extended, weights):
        total = weights[taps : taps + 1, :]
        for k in range(taps):
            total = total + weights[k : k + 1, :] * extended[
                HALO - taps + 1 + k : HALO - taps + 1 + k + rows, :
            ]
        return total

    u_x = conv(xe, conv_x)
    ux_ref[...] = u_x
    u_bc = conv(be, conv_bc)
    ubc_ref[...] = u_bc
    x_act = u_x * sigmoid(u_x)
    bc_act = u_bc * sigmoid(u_bc)
    b_mat = bc_act[:, 0:state_n].astype(bf16)
    c_mat = bc_act[:, state_n:].astype(bf16)
    lane = iota((rows, LANES), 1)
    step = jnp.where(lane < heads, softplus(dt + params[0:1, :]), 0.0)
    lower = iota((rows, rows), 0) >= iota((rows, rows), 1)
    cum = running(lower, -step * jnp.exp(params[1:2, :]))
    cum_ref[...] = cum
    cum_t = cum.T
    gram = nt(c_mat, b_mat)
    scaled = x_act * spread(step, heads, width)
    scaled16 = scaled.astype(bf16)
    skip = spread(params[...], heads, width)[2:3, :]
    pair_lane = iota((rows, 2 * width), 1)
    for q in range(heads // 2):
        cut = slice(2 * width * q, 2 * width * (q + 1))
        both = []
        for h in (2 * q, 2 * q + 1):
            decay = jnp.exp(jnp.where(lower, cum[:, h : h + 1] - cum_t[h : h + 1, :], -jnp.inf))
            both.append(nn(decay * gram, scaled16[:, cut]))
        y_ref[:, cut] = (
            jnp.where(pair_lane < width, both[0], both[1]) + x_act[:, cut] * skip[:, cut]
        )
    to_end = jnp.exp(cum[rows - 1 : rows, :] - cum)
    state_ref[...] = tn(scaled * spread(to_end, heads, width), b_mat)


def gate_kernel(pair, heads, n_blocks, n_pieces, where, *refs):
    normed, state, ubc, cum, y_loc, z, gain = refs[:7]
    blocks = refs[7 : 7 + n_blocks]
    pieces = refs[7 + n_blocks : 7 + n_blocks + n_pieces]
    rest = refs[7 + n_blocks + n_pieces :]
    y_ref, go_ref, stats_ref, normed_t, cot_t = rest[:5]
    outs, (hold, cot, weights, out_hold) = rest[5 : 5 + n_blocks], rest[5 + n_blocks :]
    rows, inner = y_ref.shape
    width = inner // heads
    state_n = ubc.shape[1] // 2
    assembled(weights, pieces, 1)
    for k, block in enumerate(blocks):
        hold[k] = block[...].astype(f32)
    for p in range(cot.shape[1] // LANES):
        block, lane = unit(pair, p, where)
        cut = slice(p * LANES, (p + 1) * LANES)
        value = hold[block, :, pl.ds(lane, LANES)]
        cot[:, cut] = value.astype(bf16)
        cot_t[cut, :] = value.T.astype(bf16)
        normed_t[cut, :] = normed[:, cut].astype(f32).T.astype(bf16)
    grad_o = nt(cot[...], weights[...])
    go_ref[...] = grad_o
    u_c = ubc[:, state_n:]
    c_mat = u_c * sigmoid(u_c)
    y = y_loc[...] + nt(c_mat, state[...]) * spread(jnp.exp(cum[...]), heads, width)
    y_ref[...] = y
    z_val = z[...].astype(f32)
    gated = y * z_val * sigmoid(z_val)
    raw = gated * gain[...]
    squares = jnp.sum(gated * gated, axis=1, keepdims=True)
    cross = jnp.sum(grad_o * raw, axis=1, keepdims=True)
    lane = iota((rows, LANES), 1)
    both = jnp.where(lane == 0, squares, jnp.where(lane == 1, cross, 0.0))
    stats_ref[...] = both.T[0:8, :]
    part = nn(raw, weights[...]).astype(bf16)
    for p in range(weights.shape[1] // LANES):
        block, lane = unit(pair, p, where)
        out_hold[block, :, pl.ds(lane, LANES)] = part[:, p * LANES : (p + 1) * LANES]
    for k, ref in enumerate(outs):
        ref[...] = out_hold[k]


def gate_back_kernel(heads, full_inner, n_stats, *refs):
    stats = refs[:n_stats]
    go, y, z, gain, ubc, cum = refs[n_stats : n_stats + 6]
    dy_ref, dz_ref, state_ref, inv_ref, ggain_ref, gated_ref = refs[n_stats + 6 :]
    rows, inner = y.shape
    width = inner // heads
    state_n = ubc.shape[1] // 2
    total = tree_sum([s[...] for s in stats])
    total = jnp.concatenate([total, jnp.zeros((LANES - total.shape[0], rows), f32)], axis=0).T
    inv = lax.rsqrt(total[:, 0:1] / full_inner + epsilon)
    coef = inv * inv * inv * (total[:, 1:2] / full_inner)
    inv_ref[...] = jnp.broadcast_to(inv, inv_ref.shape)
    z_val = z[...].astype(f32)
    sig = sigmoid(z_val)
    silu = z_val * sig
    y_val = y[...]
    gated = y_val * silu
    grad_o = go[...]
    unit_gated = gated * inv
    gated_ref[...] = (unit_gated * gain[...]).astype(bf16)
    ggain_ref[...] = jnp.sum(grad_o * unit_gated, axis=0, keepdims=True)
    grad_gin = inv * grad_o * gain[...] - gated * coef
    dy = grad_gin * silu
    dy_ref[...] = dy
    dz_ref[...] = (grad_gin * y_val * sig * (1.0 + z_val * (1.0 - sig))).astype(bf16)
    u_c = ubc[:, state_n:]
    c_mat = u_c * sigmoid(u_c)
    state_ref[...] = tn(dy * spread(jnp.exp(cum[...]), heads, width), c_mat)


def inner_back_kernel(
    heads, dy_ref, dz, cum_ref, dt, params, ux, ubc, state, gated, cot_t, normed_t,
    dxs_ref, dbc_ref, dcum_ref, own_ref, other_ref,
):
    rows, inner = dy_ref.shape
    width = inner // heads
    state_n = ubc.shape[1] // 2
    cum = cum_ref[...]
    cum_t = cum.T
    u_x, u_bc = ux[...], ubc[...]
    x_act = u_x * sigmoid(u_x)
    bc_act = u_bc * sigmoid(u_bc)
    b_mat = bc_act[:, 0:state_n].astype(bf16)
    c_mat = bc_act[:, state_n:].astype(bf16)
    lane = iota((rows, LANES), 1)
    step = jnp.where(lane < heads, softplus(dt[...] + params[0:1, :]), 0.0)
    scaled16 = (x_act * spread(step, heads, width)).astype(bf16)
    dy = dy_ref[...]
    dy16 = dy.astype(bf16)
    gram = nt(c_mat, b_mat)
    lower = iota((rows, rows), 0) >= iota((rows, rows), 1)
    pair_lane = iota((rows, 2 * width), 1)
    grad_gram = jnp.zeros((rows, rows), f32)
    dcum = jnp.zeros((rows, LANES), f32)
    sub = iota((LANES, rows), 0)
    dcum_t = jnp.zeros((LANES, rows), f32)
    for q in range(heads // 2):
        cut = slice(2 * width * q, 2 * width * (q + 1))
        both = []
        for h in (2 * q, 2 * q + 1):
            decay = jnp.exp(jnp.where(lower, cum[:, h : h + 1] - cum_t[h : h + 1, :], -jnp.inf))
            mix = decay * gram
            both.append(tn(mix, dy16[:, cut]))
            own = (pair_lane < width) == (h % 2 == 0)
            grad_mix = nt(jnp.where(own, dy[:, cut], 0.0), scaled16[:, cut])
            grad_gram = grad_gram + grad_mix * decay
            expo = grad_mix * mix
            dcum = jnp.where(lane == h, jnp.sum(expo, axis=1, keepdims=True), dcum)
            dcum_t = jnp.where(sub == h, jnp.sum(expo, axis=0, keepdims=True), dcum_t)
        dxs_ref[:, cut] = jnp.where(pair_lane < width, both[0], both[1])
    exp_cum = spread(jnp.exp(cum), heads, width)
    cross = nt(c_mat, state[...]) * exp_cum
    dcum_ref[...] = dcum - dcum_t.T + gathered_heads(dy * cross, heads, width)
    dbc_ref[:, 0:state_n] = tn(grad_gram, c_mat)
    dbc_ref[:, state_n:] = nn(dy * exp_cum, state[...]) + nn(grad_gram, b_mat)
    half = own_ref.shape[0]
    for ref, cut in ((own_ref, slice(0, half)), (other_ref, slice(half, 2 * half))):
        ref[:, 0:inner] = nn(normed_t[cut, :], dz[...]).astype(bf16)
        ref[:, inner:] = nn(cot_t[cut, :], gated[...]).astype(bf16)


def ssd_back_kernel(
    heads, next_ref, dxs, dbc, dcum_ref, dy_ref, cum_ref, dt, params, ux, ubc, state,
    gux_ref, gubc_ref, edge_ref, raw_ref, ghead_ref,
):
    rows, inner = dy_ref.shape
    width = inner // heads
    state_n = ubc.shape[1] // 2
    cum = cum_ref[...]
    u_x, u_bc = ux[...], ubc[...]
    sig_x, sig_bc = sigmoid(u_x), sigmoid(u_bc)
    x_act = u_x * sig_x
    bc_act = u_bc * sig_bc
    b_mat = bc_act[:, 0:state_n].astype(bf16)
    lane = iota((rows, LANES), 1)
    shifted = dt[...] + params[0:1, :]
    step = jnp.where(lane < heads, softplus(shifted), 0.0)
    rate = -jnp.exp(params[1:2, :])
    step_wide = spread(step, heads, width)
    scaled = x_act * step_wide
    dy = dy_ref[...]
    grad_next = next_ref[...]
    to_end = spread(jnp.exp(cum[rows - 1 : rows, :] - cum), heads, width)
    from_next = nt(b_mat, grad_next) * to_end
    grad_scaled = dxs[...] + from_next
    grad_b = dbc[:, 0:state_n] + nn(scaled * to_end, grad_next)
    end_term = gathered_heads(scaled * from_next, heads, width)
    held = jnp.sum(state[...] * grad_next, axis=1, keepdims=True)
    held = jnp.broadcast_to(held, (inner, LANES))
    head_of = iota((inner, LANES), 0) // width == iota((inner, LANES), 1)
    held = jnp.sum(jnp.where(head_of, held, 0.0), axis=0, keepdims=True)
    last = jnp.sum(end_term, axis=0, keepdims=True) + jnp.exp(cum[rows - 1 : rows, :]) * held
    upper = iota((rows, rows), 0) <= iota((rows, rows), 1)
    grad_log = last + running(upper, dcum_ref[...] - end_term)
    grad_step = gathered_heads(grad_scaled * x_act, heads, width) + grad_log * rate
    grad_raw = jnp.where(lane < heads, grad_step * sigmoid(shifted), 0.0)
    raw_ref[...] = grad_raw.astype(bf16)
    row = iota((8, LANES), 0)
    bias_grad = jnp.sum(grad_raw, axis=0, keepdims=True)
    rate_grad = jnp.sum(grad_log * step, axis=0, keepdims=True) * rate
    skip_rows = jnp.broadcast_to(jnp.sum(dy * x_act, axis=0, keepdims=True), (8, inner))
    skip_grad = gathered_heads(skip_rows, heads, width)[0:1, :]
    ghead_ref[...] = jnp.where(
        row == 0, bias_grad, jnp.where(row == 1, rate_grad, jnp.where(row == 2, skip_grad, 0.0))
    )
    skip = spread(params[...], heads, width)[2:3, :]
    gux = (grad_scaled * step_wide + dy * skip) * (sig_x * (1.0 + u_x * (1.0 - sig_x)))
    gux_ref[...] = gux
    slope = sig_bc * (1.0 + u_bc * (1.0 - sig_bc))
    gubc_ref[:, 0:state_n] = grad_b * slope[:, 0:state_n]
    gubc_ref[:, state_n:] = dbc[:, state_n:] * slope[:, state_n:]
    edge_ref[:, 0:inner] = gux_ref[0:EDGE, :]
    edge_ref[:, inner:] = gubc_ref[0:EDGE, :]


def last_kernel(pair, gain_lane, n_blocks, where, *refs):
    edge, gux, gubc, xe, be, dz, raw, normed_t, x_perm, inv, gain, conv_x, conv_bc, w_in = refs[:14]
    ggain, ghead = refs[14:16]
    blocks = refs[16 : 16 + n_blocks]
    gx_own, gx_other, gb_own, gb_other = refs[16 + n_blocks : 20 + n_blocks]
    hold, gx_ext, gb_ext, x_ext, b_ext, small, grads = refs[20 + n_blocks :]
    rows, inner = gux.shape
    wide_bc = gubc.shape[1]
    taps = conv_x.shape[0] - 1
    small[...] = jnp.zeros(small.shape, f32)

    def conv_back(grad, ext, raw_ref, raw_ext, weights, next_rows, firsts, width):
        value = grad[...]
        ext[0:rows, :] = value
        ext[rows : rows + EDGE, :] = next_rows
        raw_ext[...] = raw_ref[...].astype(f32)

        def kept(k, row):
            for j, first in enumerate(firsts):
                small[first + k : first + k + 1, 0:wide_bc] = row[:, j * wide_bc : (j + 1) * wide_bc]

        total = jnp.zeros((rows, width), f32)
        for k in range(taps):
            ahead = taps - 1 - k
            total = total + weights[k : k + 1, :] * ext[ahead : ahead + rows, :]
            back = HALO - taps + 1 + k
            kept(k, jnp.sum(raw_ext[back : back + rows, :] * value, axis=0, keepdims=True))
        kept(taps, jnp.sum(value, axis=0, keepdims=True))
        return total.astype(bf16)

    n = taps + 1
    dx = conv_back(gux, gx_ext, xe, x_ext, conv_x, edge[:, 0:inner], (0, n), inner)
    dbc = conv_back(gubc, gb_ext, be, b_ext, conv_bc, edge[:, inner:], (2 * n,), wide_bc)
    for j in range(2):
        small[3 * n + j : 3 * n + j + 1, 0:wide_bc] = ggain[:, j * wide_bc : (j + 1) * wide_bc]
    small[3 * n + 2 : 3 * n + 5, 0:LANES] = ghead[0:3, :]
    grads[:, 0:inner] = dz[...]
    grads[:, inner : 2 * inner] = dx
    grads[:, 2 * inner : 2 * inner + wide_bc] = dbc
    grads[:, 2 * inner + wide_bc :] = raw[...]
    part = nt(grads[...], w_in[...])
    for p in range(part.shape[1] // LANES):
        block, lane = unit(pair, p, where)
        hold[block, :, pl.ds(lane, LANES)] = part[:, p * LANES : (p + 1) * LANES].astype(bf16)
    along = part * (x_perm[...].astype(f32) * inv[:, 0:1])
    dots = row_of(jnp.sum(along * gain[...], axis=1, keepdims=True))
    high = dots.astype(bf16).astype(f32)
    extra = jnp.where(iota((16, rows), 0) == 0, high, dots - high)
    extra = jnp.where(iota((16, rows), 0) < 2, extra, 0.0).astype(bf16)
    for k, ref in enumerate(blocks):
        ref[0:rows, :] = hold[k]
        ref[rows : rows + 16, :] = extra
    half = gx_own.shape[0]
    at = iota((half, LANES), 1) == gain_lane
    high = small[...].astype(bf16)
    low = (small[...] - high.astype(f32)).astype(bf16)
    count = small.shape[0]
    gain_sum = jnp.sum(along, axis=0, keepdims=True)
    for first, gx_ref, gb_ref in ((0, gx_own, gb_own), (half, gx_other, gb_other)):
        cut = slice(first, first + half)
        g_both = nn(normed_t[cut, :], grads[:, inner:])
        gx_ref[...] = g_both[:, 0:inner].astype(bf16)
        g_bcd = g_both[:, inner:]
        g_gain = jnp.concatenate(
            [column_of(gain_sum[:, j : j + LANES]) for j in range(first, first + half, LANES)], axis=0
        )
        gb_ref[0:half, 0:wide_bc] = g_bcd[:, 0:wide_bc].astype(bf16)
        gb_ref[0:half, wide_bc:] = jnp.where(at, g_gain, g_bcd[:, wide_bc:]).astype(bf16)
        gb_ref[half : half + count, :] = high
        gb_ref[half + count :, :] = low


def fold_kernel(n_blocks, own, other, x_own, x_other, *refs):
    blocks, x_blocks = refs[:n_blocks], refs[n_blocks:]
    size = x_blocks[0].shape[0]
    first, half = n_blocks * size, (blocks[0].shape[0] - size) // 2
    total = [ref[first:, :].astype(f32) for ref in (own, other)]
    total = (total[0][:half] + total[0][half:]) + (total[1][:half] + total[1][half:])
    high, low = terms(total, 2)
    for k in range(n_blocks):
        cut = slice(k * size, (k + 1) * size)
        blocks[k][0:size, :] = (own[cut, :].astype(f32) + other[cut, :].astype(f32)).astype(bf16)
        blocks[k][size : size + half, :] = high
        blocks[k][size + half :, :] = low
        x_blocks[k][...] = (x_own[cut, :].astype(f32) + x_other[cut, :].astype(f32)).astype(bf16)


def small_kernel(taps, heads, n_blocks, *refs):
    gdt_ref, cx_ref, ghead_ref, ggain_ref, shared_ref = refs[n_blocks:]
    total = tree_sum([b[...].astype(f32) for b in refs[:n_blocks]])
    wide_bc = cx_ref.shape[1] // 2
    n, size = taps + 1, gdt_ref.shape[1]
    half = (total.shape[0] - size) // 2
    small = total[size : size + half] + total[size + half :]
    gdt_ref[...] = total[0:size, wide_bc:].T[0:heads, :]
    for j in range(2):
        cut = slice(j * wide_bc, (j + 1) * wide_bc)
        cx_ref[:, cut] = small[j * n : (j + 1) * n, 0:wide_bc]
        ggain_ref[:, cut] = small[3 * n + j : 3 * n + j + 1, 0:wide_bc]
    ghead_ref[...] = small[3 * n + 2 : 3 * n + 5, 0:heads]
    shared_ref[0:size, :] = total[0:size, 0:wide_bc].astype(bf16)
    tail = jnp.concatenate([small[2 * n : 2 * n + 7, 0:wide_bc], jnp.zeros((1, wide_bc), f32)], axis=0)
    gain = row_of(total[0:size, wide_bc:][:, heads : heads + 1])
    gain = jnp.concatenate([gain, jnp.zeros((1, wide_bc - size), f32)], axis=1)
    tail = jnp.where(iota((8, wide_bc), 0) == 7, gain, tail)
    high, low = terms(tail, 2)
    shared_ref[size : size + 8, :] = high
    shared_ref[size + 8 :, :] = low


def shared_kernel(n_blocks, *refs):
    gbc_ref, cbc_ref, ngain_ref = refs[n_blocks:]
    total = tree_sum([b[...].astype(f32) for b in refs[:n_blocks]])
    size = gbc_ref.shape[0]
    gbc_ref[...] = total[0:size]
    rows = total[size : size + 8] + total[size + 8 :]
    cbc_ref[...] = rows[0 : cbc_ref.shape[0]]
    ngain_ref[...] = rows[7:8, 0 : ngain_ref.shape[1]]


def input_kernel(pair, full_d, n_blocks, n_grads, where, *refs):
    blocks, outs = refs[:n_blocks], refs[n_blocks : 2 * n_blocks]
    early, late = (refs[(2 * n_blocks + j * n_grads) :][:n_grads] for j in range(2))
    rest = refs[2 * n_blocks + 2 * n_grads :]
    x_local, cot, inv, gain, inv_gate = rest[:5]
    gains = rest[-1]
    output_ref, grad_ref = rest[5:7]
    rows, _ = x_local.shape
    total = tree_sum([b[...].astype(f32) for b in outs])
    x_val = x_local[...].astype(f32)
    output_ref[...] = (x_val + total * inv_gate[:, 0:1]).astype(bf16)
    total = tree_sum([b[...].astype(f32) for b in blocks])
    dots = column_of((total[rows : rows + 1, :] + total[rows + 1 : rows + 2, :]) / full_d)[:, 0:1]
    scale = inv[:, 0:1]
    for p in range(gain.shape[1] // LANES):
        block, lane = unit(pair, p, where)

        @pl.when(block == 0)
        def _():
            gains[:, pl.ds(lane, LANES)] = jnp.broadcast_to(
                gain[:, p * LANES : (p + 1) * LANES], (8, LANES)
            )

    grad = scale * (total[0:rows, :] * gains[0:1, :] - x_val * (scale * dots))
    grad_ref[...] = (cot[...].astype(f32) + grad).astype(bf16)
    if n_grads > 0:
        gzx_ref, gout_ref = rest[7:9]
        inner = gzx_ref.shape[2]
        total = tree_sum([b[...].astype(f32) for b in early])
        gzx_ref[:, 0, :] = total[:, 0:inner]
        gzx_ref[:, 1, :] = tree_sum([b[...].astype(f32) for b in late])
        gout_ref[...] = total[:, inner:].T


VMEM = pl.BlockSpec(memory_space=pltpu.VMEM)
SMEM = pl.BlockSpec(memory_space=pltpu.SMEM)


def call(kernel, outs, inputs, scratch=(), scalars=0):
    return pl.pallas_call(
        kernel,
        out_shape=[jax.ShapeDtypeStruct(shape, kind) for shape, kind in outs],
        in_specs=[SMEM] * scalars + [VMEM] * (len(inputs) - scalars),
        out_specs=[VMEM] * len(outs),
        scratch_shapes=[pltpu.VMEM(shape, kind) for shape, kind in scratch],
    )(*inputs)


def local(
    hidden_in, cotangent, norm_gain, w_zx, w_bc, w_dt, w_out, conv_x, conv_bc, head_params, gate_gain
):
    rows, part_d = hidden_in.shape[2:]
    heads = head_params.shape[1]
    inner = conv_x.shape[1]
    wide_bc = w_bc.shape[1]
    taps = conv_x.shape[0] - 1
    shard = w_zx.shape[0]
    dp_n, seq_n, head_n = lax.axis_size("dp"), lax.axis_size("seq"), lax.axis_size("head")
    full_d = part_d * head_n
    full_inner = inner * head_n
    dp_i, seq_i, head_i = lax.axis_index("dp"), lax.axis_index("seq"), lax.axis_index("head")
    pair = seq_n == 2 and dp_n == head_n == 4 and shard == LANES and part_d == 2 * LANES
    state_n = wide_bc // 2

    where = ((head_i ^ dp_i) * 2 + seq_i if pair else head_i * 2).astype(jnp.int32).reshape(1)

    def gathered(part, axis):
        if not pair:
            return [lax.all_gather(part, ("dp", "seq"), axis=axis, tiled=True)]
        own = exchanged(part, "dp")
        return own + [sent(p, "seq", 1) for p in own]

    def reduced(own, other):
        recv = sent(other, "seq", 1)
        both = (own.astype(f32) + recv.astype(f32)).astype(bf16)
        blocks = [both[k * shard : (k + 1) * shard] for k in range(dp_n)]
        return scattered(blocks, "dp")

    def reduced_apart(own, other):
        both = jnp.concatenate([own[: full_d // 2], other[: full_d // 2]], axis=0).astype(f32)
        return lax.psum_scatter(both, ("dp", "seq"), scatter_dimension=0, tiled=True)

    x_local = hidden_in[0, 0]
    cot_local = cotangent[0, 0]
    wide_bcd = wide_bc + LANES
    x_halo = passed_along(x_local, "seq", 1)[rows - HALO :]
    zx_pieces = gathered(w_zx.reshape(shard, 2 * inner), 0)
    x_blocks = exchanged(jnp.concatenate([x_halo, x_local], axis=0), "head")
    if pair:
        packed, params = call(
            pack_kernel,
            [((shard, wide_bcd), bf16), ((8, LANES), f32)],
            [w_bc, w_dt.T, norm_gain[None], head_params],
        )
    else:
        pad = jnp.zeros((shard, LANES - heads - 1), bf16)
        packed = jnp.concatenate([w_bc, w_dt, norm_gain[:, None], pad], axis=1)
        params = jnp.pad(head_params, ((0, 5), (0, LANES - heads)))
    bcd_pieces = gathered(packed, 0)
    out_pieces = gathered(w_out, 1)
    cot_blocks = exchanged(cot_local, "head")
    gain_row = gate_gain[None]
    n_in, n_out = len(zx_pieces), len(out_pieces)

    (
        z, x_ext, bc_ext, u_x, u_bc, dt, cum, y_loc, own_state, w_in, x_perm, inv_in, normed, norm_row,
    ) = call(
        functools.partial(forward_kernel, pair, heads, head_n, n_in),
        [
            ((rows, inner), bf16),
            ((HALO + rows, inner), bf16),
            ((HALO + rows, wide_bc), bf16),
            ((rows, inner), f32),
            ((rows, wide_bc), f32),
            ((rows, LANES), f32),
            ((rows, LANES), f32),
            ((rows, inner), f32),
            ((inner, state_n), f32),
            ((full_d, 2 * inner + wide_bcd), bf16),
            ((rows, full_d), bf16),
            ((rows, LANES), f32),
            ((rows, full_d), bf16),
            ((1, full_d), f32),
        ],
        [where, conv_x, conv_bc, params, *x_blocks, *zx_pieces, *bcd_pieces],
        [
            ((HALO + rows, full_d), bf16),
            ((HALO + rows, inner), f32),
            ((HALO + rows, wide_bc), f32),
            ((head_n, HALO + rows, part_d), f32),
        ],
        1,
    )
    total_decay = jnp.repeat(jnp.exp(cum[rows - 1, :heads]), inner // heads)[:, None]
    state_in = entering(total_decay, own_state, "seq", False)
    y, grad_o, stats, normed_t, cot_t, *out_blocks = call(
        functools.partial(gate_kernel, pair, heads, head_n, n_out),
        [
            ((rows, inner), f32),
            ((rows, inner), f32),
            ((8, rows), f32),
            ((full_d, rows), bf16),
            ((full_d, rows), bf16),
        ]
        + [((rows, part_d), bf16)] * head_n,
        [where, normed, state_in, u_bc, cum, y_loc, z, gain_row, *cot_blocks, *out_pieces],
        [
            ((head_n, rows, part_d), f32),
            ((rows, full_d), bf16),
            ((inner, full_d), bf16),
            ((head_n, rows, part_d), bf16),
        ],
        1,
    )
    stats = exchanged(stats, "head")
    out_parts = scattered(out_blocks, "head")

    dy, dz, from_cross, inv_gate, g_ggain, gated = call(
        functools.partial(gate_back_kernel, heads, full_inner, head_n),
        [
            ((rows, inner), f32),
            ((rows, inner), bf16),
            ((inner, state_n), f32),
            ((rows, LANES), f32),
            ((1, inner), f32),
            ((rows, inner), bf16),
        ],
        [*stats, grad_o, y, z, gain_row, u_bc, cum],
    )
    grad_next = entering(total_decay, from_cross, "seq", True)
    dxs, dbc, dcum, early_own, early_other = call(
        functools.partial(inner_back_kernel, heads),
        [
            ((rows, inner), f32),
            ((rows, wide_bc), f32),
            ((rows, LANES), f32),
            ((full_d // 2, 2 * inner), bf16),
            ((full_d // 2, 2 * inner), bf16),
        ],
        [dy, dz, cum, dt, params, u_x, u_bc, state_in, gated, cot_t, normed_t],
    )
    gux, gubc, edge_out, raw16, g_head = call(
        functools.partial(ssd_back_kernel, heads),
        [
            ((rows, inner), f32),
            ((rows, wide_bc), f32),
            ((EDGE, inner + wide_bc), f32),
            ((rows, LANES), bf16),
            ((8, LANES), f32),
        ],
        [grad_next, dxs, dbc, dcum, dy, cum, dt, params, u_x, u_bc, state_in],
    )
    edge_next = passed_along(edge_out, "seq", -1)
    n = taps + 1
    count = 24
    results = call(
        functools.partial(last_kernel, pair, heads, head_n),
        [((rows + 16, part_d), bf16)] * head_n
        + [((full_d // 2, inner), bf16)] * 2
        + [((full_d // 2 + 2 * count, wide_bcd), bf16)] * 2,
        [
            where, edge_next, gux, gubc, x_ext, bc_ext, dz, raw16, normed_t, x_perm, inv_in, norm_row,
            conv_x, conv_bc, w_in, g_ggain, g_head,
        ],
        [
            ((head_n, rows, part_d), bf16),
            ((rows + EDGE, inner), f32),
            ((rows + EDGE, wide_bc), f32),
            ((HALO + rows, inner), f32),
            ((HALO + rows, wide_bc), f32),
            ((count, wide_bcd), f32),
            ((rows, 2 * inner + wide_bcd), bf16),
        ],
        1,
    )
    blocks, (gx_own, gx_other, gb_own, gb_other) = results[:head_n], results[head_n:]
    if pair:
        early = reduced(early_own, early_other)
        gb_recv = sent(gb_other, "seq", 1)
        gx_recv = sent(gx_other, "seq", 1)
        folded = call(
            functools.partial(fold_kernel, dp_n),
            [((shard + 2 * count, wide_bcd), bf16)] * dp_n + [((shard, inner), bf16)] * dp_n,
            [gb_own, gb_recv, gx_own, gx_recv],
        )
        g_bcd = scattered(folded[:dp_n], "dp")
        g_x = scattered(folded[dp_n:], "dp")
        g_dt, g_cx, g_head, g_ggain, shared = call(
            functools.partial(small_kernel, taps, heads, dp_n),
            [
                ((heads, shard), f32),
                ((n, inner), f32),
                ((3, heads), f32),
                ((1, inner), f32),
                ((shard + 16, wide_bc), bf16),
            ],
            g_bcd,
        )
        g_dt = g_dt.T
    else:
        early = reduced_apart(early_own, early_other)
        g_bcd = reduced_apart(gb_own, gb_other)
        g_x = reduced_apart(gx_own, gx_other)
        small = lax.psum(
            gb_own[full_d // 2 :][:count].astype(f32) + gb_own[full_d // 2 + count :].astype(f32),
            ("dp", "seq"),
        )
        g_dt = g_bcd[:, wide_bc : wide_bc + heads]
        g_cx = jnp.concatenate([small[:n, :wide_bc], small[n : 2 * n, :wide_bc]], axis=1)
        g_ggain = small[3 * n : 3 * n + 2, :wide_bc].reshape(1, inner)
        g_head = small[3 * n + 2 : 3 * n + 5, :heads]
        shared = jnp.concatenate([g_bcd, small[2 * n : 3 * n]], axis=0)
    parts = scattered(blocks, "head")
    grads = [((shard, 2, inner), f32), ((inner, shard), f32)] if pair else []
    output, grad_input, *grads = call(
        functools.partial(input_kernel, pair, full_d, head_n, dp_n if pair else 0),
        [((rows, part_d), bf16), ((rows, part_d), bf16), *grads],
        [
            where, *parts, *out_parts, *(early if pair else []), *(g_x if pair else []),
            x_local, cot_local, inv_in, norm_row, inv_gate,
        ],
        [((8, part_d), f32)],
        1,
    )
    shared = exchanged(shared, "head")
    if pair:
        g_bc, g_cbc, g_ngain = call(
            functools.partial(shared_kernel, head_n),
            [((shard, wide_bc), f32), ((n, wide_bc), f32), ((1, shard), f32)],
            shared,
        )
        g_ngain = g_ngain.reshape(shard)
        g_zx, g_out = grads
    else:
        shared = tree_sum(shared)
        g_bc, g_cbc = shared[:shard, :wide_bc], shared[shard:, :wide_bc]
        g_ngain = shared[:shard, wide_bc + heads]
        g_zx = jnp.stack([early[:, :inner], g_x], axis=1)
        g_out = early[:, inner:].T
    return (
        output[None, None],
        grad_input[None, None],
        g_ngain,
        g_zx,
        g_bc,
        g_dt,
        g_out,
        g_cx,
        g_cbc,
        g_head,
        g_ggain.reshape(inner),
    )


def solution(mesh):
    tokens = P(None, "dp", "seq", "head")
    zx = P(("dp", "seq"), None, "head")
    bc = P(("dp", "seq"), None)
    dt = P(("dp", "seq"), "head")
    out = P("head", ("dp", "seq"))
    gain, heads = P(("dp", "seq")), P(None, "head")

    return jax.shard_map(
        local,
        mesh=mesh,
        in_specs=(tokens, tokens, gain, zx, bc, dt, out, heads, P(), heads, P("head")),
        out_specs=(tokens, tokens, gain, zx, bc, dt, out, heads, P(), heads, P("head")),
        check_vma=False,
    )
```

```python
import functools

import jax
import jax.numpy as jnp
from jax import lax
from jax.experimental import pallas as pl
from jax.experimental.pallas import tpu as pltpu
from jax.sharding import PartitionSpec as P


epsilon = 1e-05
f32 = jnp.float32
bf16 = jnp.bfloat16
LANES = 128
HALO = 16
EDGE = 8


def xor_route(count, k):
    return [(i, i ^ k) for i in range(count)]


def sent(block, axis, k):
    return lax.ppermute(block, axis, xor_route(lax.axis_size(axis), k))


def exchanged(block, axis):
    count = lax.axis_size(axis)
    return [block] + [sent(block, axis, k) for k in range(1, count)]


def scattered(blocks, axis):
    count = lax.axis_size(axis)
    return [blocks[0]] + [sent(blocks[k], axis, k) for k in range(1, count)]


def tree_sum(parts):
    while len(parts) > 1:
        parts = [a + b for a, b in zip(parts[0::2], parts[1::2])]
    return parts[0]


def passed_along(block, axis, distance):
    devices = range(lax.axis_size(axis))
    route = [(i - distance, i) for i in devices if i - distance in devices]
    return lax.ppermute(block, axis, route)


def entering(decay, state, axis, reverse):
    count, place = lax.axis_size(axis), lax.axis_index(axis)
    if count == 2:
        return passed_along(state, axis, -1 if reverse else 1)
    decays, states = lax.all_gather(decay, axis), lax.all_gather(state, axis)

    def turn(k, before):
        at = count - 1 - k if reverse else k
        reached = at > place if reverse else at < place
        return jnp.where(reached, decays[at] * before + states[at], before)

    return lax.fori_loop(0, count, turn, jnp.zeros_like(state))


def dot(a, b, left, right):
    return lax.dot_general(
        a.astype(bf16), b.astype(bf16), (((left,), (right,)), ((), ())), preferred_element_type=f32
    )


def nn(a, b):
    return dot(a, b, 1, 0)


def nt(a, b):
    return dot(a, b, 1, 1)


def tn(a, b):
    return dot(a, b, 0, 0)


def sigmoid(v):
    return 1.0 / (1.0 + jnp.exp(-v))


def softplus(v):
    e = jnp.exp(-jnp.abs(v))
    small = e * (1.0 - e * (0.5 - e * (1.0 / 3.0 - e * 0.25)))
    return jnp.maximum(v, 0.0) + jnp.where(e < 0.03, small, jnp.log(1.0 + e))


def iota(shape, axis):
    return lax.broadcasted_iota(jnp.int32, shape, axis)


def row_of(column):
    return jnp.broadcast_to(column, (column.shape[0], LANES)).T[0:1]


def column_of(row):
    return jnp.broadcast_to(row, (LANES, row.shape[1])).T


def terms(values, count):
    parts = []
    for _ in range(count):
        parts.append(values.astype(bf16))
        values = values - parts[-1].astype(f32)
    return parts


def spread(values, heads, width):
    same = iota((LANES, heads * width), 1) // width == iota((LANES, heads * width), 0)
    same = same.astype(bf16)
    return sum(nn(part, same) for part in terms(values, 2))


def gathered_heads(values, heads, width):
    same = iota((heads * width, LANES), 0) // width == iota((heads * width, LANES), 1)
    same = same.astype(bf16)
    return sum(nn(part, same) for part in terms(values, 2))


def running(mask, values):
    mask = mask.astype(bf16)
    return sum(nn(mask, part) for part in terms(values, 3))


def unit(pair, p, where):
    if pair:
        t, k = divmod(p, 4)
        return k ^ (where[0] >> 1), pl.multiple_of((t ^ (where[0] & 1)) * LANES, LANES)
    j, u = divmod(p, 2)
    return j ^ (where[0] >> 1), u * LANES


def assembled(scratch, pieces, axis):
    at = 0
    for piece in pieces:
        size = piece.shape[axis]
        if axis == 0:
            scratch[at : at + size, :] = piece[...]
        else:
            scratch[:, at : at + size] = piece[...]
        at += size


def pack_kernel(w_bc, w_dt, gain, params, out, params_out):
    shard, wide_bc = w_bc.shape
    heads = w_dt.shape[0]
    out[:, 0:wide_bc] = w_bc[...]
    row = iota((LANES - heads, shard), 0)
    rest = jnp.where(row == 0, gain[...].astype(f32), 0.0)
    tile = jnp.concatenate([w_dt[...].astype(f32), rest], axis=0).T
    out[:, wide_bc:] = tile.astype(bf16)
    params_out[...] = jnp.zeros(params_out.shape, f32)
    params_out[0:3, 0:heads] = params[...]


def forward_kernel(pair, heads, n_blocks, n_pieces, where, *refs):
    conv_x, conv_bc, params = refs[:3]
    blocks = refs[3 : 3 + n_blocks]
    zx_pieces = refs[3 + n_blocks : 3 + n_blocks + n_pieces]
    bcd_pieces = refs[3 + n_blocks + n_pieces : 3 + n_blocks + 2 * n_pieces]
    (
        z_ref, xe_ref, be_ref, ux_ref, ubc_ref, dt_ref, cum_ref, y_ref, state_ref, w_in, x_perm,
        inv_ref, normed, gain_ref, rows_in, xe, be, hold,
    ) = refs[3 + n_blocks + 2 * n_pieces :]
    rows, inner = ux_ref.shape
    width = inner // heads
    state_n = ubc_ref.shape[1] // 2
    taps = conv_x.shape[0] - 1
    assembled(w_in.at[:, 0 : 2 * inner], zx_pieces, 0)
    assembled(w_in.at[:, 2 * inner :], bcd_pieces, 0)
    total = jnp.zeros((HALO + rows, 1), f32)
    for k, block in enumerate(blocks):
        value = block[...].astype(f32)
        hold[k] = value
        total += jnp.sum(value * value, axis=1, keepdims=True)
    inv = lax.rsqrt(total / x_perm.shape[1] + epsilon)
    inv_ref[...] = jnp.broadcast_to(inv[HALO:], inv_ref.shape)
    tile = 2 * inner + 2 * state_n
    eye = iota((LANES, LANES), 0) == iota((LANES, LANES), 1)
    for p in range(w_in.shape[0] // LANES):
        cut = slice(p * LANES, (p + 1) * LANES)
        gain = w_in[cut, tile : tile + LANES][:, heads : heads + 1].astype(f32)
        gain = jnp.sum(jnp.where(eye, gain, 0.0), axis=0, keepdims=True)
        gain_ref[:, cut] = gain
        block, lane = unit(pair, p, where)
        value = hold[block, :, pl.ds(lane, LANES)]
        x_perm[:, cut] = value[HALO:].astype(bf16)
        rows_in[:, cut] = (value * inv * gain).astype(bf16)
    normed[...] = rows_in[HALO : HALO + rows, :]
    z_ref[...] = nn(normed[...], w_in[:, 0:inner]).astype(bf16)
    x_raw = nn(rows_in[...], w_in[:, inner : 2 * inner]).astype(bf16)
    xe_ref[...] = x_raw
    xe[...] = x_raw.astype(f32)
    bcd = nn(rows_in[...], w_in[:, 2 * inner :])
    bc_raw = bcd[:, 0 : 2 * state_n].astype(bf16)
    be_ref[...] = bc_raw
    be[...] = bc_raw.astype(f32)
    dt = bcd[HALO:, 2 * state_n :]
    dt_ref[...] = dt

    def conv(extended, weights):
        total = weights[taps : taps + 1, :]
        for k in range(taps):
            total = total + weights[k : k + 1, :] * extended[
                HALO - taps + 1 + k : HALO - taps + 1 + k + rows, :
            ]
        return total

    u_x = conv(xe, conv_x)
    ux_ref[...] = u_x
    u_bc = conv(be, conv_bc)
    ubc_ref[...] = u_bc
    x_act = u_x * sigmoid(u_x)
    bc_act = u_bc * sigmoid(u_bc)
    b_mat = bc_act[:, 0:state_n].astype(bf16)
    c_mat = bc_act[:, state_n:].astype(bf16)
    lane = iota((rows, LANES), 1)
    step = jnp.where(lane < heads, softplus(dt + params[0:1, :]), 0.0)
    lower = iota((rows, rows), 0) >= iota((rows, rows), 1)
    cum = running(lower, -step * jnp.exp(params[1:2, :]))
    cum_ref[...] = cum
    cum_t = cum.T
    gram = nt(c_mat, b_mat)
    scaled = x_act * spread(step, heads, width)
    scaled16 = scaled.astype(bf16)
    skip = spread(params[...], heads, width)[2:3, :]
    pair_lane = iota((rows, 2 * width), 1)
    for q in range(heads // 2):
        cut = slice(2 * width * q, 2 * width * (q + 1))
        both = []
        for h in (2 * q, 2 * q + 1):
            decay = jnp.exp(jnp.where(lower, cum[:, h : h + 1] - cum_t[h : h + 1, :], -jnp.inf))
            both.append(nn(decay * gram, scaled16[:, cut]))
        y_ref[:, cut] = (
            jnp.where(pair_lane < width, both[0], both[1]) + x_act[:, cut] * skip[:, cut]
        )
    to_end = jnp.exp(cum[rows - 1 : rows, :] - cum)
    state_ref[...] = tn(scaled * spread(to_end, heads, width), b_mat)


def gate_kernel(pair, heads, n_blocks, n_pieces, where, *refs):
    normed, state, ubc, cum, y_loc, z, gain = refs[:7]
    blocks = refs[7 : 7 + n_blocks]
    pieces = refs[7 + n_blocks : 7 + n_blocks + n_pieces]
    rest = refs[7 + n_blocks + n_pieces :]
    y_ref, go_ref, stats_ref, normed_t, cot_t = rest[:5]
    outs, (hold, cot, weights, out_hold) = rest[5 : 5 + n_blocks], rest[5 + n_blocks :]
    rows, inner = y_ref.shape
    width = inner // heads
    state_n = ubc.shape[1] // 2
    assembled(weights, pieces, 1)
    for k, block in enumerate(blocks):
        hold[k] = block[...].astype(f32)
    for p in range(cot.shape[1] // LANES):
        block, lane = unit(pair, p, where)
        cut = slice(p * LANES, (p + 1) * LANES)
        value = hold[block, :, pl.ds(lane, LANES)]
        cot[:, cut] = value.astype(bf16)
        cot_t[cut, :] = value.T.astype(bf16)
        normed_t[cut, :] = normed[:, cut].astype(f32).T.astype(bf16)
    grad_o = nt(cot[...], weights[...])
    go_ref[...] = grad_o
    u_c = ubc[:, state_n:]
    c_mat = u_c * sigmoid(u_c)
    y = y_loc[...] + nt(c_mat, state[...]) * spread(jnp.exp(cum[...]), heads, width)
    y_ref[...] = y
    z_val = z[...].astype(f32)
    gated = y * z_val * sigmoid(z_val)
    raw = gated * gain[...]
    squares = jnp.sum(gated * gated, axis=1, keepdims=True)
    cross = jnp.sum(grad_o * raw, axis=1, keepdims=True)
    lane = iota((rows, LANES), 1)
    both = jnp.where(lane == 0, squares, jnp.where(lane == 1, cross, 0.0))
    stats_ref[...] = both.T[0:8, :]
    part = nn(raw, weights[...]).astype(bf16)
    for p in range(weights.shape[1] // LANES):
        block, lane = unit(pair, p, where)
        out_hold[block, :, pl.ds(lane, LANES)] = part[:, p * LANES : (p + 1) * LANES]
    for k, ref in enumerate(outs):
        ref[...] = out_hold[k]


def gate_back_kernel(heads, full_inner, n_stats, *refs):
    stats = refs[:n_stats]
    go, y, z, gain, ubc, cum = refs[n_stats : n_stats + 6]
    dy_ref, dz_ref, state_ref, inv_ref, ggain_ref, gated_ref = refs[n_stats + 6 :]
    rows, inner = y.shape
    width = inner // heads
    state_n = ubc.shape[1] // 2
    total = tree_sum([s[...] for s in stats])
    total = jnp.concatenate([total, jnp.zeros((LANES - total.shape[0], rows), f32)], axis=0).T
    inv = lax.rsqrt(total[:, 0:1] / full_inner + epsilon)
    coef = inv * inv * inv * (total[:, 1:2] / full_inner)
    inv_ref[...] = jnp.broadcast_to(inv, inv_ref.shape)
    z_val = z[...].astype(f32)
    sig = sigmoid(z_val)
    silu = z_val * sig
    y_val = y[...]
    gated = y_val * silu
    grad_o = go[...]
    unit_gated = gated * inv
    gated_ref[...] = (unit_gated * gain[...]).astype(bf16)
    ggain_ref[...] = jnp.sum(grad_o * unit_gated, axis=0, keepdims=True)
    grad_gin = inv * grad_o * gain[...] - gated * coef
    dy = grad_gin * silu
    dy_ref[...] = dy
    dz_ref[...] = (grad_gin * y_val * sig * (1.0 + z_val * (1.0 - sig))).astype(bf16)
    u_c = ubc[:, state_n:]
    c_mat = u_c * sigmoid(u_c)
    state_ref[...] = tn(dy * spread(jnp.exp(cum[...]), heads, width), c_mat)


def inner_back_kernel(
    heads, dy_ref, dz, cum_ref, dt, params, ux, ubc, state, gated, cot_t, normed_t,
    dxs_ref, dbc_ref, dcum_ref, own_ref, other_ref,
):
    rows, inner = dy_ref.shape
    width = inner // heads
    state_n = ubc.shape[1] // 2
    cum = cum_ref[...]
    cum_t = cum.T
    u_x, u_bc = ux[...], ubc[...]
    x_act = u_x * sigmoid(u_x)
    bc_act = u_bc * sigmoid(u_bc)
    b_mat = bc_act[:, 0:state_n].astype(bf16)
    c_mat = bc_act[:, state_n:].astype(bf16)
    lane = iota((rows, LANES), 1)
    step = jnp.where(lane < heads, softplus(dt[...] + params[0:1, :]), 0.0)
    scaled16 = (x_act * spread(step, heads, width)).astype(bf16)
    dy = dy_ref[...]
    dy16 = dy.astype(bf16)
    gram = nt(c_mat, b_mat)
    lower = iota((rows, rows), 0) >= iota((rows, rows), 1)
    pair_lane = iota((rows, 2 * width), 1)
    grad_gram = jnp.zeros((rows, rows), f32)
    dcum = jnp.zeros((rows, LANES), f32)
    sub = iota((LANES, rows), 0)
    dcum_t = jnp.zeros((LANES, rows), f32)
    for q in range(heads // 2):
        cut = slice(2 * width * q, 2 * width * (q + 1))
        both = []
        for h in (2 * q, 2 * q + 1):
            decay = jnp.exp(jnp.where(lower, cum[:, h : h + 1] - cum_t[h : h + 1, :], -jnp.inf))
            mix = decay * gram
            both.append(tn(mix, dy16[:, cut]))
            own = (pair_lane < width) == (h % 2 == 0)
            grad_mix = nt(jnp.where(own, dy[:, cut], 0.0), scaled16[:, cut])
            grad_gram = grad_gram + grad_mix * decay
            expo = grad_mix * mix
            dcum = jnp.where(lane == h, jnp.sum(expo, axis=1, keepdims=True), dcum)
            dcum_t = jnp.where(sub == h, jnp.sum(expo, axis=0, keepdims=True), dcum_t)
        dxs_ref[:, cut] = jnp.where(pair_lane < width, both[0], both[1])
    exp_cum = spread(jnp.exp(cum), heads, width)
    cross = nt(c_mat, state[...]) * exp_cum
    dcum_ref[...] = dcum - dcum_t.T + gathered_heads(dy * cross, heads, width)
    dbc_ref[:, 0:state_n] = tn(grad_gram, c_mat)
    dbc_ref[:, state_n:] = nn(dy * exp_cum, state[...]) + nn(grad_gram, b_mat)
    half = own_ref.shape[0]
    for ref, cut in ((own_ref, slice(0, half)), (other_ref, slice(half, 2 * half))):
        ref[:, 0:inner] = nn(normed_t[cut, :], dz[...]).astype(bf16)
        ref[:, inner:] = nn(cot_t[cut, :], gated[...]).astype(bf16)


def ssd_back_kernel(
    heads, next_ref, dxs, dbc, dcum_ref, dy_ref, cum_ref, dt, params, ux, ubc, state,
    gux_ref, gubc_ref, edge_ref, raw_ref, ghead_ref,
):
    rows, inner = dy_ref.shape
    width = inner // heads
    state_n = ubc.shape[1] // 2
    cum = cum_ref[...]
    u_x, u_bc = ux[...], ubc[...]
    sig_x, sig_bc = sigmoid(u_x), sigmoid(u_bc)
    x_act = u_x * sig_x
    bc_act = u_bc * sig_bc
    b_mat = bc_act[:, 0:state_n].astype(bf16)
    lane = iota((rows, LANES), 1)
    shifted = dt[...] + params[0:1, :]
    step = jnp.where(lane < heads, softplus(shifted), 0.0)
    rate = -jnp.exp(params[1:2, :])
    step_wide = spread(step, heads, width)
    scaled = x_act * step_wide
    dy = dy_ref[...]
    grad_next = next_ref[...]
    to_end = spread(jnp.exp(cum[rows - 1 : rows, :] - cum), heads, width)
    from_next = nt(b_mat, grad_next) * to_end
    grad_scaled = dxs[...] + from_next
    grad_b = dbc[:, 0:state_n] + nn(scaled * to_end, grad_next)
    end_term = gathered_heads(scaled * from_next, heads, width)
    held = jnp.sum(state[...] * grad_next, axis=1, keepdims=True)
    held = jnp.broadcast_to(held, (inner, LANES))
    head_of = iota((inner, LANES), 0) // width == iota((inner, LANES), 1)
    held = jnp.sum(jnp.where(head_of, held, 0.0), axis=0, keepdims=True)
    last = jnp.sum(end_term, axis=0, keepdims=True) + jnp.exp(cum[rows - 1 : rows, :]) * held
    upper = iota((rows, rows), 0) <= iota((rows, rows), 1)
    grad_log = last + running(upper, dcum_ref[...] - end_term)
    grad_step = gathered_heads(grad_scaled * x_act, heads, width) + grad_log * rate
    grad_raw = jnp.where(lane < heads, grad_step * sigmoid(shifted), 0.0)
    raw_ref[...] = grad_raw.astype(bf16)
    row = iota((8, LANES), 0)
    bias_grad = jnp.sum(grad_raw, axis=0, keepdims=True)
    rate_grad = jnp.sum(grad_log * step, axis=0, keepdims=True) * rate
    skip_rows = jnp.broadcast_to(jnp.sum(dy * x_act, axis=0, keepdims=True), (8, inner))
    skip_grad = gathered_heads(skip_rows, heads, width)[0:1, :]
    ghead_ref[...] = jnp.where(
        row == 0, bias_grad, jnp.where(row == 1, rate_grad, jnp.where(row == 2, skip_grad, 0.0))
    )
    skip = spread(params[...], heads, width)[2:3, :]
    gux = (grad_scaled * step_wide + dy * skip) * (sig_x * (1.0 + u_x * (1.0 - sig_x)))
    gux_ref[...] = gux
    slope = sig_bc * (1.0 + u_bc * (1.0 - sig_bc))
    gubc_ref[:, 0:state_n] = grad_b * slope[:, 0:state_n]
    gubc_ref[:, state_n:] = dbc[:, state_n:] * slope[:, state_n:]
    edge_ref[:, 0:inner] = gux_ref[0:EDGE, :]
    edge_ref[:, inner:] = gubc_ref[0:EDGE, :]


def last_kernel(pair, gain_lane, n_blocks, where, *refs):
    edge, gux, gubc, xe, be, dz, raw, normed_t, x_perm, inv, gain, conv_x, conv_bc, w_in = refs[:14]
    ggain, ghead = refs[14:16]
    blocks = refs[16 : 16 + n_blocks]
    gx_own, gx_other, gb_own, gb_other = refs[16 + n_blocks : 20 + n_blocks]
    hold, gx_ext, gb_ext, small, grads = refs[20 + n_blocks :]
    rows, inner = gux.shape
    wide_bc = gubc.shape[1]
    taps = conv_x.shape[0] - 1
    small[...] = jnp.zeros(small.shape, f32)

    def conv_back(grad, ext, raw_ref, weights, next_rows, firsts, width):
        value = grad[...]
        ext[0:rows, :] = value
        ext[rows : rows + EDGE, :] = next_rows
        before = raw_ref[HALO:, :].astype(f32)

        def kept(k, row):
            for j, first in enumerate(firsts):
                small[first + k : first + k + 1, 0:wide_bc] = row[:, j * wide_bc : (j + 1) * wide_bc]

        total = jnp.zeros((rows, width), f32)
        for k in range(taps):
            ahead = taps - 1 - k
            later = ext[ahead : ahead + rows, :] if ahead > 0 else value
            total = total + weights[k : k + 1, :] * later
            kept(k, jnp.sum(before * later, axis=0, keepdims=True))
        kept(taps, jnp.sum(value, axis=0, keepdims=True))
        return total.astype(bf16)

    n = taps + 1
    dx = conv_back(gux, gx_ext, xe, conv_x, edge[:, 0:inner], (0, n), inner)
    dbc = conv_back(gubc, gb_ext, be, conv_bc, edge[:, inner:], (2 * n,), wide_bc)
    for j in range(2):
        small[3 * n + j : 3 * n + j + 1, 0:wide_bc] = ggain[:, j * wide_bc : (j + 1) * wide_bc]
    small[3 * n + 2 : 3 * n + 5, 0:LANES] = ghead[0:3, :]
    grads[:, 0:inner] = dz[...]
    grads[:, inner : 2 * inner] = dx
    grads[:, 2 * inner : 2 * inner + wide_bc] = dbc
    grads[:, 2 * inner + wide_bc :] = raw[...]
    part = nt(grads[...], w_in[...])
    for p in range(part.shape[1] // LANES):
        block, lane = unit(pair, p, where)
        hold[block, :, pl.ds(lane, LANES)] = part[:, p * LANES : (p + 1) * LANES].astype(bf16)
    along = part * (x_perm[...].astype(f32) * inv[:, 0:1])
    dots = row_of(jnp.sum(along * gain[...], axis=1, keepdims=True))
    high = dots.astype(bf16).astype(f32)
    extra = jnp.where(iota((16, rows), 0) == 0, high, dots - high)
    extra = jnp.where(iota((16, rows), 0) < 2, extra, 0.0).astype(bf16)
    for k, ref in enumerate(blocks):
        ref[0:rows, :] = hold[k]
        ref[rows : rows + 16, :] = extra
    half = gx_own.shape[0]
    at = iota((half, LANES), 1) == gain_lane
    high = small[...].astype(bf16)
    low = (small[...] - high.astype(f32)).astype(bf16)
    count = small.shape[0]
    gain_sum = jnp.sum(along, axis=0, keepdims=True)
    for first, gx_ref, gb_ref in ((0, gx_own, gb_own), (half, gx_other, gb_other)):
        cut = slice(first, first + half)
        g_both = nn(normed_t[cut, :], grads[:, inner:])
        gx_ref[...] = g_both[:, 0:inner].astype(bf16)
        g_bcd = g_both[:, inner:]
        g_gain = jnp.concatenate(
            [column_of(gain_sum[:, j : j + LANES]) for j in range(first, first + half, LANES)], axis=0
        )
        gb_ref[0:half, 0:wide_bc] = g_bcd[:, 0:wide_bc].astype(bf16)
        gb_ref[0:half, wide_bc:] = jnp.where(at, g_gain, g_bcd[:, wide_bc:]).astype(bf16)
        gb_ref[half : half + count, :] = high
        gb_ref[half + count :, :] = low


def fold_kernel(n_blocks, own, other, x_own, x_other, *refs):
    blocks, x_blocks = refs[:n_blocks], refs[n_blocks:]
    size = x_blocks[0].shape[0]
    first, half = n_blocks * size, (blocks[0].shape[0] - size) // 2
    total = [ref[first:, :].astype(f32) for ref in (own, other)]
    total = (total[0][:half] + total[0][half:]) + (total[1][:half] + total[1][half:])
    high, low = terms(total, 2)
    for k in range(n_blocks):
        cut = slice(k * size, (k + 1) * size)
        blocks[k][0:size, :] = (own[cut, :].astype(f32) + other[cut, :].astype(f32)).astype(bf16)
        blocks[k][size : size + half, :] = high
        blocks[k][size + half :, :] = low
        x_blocks[k][...] = (x_own[cut, :].astype(f32) + x_other[cut, :].astype(f32)).astype(bf16)


def small_kernel(taps, heads, n_blocks, *refs):
    gdt_ref, cx_ref, ghead_ref, ggain_ref, shared_ref = refs[n_blocks:]
    total = tree_sum([b[...].astype(f32) for b in refs[:n_blocks]])
    wide_bc = cx_ref.shape[1] // 2
    n, size = taps + 1, gdt_ref.shape[1]
    half = (total.shape[0] - size) // 2
    small = total[size : size + half] + total[size + half :]
    gdt_ref[...] = total[0:size, wide_bc:].T[0:heads, :]
    for j in range(2):
        cut = slice(j * wide_bc, (j + 1) * wide_bc)
        cx_ref[:, cut] = small[j * n : (j + 1) * n, 0:wide_bc]
        ggain_ref[:, cut] = small[3 * n + j : 3 * n + j + 1, 0:wide_bc]
    ghead_ref[...] = small[3 * n + 2 : 3 * n + 5, 0:heads]
    shared_ref[0:size, :] = total[0:size, 0:wide_bc].astype(bf16)
    tail = jnp.concatenate([small[2 * n : 2 * n + 7, 0:wide_bc], jnp.zeros((1, wide_bc), f32)], axis=0)
    gain = row_of(total[0:size, wide_bc:][:, heads : heads + 1])
    gain = jnp.concatenate([gain, jnp.zeros((1, wide_bc - size), f32)], axis=1)
    tail = jnp.where(iota((8, wide_bc), 0) == 7, gain, tail)
    high, low = terms(tail, 2)
    shared_ref[size : size + 8, :] = high
    shared_ref[size + 8 :, :] = low


def shared_kernel(n_blocks, *refs):
    gbc_ref, cbc_ref, ngain_ref = refs[n_blocks:]
    total = tree_sum([b[...].astype(f32) for b in refs[:n_blocks]])
    size = gbc_ref.shape[0]
    gbc_ref[...] = total[0:size]
    rows = total[size : size + 8] + total[size + 8 :]
    cbc_ref[...] = rows[0 : cbc_ref.shape[0]]
    ngain_ref[...] = rows[7:8, 0 : ngain_ref.shape[1]]


def input_kernel(pair, full_d, n_blocks, n_grads, where, *refs):
    blocks, outs = refs[:n_blocks], refs[n_blocks : 2 * n_blocks]
    early, late = (refs[(2 * n_blocks + j * n_grads) :][:n_grads] for j in range(2))
    rest = refs[2 * n_blocks + 2 * n_grads :]
    x_local, cot, inv, gain, inv_gate = rest[:5]
    gains = rest[-1]
    output_ref, grad_ref = rest[5:7]
    rows, _ = x_local.shape
    total = tree_sum([b[...].astype(f32) for b in outs])
    x_val = x_local[...].astype(f32)
    output_ref[...] = (x_val + total * inv_gate[:, 0:1]).astype(bf16)
    total = tree_sum([b[...].astype(f32) for b in blocks])
    dots = column_of((total[rows : rows + 1, :] + total[rows + 1 : rows + 2, :]) / full_d)[:, 0:1]
    scale = inv[:, 0:1]
    for p in range(gain.shape[1] // LANES):
        block, lane = unit(pair, p, where)

        @pl.when(block == 0)
        def _():
            gains[:, pl.ds(lane, LANES)] = jnp.broadcast_to(
                gain[:, p * LANES : (p + 1) * LANES], (8, LANES)
            )

    grad = scale * (total[0:rows, :] * gains[0:1, :] - x_val * (scale * dots))
    grad_ref[...] = (cot[...].astype(f32) + grad).astype(bf16)
    if n_grads > 0:
        gzx_ref, gout_ref = rest[7:9]
        inner = gzx_ref.shape[2]
        total = tree_sum([b[...].astype(f32) for b in early])
        gzx_ref[:, 0, :] = total[:, 0:inner]
        gzx_ref[:, 1, :] = tree_sum([b[...].astype(f32) for b in late])
        gout_ref[...] = total[:, inner:].T


VMEM = pl.BlockSpec(memory_space=pltpu.VMEM)
SMEM = pl.BlockSpec(memory_space=pltpu.SMEM)


def call(kernel, outs, inputs, scratch=(), scalars=0):
    return pl.pallas_call(
        kernel,
        out_shape=[jax.ShapeDtypeStruct(shape, kind) for shape, kind in outs],
        in_specs=[SMEM] * scalars + [VMEM] * (len(inputs) - scalars),
        out_specs=[VMEM] * len(outs),
        scratch_shapes=[pltpu.VMEM(shape, kind) for shape, kind in scratch],
    )(*inputs)


def local(
    hidden_in, cotangent, norm_gain, w_zx, w_bc, w_dt, w_out, conv_x, conv_bc, head_params, gate_gain
):
    rows, part_d = hidden_in.shape[2:]
    heads = head_params.shape[1]
    inner = conv_x.shape[1]
    wide_bc = w_bc.shape[1]
    taps = conv_x.shape[0] - 1
    shard = w_zx.shape[0]
    dp_n, seq_n, head_n = lax.axis_size("dp"), lax.axis_size("seq"), lax.axis_size("head")
    full_d = part_d * head_n
    full_inner = inner * head_n
    dp_i, seq_i, head_i = lax.axis_index("dp"), lax.axis_index("seq"), lax.axis_index("head")
    pair = seq_n == 2 and dp_n == head_n == 4 and shard == LANES and part_d == 2 * LANES
    state_n = wide_bc // 2

    where = ((head_i ^ dp_i) * 2 + seq_i if pair else head_i * 2).astype(jnp.int32).reshape(1)

    def gathered(part, axis):
        if not pair:
            return [lax.all_gather(part, ("dp", "seq"), axis=axis, tiled=True)]
        own = exchanged(part, "dp")
        return own + [sent(p, "seq", 1) for p in own]

    def reduced(own, other):
        recv = sent(other, "seq", 1)
        both = (own.astype(f32) + recv.astype(f32)).astype(bf16)
        blocks = [both[k * shard : (k + 1) * shard] for k in range(dp_n)]
        return scattered(blocks, "dp")

    def reduced_apart(own, other):
        both = jnp.concatenate([own[: full_d // 2], other[: full_d // 2]], axis=0).astype(f32)
        return lax.psum_scatter(both, ("dp", "seq"), scatter_dimension=0, tiled=True)

    x_local = hidden_in[0, 0]
    cot_local = cotangent[0, 0]
    wide_bcd = wide_bc + LANES
    x_halo = passed_along(x_local, "seq", 1)[rows - HALO :]
    zx_pieces = gathered(w_zx.reshape(shard, 2 * inner), 0)
    x_blocks = exchanged(jnp.concatenate([x_halo, x_local], axis=0), "head")
    if pair:
        packed, params = call(
            pack_kernel,
            [((shard, wide_bcd), bf16), ((8, LANES), f32)],
            [w_bc, w_dt.T, norm_gain[None], head_params],
        )
    else:
        pad = jnp.zeros((shard, LANES - heads - 1), bf16)
        packed = jnp.concatenate([w_bc, w_dt, norm_gain[:, None], pad], axis=1)
        params = jnp.pad(head_params, ((0, 5), (0, LANES - heads)))
    bcd_pieces = gathered(packed, 0)
    out_pieces = gathered(w_out, 1)
    cot_blocks = exchanged(cot_local, "head")
    gain_row = gate_gain[None]
    n_in, n_out = len(zx_pieces), len(out_pieces)

    (
        z, x_ext, bc_ext, u_x, u_bc, dt, cum, y_loc, own_state, w_in, x_perm, inv_in, normed, norm_row,
    ) = call(
        functools.partial(forward_kernel, pair, heads, head_n, n_in),
        [
            ((rows, inner), bf16),
            ((HALO + rows, inner), bf16),
            ((HALO + rows, wide_bc), bf16),
            ((rows, inner), f32),
            ((rows, wide_bc), f32),
            ((rows, LANES), f32),
            ((rows, LANES), f32),
            ((rows, inner), f32),
            ((inner, state_n), f32),
            ((full_d, 2 * inner + wide_bcd), bf16),
            ((rows, full_d), bf16),
            ((rows, LANES), f32),
            ((rows, full_d), bf16),
            ((1, full_d), f32),
        ],
        [where, conv_x, conv_bc, params, *x_blocks, *zx_pieces, *bcd_pieces],
        [
            ((HALO + rows, full_d), bf16),
            ((HALO + rows, inner), f32),
            ((HALO + rows, wide_bc), f32),
            ((head_n, HALO + rows, part_d), f32),
        ],
        1,
    )
    total_decay = jnp.repeat(jnp.exp(cum[rows - 1, :heads]), inner // heads)[:, None]
    state_in = entering(total_decay, own_state, "seq", False)
    y, grad_o, stats, normed_t, cot_t, *out_blocks = call(
        functools.partial(gate_kernel, pair, heads, head_n, n_out),
        [
            ((rows, inner), f32),
            ((rows, inner), f32),
            ((8, rows), f32),
            ((full_d, rows), bf16),
            ((full_d, rows), bf16),
        ]
        + [((rows, part_d), bf16)] * head_n,
        [where, normed, state_in, u_bc, cum, y_loc, z, gain_row, *cot_blocks, *out_pieces],
        [
            ((head_n, rows, part_d), f32),
            ((rows, full_d), bf16),
            ((inner, full_d), bf16),
            ((head_n, rows, part_d), bf16),
        ],
        1,
    )
    stats = exchanged(stats, "head")
    out_parts = scattered(out_blocks, "head")

    dy, dz, from_cross, inv_gate, g_ggain, gated = call(
        functools.partial(gate_back_kernel, heads, full_inner, head_n),
        [
            ((rows, inner), f32),
            ((rows, inner), bf16),
            ((inner, state_n), f32),
            ((rows, LANES), f32),
            ((1, inner), f32),
            ((rows, inner), bf16),
        ],
        [*stats, grad_o, y, z, gain_row, u_bc, cum],
    )
    grad_next = entering(total_decay, from_cross, "seq", True)
    dxs, dbc, dcum, early_own, early_other = call(
        functools.partial(inner_back_kernel, heads),
        [
            ((rows, inner), f32),
            ((rows, wide_bc), f32),
            ((rows, LANES), f32),
            ((full_d // 2, 2 * inner), bf16),
            ((full_d // 2, 2 * inner), bf16),
        ],
        [dy, dz, cum, dt, params, u_x, u_bc, state_in, gated, cot_t, normed_t],
    )
    gux, gubc, edge_out, raw16, g_head = call(
        functools.partial(ssd_back_kernel, heads),
        [
            ((rows, inner), f32),
            ((rows, wide_bc), f32),
            ((EDGE, inner + wide_bc), f32),
            ((rows, LANES), bf16),
            ((8, LANES), f32),
        ],
        [grad_next, dxs, dbc, dcum, dy, cum, dt, params, u_x, u_bc, state_in],
    )
    edge_next = passed_along(edge_out, "seq", -1)
    n = taps + 1
    count = 24
    results = call(
        functools.partial(last_kernel, pair, heads, head_n),
        [((rows + 16, part_d), bf16)] * head_n
        + [((full_d // 2, inner), bf16)] * 2
        + [((full_d // 2 + 2 * count, wide_bcd), bf16)] * 2,
        [
            where, edge_next, gux, gubc, x_ext, bc_ext, dz, raw16, normed_t, x_perm, inv_in, norm_row,
            conv_x, conv_bc, w_in, g_ggain, g_head,
        ],
        [
            ((head_n, rows, part_d), bf16),
            ((rows + EDGE, inner), f32),
            ((rows + EDGE, wide_bc), f32),
            ((count, wide_bcd), f32),
            ((rows, 2 * inner + wide_bcd), bf16),
        ],
        1,
    )
    blocks, (gx_own, gx_other, gb_own, gb_other) = results[:head_n], results[head_n:]
    if pair:
        early = reduced(early_own, early_other)
        gb_recv = sent(gb_other, "seq", 1)
        gx_recv = sent(gx_other, "seq", 1)
        folded = call(
            functools.partial(fold_kernel, dp_n),
            [((shard + 2 * count, wide_bcd), bf16)] * dp_n + [((shard, inner), bf16)] * dp_n,
            [gb_own, gb_recv, gx_own, gx_recv],
        )
        g_bcd = scattered(folded[:dp_n], "dp")
        g_x = scattered(folded[dp_n:], "dp")
        g_dt, g_cx, g_head, g_ggain, shared = call(
            functools.partial(small_kernel, taps, heads, dp_n),
            [
                ((heads, shard), f32),
                ((n, inner), f32),
                ((3, heads), f32),
                ((1, inner), f32),
                ((shard + 16, wide_bc), bf16),
            ],
            g_bcd,
        )
        g_dt = g_dt.T
    else:
        early = reduced_apart(early_own, early_other)
        g_bcd = reduced_apart(gb_own, gb_other)
        g_x = reduced_apart(gx_own, gx_other)
        small = lax.psum(
            gb_own[full_d // 2 :][:count].astype(f32) + gb_own[full_d // 2 + count :].astype(f32),
            ("dp", "seq"),
        )
        g_dt = g_bcd[:, wide_bc : wide_bc + heads]
        g_cx = jnp.concatenate([small[:n, :wide_bc], small[n : 2 * n, :wide_bc]], axis=1)
        g_ggain = small[3 * n : 3 * n + 2, :wide_bc].reshape(1, inner)
        g_head = small[3 * n + 2 : 3 * n + 5, :heads]
        shared = jnp.concatenate([g_bcd, small[2 * n : 3 * n]], axis=0)
    parts = scattered(blocks, "head")
    grads = [((shard, 2, inner), f32), ((inner, shard), f32)] if pair else []
    output, grad_input, *grads = call(
        functools.partial(input_kernel, pair, full_d, head_n, dp_n if pair else 0),
        [((rows, part_d), bf16), ((rows, part_d), bf16), *grads],
        [
            where, *parts, *out_parts, *(early if pair else []), *(g_x if pair else []),
            x_local, cot_local, inv_in, norm_row, inv_gate,
        ],
        [((8, part_d), f32)],
        1,
    )
    shared = exchanged(shared, "head")
    if pair:
        g_bc, g_cbc, g_ngain = call(
            functools.partial(shared_kernel, head_n),
            [((shard, wide_bc), f32), ((n, wide_bc), f32), ((1, shard), f32)],
            shared,
        )
        g_ngain = g_ngain.reshape(shard)
        g_zx, g_out = grads
    else:
        shared = tree_sum(shared)
        g_bc, g_cbc = shared[:shard, :wide_bc], shared[shard:, :wide_bc]
        g_ngain = shared[:shard, wide_bc + heads]
        g_zx = jnp.stack([early[:, :inner], g_x], axis=1)
        g_out = early[:, inner:].T
    return (
        output[None, None],
        grad_input[None, None],
        g_ngain,
        g_zx,
        g_bc,
        g_dt,
        g_out,
        g_cx,
        g_cbc,
        g_head,
        g_ggain.reshape(inner),
    )


def solution(mesh):
    tokens = P(None, "dp", "seq", "head")
    zx = P(("dp", "seq"), None, "head")
    bc = P(("dp", "seq"), None)
    dt = P(("dp", "seq"), "head")
    out = P("head", ("dp", "seq"))
    gain, heads = P(("dp", "seq")), P(None, "head")

    return jax.shard_map(
        local,
        mesh=mesh,
        in_specs=(tokens, tokens, gain, zx, bc, dt, out, heads, P(), heads, P("head")),
        out_specs=(tokens, tokens, gain, zx, bc, dt, out, heads, P(), heads, P("head")),
        check_vma=False,
    )
```
